32 devices in a mesh: ens: 2 (over x), along: 16 (over z, y, core).
Axes of the slice: x: 2, y: 2, z: 4, core: 2. Of those that a mesh axis runs over, the one named last changes fastest.
Arguments:
- basic_state: float32 [40, 512, 1024], P(None, ('ens', 'along')), parts along dimension 1, may hold values from -4 to 4
- land_sea: int32 [512, 1024], P(('ens', 'along')), parts along dimension 0, may hold values 0 or 1
- obs_cells: int32 [32, 3, 512], P(('ens', 'along')), parts along dimension 0, may hold values from 0 to 655359
- obs_count: int32 [32, 3], P(('ens', 'along')), parts along dimension 0, may hold values from 1 to 512, as said below
- obs_value: float32 [32, 3, 512], P(('ens', 'along')), parts along dimension 0, may hold values from -12 to 12
Outputs:
- gradient: float32 [40, 512, 1024], P(None, ('ens', 'along')), parts along dimension 1
- misfit: float32 [2], P('ens'), parts along dimension 0
The draws below stay inside these ranges and needn't reach their ends.
There are 2 independent parts, one for each index of `ens`. The reference program is written for one: setup_inputs(seed, part) draws one part's arguments, and reference() takes and returns one part's arrays. A program takes and returns all parts, laid end to end along the dimension named above; each array names one. Nothing has to cross between parts.
Inputs may be any that keep to these rules, and one draw needn't show every extreme that they name: `obs_cells`: each entry is a cell of the tile's own block, flattened as (level * 16 + row) * 1024 + column; cells may repeat; slots from obs_count on are unused. Slots 0 .. obs_count - 1 of a tile's list at a time are live; in every draw some tile is full at some time.
All inputs are finite; a program needn't handle non-finite values. No bound on the sum of `land_sea` on one device may be relied on, other than what follows from the above.
Results may differ from the reference program's by a relative error of at most 0.0001.
Values sent between devices are 32-bit elements; how exact they have to be, the bound alone decides.
No kernel may reach another device: no remote copies, remote signals or barrier semaphores. Data moves between devices by JAX's collectives and lax.ppermute only.
A program may use at most 128 MiB of HBM per device.

```python
import jax
import jax.numpy as jnp

LEVELS = 40
ROWS_DEV = 16
NC = 1024
NSTEP = 3
OBS_CAP = 512
TILES = 16
NX = 256


def draw_obs_count(key, part):
    counts = jax.random.randint(key, (TILES, NSTEP), 1, OBS_CAP + 1)
    chosen = jax.random.randint(jax.random.fold_in(key, 11), (), 0, TILES)
    when = jax.random.randint(jax.random.fold_in(key, 12), (), 0, NSTEP)
    tiles = jnp.arange(TILES)[:, None]
    times = jnp.arange(NSTEP)[None, :]
    full = (tiles == chosen) & (times == when)
    return jnp.where(full, OBS_CAP, counts).astype(jnp.int32)


def draw_obs_value(key, part):
    tiles = jnp.arange(TILES, dtype=jnp.float32)[:, None, None]
    ramp = 1.0 + 2.0 * tiles / max(TILES - 1, 1)
    base = jnp.clip(jax.random.normal(key, (TILES, NSTEP, OBS_CAP), jnp.float32), -4.0, 4.0)
    return (base * ramp).astype(jnp.float32)


def with_ends(entries, stream_key, low, largest):
    longest = entries.shape.index(max(entries.shape))
    spots = []
    for shift in (0, 1):
        where = [jax.random.randint(jax.random.fold_in(stream_key, axis), (), 0, length) for axis, length in enumerate(entries.shape)]
        where[longest] = (where[longest] + shift) % entries.shape[longest]
        spots.append(tuple(where))
    return entries.at[spots[0]].set(low).at[spots[1]].set(largest)


def steps_of(stream_key, shape, cuts, least, largest):
    def one(axis_at, parts):
        draws = jax.random.uniform(jax.random.fold_in(jax.random.fold_in(stream_key, 6), axis_at), (parts,), jnp.float32, least / len(cuts), largest / len(cuts))
        return jnp.repeat(jnp.exp(draws), shape[axis_at] // parts).reshape((-1,) + (1,) * (len(shape) - axis_at - 1))

    loudness = one(*cuts[0])
    for cut in cuts[1:]:
        loudness = loudness * one(*cut)
    return loudness


def noise(rng, dims, spread, most, cuts=(), kind=jnp.bfloat16):
    drawn = jax.random.normal(rng, dims, jnp.float32) * spread
    if len(cuts) > 0:
        drawn = steps_of(rng, dims, cuts, -0.22, 0.18) * drawn
    return jnp.clip(drawn, min=-most, max=most).astype(kind)


def setup_inputs(seed: int = 0, part: int = 0) -> dict:
    arg_keys = jax.random.split(jax.random.key(seed), 6)
    part_splits = jax.random.split(jax.random.fold_in(arg_keys[5], part), 6)
    return {
        "basic_state": noise(part_splits[0], (LEVELS, NX, NC), 1.0, 4.0, ((1, 16),), jnp.float32),
        "land_sea": with_ends((jax.random.randint(part_splits[1], (NX, NC), 0, 5) < 4).astype(jnp.int32), jax.random.fold_in(part_splits[1], 1), 0, 1),
        "obs_cells": with_ends(jax.random.randint(part_splits[2], (TILES, NSTEP, OBS_CAP), 0, LEVELS * ROWS_DEV * NC), jax.random.fold_in(part_splits[2], 1), 0, (LEVELS * ROWS_DEV * NC) - 1).astype(jnp.int32),
        "obs_count": draw_obs_count(jax.random.fold_in(jax.random.fold_in(arg_keys[5], part), 71), part),
        "obs_value": draw_obs_value(jax.random.fold_in(jax.random.fold_in(arg_keys[5], part), 71), part),
    }


A_H = 0.2
B_V = 0.04
C_DRAG = 0.05


def vertical_mix(field):
    fluxes = field[1:] - field[:-1]
    zero = jnp.zeros_like(field[:1])
    padded = jnp.concatenate([zero, fluxes, zero], axis=0)
    return padded[1:] - padded[:-1]


def lateral_mix(extended):
    centre = extended[:, 1:-1]
    sides = jnp.pad(centre, ((0, 0), (0, 0), (1, 1)))
    return extended[:, 2:] + extended[:, :-2] + sides[:, :, 2:] + sides[:, :, :-2] - 4.0 * centre


def extend_rows(field):
    return jnp.pad(field, ((0, 0), (1, 1), (0, 0)))


def forward_rows(extended, weights):
    centre = extended[:, 1:-1]
    return weights * (centre + A_H * lateral_mix(extended) + B_V * vertical_mix(centre) - C_DRAG * centre * centre * centre)


def adjoint_step(adjoint, state, weights):
    masked = weights * adjoint
    return masked + A_H * lateral_mix(extend_rows(masked)) + B_V * vertical_mix(masked) - 3.0 * C_DRAG * state * state * masked


def reference(basic_state, land_sea, obs_cells, obs_count, obs_value):
    weights = land_sea.astype(jnp.float32)
    states = [weights * basic_state]
    for step_index in range(NSTEP):
        states.append(forward_rows(extend_rows(states[-1]), weights))
    tile_ids = jnp.arange(TILES, dtype=jnp.int32)[:, None]
    slot_ids = jnp.arange(OBS_CAP, dtype=jnp.int32)[None, :]
    forcings = []
    total = jnp.float32(0.0)
    for step_index in range(NSTEP):
        cells = obs_cells[:, step_index, :]
        level = cells // (ROWS_DEV * NC)
        within = cells % (ROWS_DEV * NC)
        row_id = within // NC + tile_ids * ROWS_DEV
        column = within % NC
        global_ids = ((level * NX + row_id) * NC + column).astype(jnp.int32)
        flat = states[step_index + 1].reshape(-1)
        live = slot_ids < obs_count[:, step_index][:, None]
        terms = jnp.where(live, flat[global_ids] - obs_value[:, step_index, :], 0.0)
        forcing = jnp.zeros_like(flat).at[global_ids.reshape(-1)].add(terms.reshape(-1))
        forcings.append(forcing.reshape(states[0].shape))
        total = total + jnp.sum(terms * terms)
    adjoint = forcings[NSTEP - 1]
    for index in range(NSTEP - 2, -1, -1):
        adjoint = adjoint_step(adjoint, states[index + 1], weights) + forcings[index]
    gradient = adjoint_step(adjoint, states[0], weights)
    misfit = (total / (2.0 * TILES * NSTEP * OBS_CAP)).reshape(1)
    return gradient, misfit
```

```python
import functools

import jax
import jax.numpy as jnp
from jax import lax
from jax.experimental import pallas as pl
from jax.experimental.pallas import tpu as pltpu
from jax.sharding import PartitionSpec as P

F32 = jnp.float32
I32 = jnp.int32
ROWS, CT, LV, LN = 16, 8, 40, 128
H = 3
RX = ROWS + 2 * H
COL = CT * LV
EDGE = H * COL + H * CT
CAP = 512
PAY = 32

VM = pl.BlockSpec(memory_space=pltpu.VMEM)
SM = pl.BlockSpec(memory_space=pltpu.SMEM)
ANY = pl.BlockSpec(memory_space=pl.ANY)
FIELD = jax.ShapeDtypeStruct((RX * COL, LN), F32)
MASK = jax.ShapeDtypeStruct((RX * CT, LN), F32)


def params(mib):
    return pltpu.CompilerParams(vmem_limit_bytes=mib << 20)


def cost(us):
    return pl.CostEstimate(flops=0, bytes_accessed=int(us * 3.0e6), transcendentals=0)


def lanes():
    return lax.broadcasted_iota(I32, (8, LN), 1)


def sublanes():
    return lax.broadcasted_iota(I32, (8, LN), 0)


def stencil_row(src, at, emit):
    lane, sub = lanes(), sublanes()
    first, last = lane == 0, lane == LN - 1
    low, high = sub == 0, sub == 7
    base = pl.multiple_of(at * COL, COL)
    for k in range(LV // 8):
        offs = [base + c * LV + k * 8 for c in range(CT)]
        mids = [src[pl.ds(pl.multiple_of(o, 8), 8), :] for o in offs]
        fwd = [pltpu.roll(v, 1, 1) for v in mids]
        bwd = [pltpu.roll(v, LN - 1, 1) for v in mids]
        for c in range(CT):
            v, o = mids[c], offs[c]
            west = jnp.where(first, fwd[c - 1] if c > 0 else 0.0, fwd[c])
            east = jnp.where(last, bwd[c + 1] if c < CT - 1 else 0.0, bwd[c])
            north = src[pl.ds(pl.multiple_of(o - COL, 8), 8), :]
            south = src[pl.ds(pl.multiple_of(o + COL, 8), 8), :]
            if k > 0:
                down = src[pl.ds(o - 1, 8), :]
            else:
                down = jnp.where(low, v, pltpu.roll(v, 1, 0))
            if k < LV // 8 - 1:
                up = src[pl.ds(o + 1, 8), :]
            else:
                up = jnp.where(high, v, pltpu.roll(v, 7, 0))
            s = ((north + south) + (west + east)) + 0.2 * (down + up)
            emit(c, k, v, s, o)


def mask_row(mask, at, c):
    return mask[pl.ds(at * CT + c, 8, stride=0), :]


def forward_row(src, dst, mask, at):
    ms = [mask_row(mask, at, c) for c in range(CT)]

    def emit(c, k, v, s, o):
        dst[pl.ds(pl.multiple_of(o, 8), 8), :] = ms[c] * (s + v * (0.6 - v * v))

    stencil_row(src, at, emit)


def adjoint_row(src, state, forcing, mask, at):
    ms = [mask_row(mask, at, c) for c in range(CT)]

    def emit(c, k, g, s, o):
        spot = pl.ds(pl.multiple_of(o, 8), 8)
        y = state[spot, :]
        forcing[spot, :] = ms[c] * (s + g * (0.6 - 3.0 * (y * y)) + forcing[spot, :])

    stencil_row(src, at, emit)


def gradient_row(src, state, out, at):
    def emit(c, k, g, s, o):
        y = state[pl.ds(pl.multiple_of(o, 8), 8), :]
        out[pl.ds(pl.multiple_of(o - H * COL, 8), 8), :] = 0.2 * (s + g * (0.6 - 3.0 * (y * y)))

    stencil_row(src, at, emit)


def loop(first, last, body):
    lax.fori_loop(first + H, last + H + 1, lambda at, _: (body(at), 0)[1], 0)


def cell_parts(cell):
    spot = (cell >> 7) & (ROWS * CT - 1)
    return spot, (spot + H * CT) * LV + (cell >> 14), cell & (LN - 1)


def edges_kernel(basic, land, staged, up, down, mask, sems):
    def copy(c):
        return pltpu.make_async_copy(basic.at[:, :, pl.ds(c * LN, LN)], staged.at[c], sems.at[c])

    for c in range(CT):
        copy(c).start()
    for c in range(CT):
        mask[pl.ds(H * CT + c, ROWS, stride=CT), :] = 0.2 * land[:, pl.ds(c * LN, LN)].astype(F32)
    for c in range(CT):
        copy(c).wait()
        flat = staged.at[c].reshape(LV * ROWS, LN)
        for out, first in ((up, 0), (down, ROWS - H)):
            for j in range(H):
                r = first + j
                half = 2.5 * mask_row(mask, r + H, c)
                for k in range(LV // 8):
                    v = flat[pl.ds(k * 8 * ROWS + r, 8, stride=ROWS), :]
                    out[pl.ds((j * CT + c) * LV + k * 8, 8), :] = half * v
                out[pl.ds(H * COL + j * CT + c, 1), :] = mask[pl.ds((r + H) * CT + c, 1), :]


def edges(basic, land):
    return pl.pallas_call(
        edges_kernel,
        out_shape=[
            jax.ShapeDtypeStruct((CT, LV, ROWS, LN), F32),
            jax.ShapeDtypeStruct((EDGE, LN), F32),
            jax.ShapeDtypeStruct((EDGE, LN), F32),
            MASK,
        ],
        in_specs=[ANY, VM],
        out_specs=[VM] * 4,
        scratch_shapes=[pltpu.SemaphoreType.DMA((CT,))],
        compiler_params=params(4),
        cost_estimate=cost(2),
        name="edges",
    )(basic, land)


def interior_kernel(staged, mask, cells, count, value, y0, y1, y2, f1, f2, f3, total, picks, y3):
    lane = lax.broadcasted_iota(I32, (1, LN), 1)
    for c in range(CT):
        flat = staged.at[c].reshape(LV * ROWS, LN)

        def turn(r, _):
            half = 2.5 * mask_row(mask, r + H, c)
            for k in range(LV // 8):
                v = flat[pl.ds(k * 8 * ROWS + r, 8, stride=ROWS), :]
                y0[pl.ds(pl.multiple_of((r + H) * COL + c * LV + k * 8, 8), 8), :] = half * v
            return 0

        lax.fori_loop(0, ROWS, turn, 0)

    zero = jnp.zeros((8, LN), F32)

    def clear(at, _):
        for f in (f1, f2, f3):
            for j in range(COL // 8):
                f[pl.ds(pl.multiple_of(at * COL, 8) + j * 8, 8), :] = zero
        return 0

    lax.fori_loop(0, RX, clear, 0)
    for at in (H - 2, ROWS + H + 1):
        for j in range(COL // 8):
            y2[pl.ds(at * COL + j * 8, 8), :] = zero
    loop(1, 14, lambda at: forward_row(y0, y1, mask, at))
    loop(2, 13, lambda at: forward_row(y1, y2, mask, at))
    loop(3, 12, lambda at: forward_row(y2, y3, mask, at))
    total[...] = zero
    for t, (y, f, scale) in enumerate(((y1, f1, 25.0), (y2, f2, 25.0), (y3, f3, 5.0))):
        near = t + 1
        n = count[0, t]

        def group(i, carry):
            acc, na, nb = carry
            for u in range(8):
                s = i * 8 + u
                cell = cells[0, t, s]
                spot, addr, ln = cell_parts(cell)
                row = spot >> 3
                live = s < n
                top = jnp.logical_and(live, row < near)
                bottom = jnp.logical_and(live, row > ROWS - 1 - near)
                picks[2 * t, na] = s
                picks[2 * t + 1, nb] = s
                na = na + top.astype(I32)
                nb = nb + bottom.astype(I32)
                early = jnp.logical_and(live, jnp.logical_and(row >= near, row <= ROWS - 1 - near))
                hit = lane == jnp.where(early, ln, -1)
                x = 2.0 * y[pl.ds(addr, 1), :]
                d = jnp.where(hit, x - value[0, t, s], 0.0)
                acc = acc + d * d
                m = mask[pl.ds(spot + H * CT, 1), :]
                f[pl.ds(addr, 1), :] = f[pl.ds(addr, 1), :] + scale * (m * d)
            return acc, na, nb

        acc, na, nb = lax.fori_loop(0, (n + 7) // 8, group, (jnp.zeros((1, LN), F32), 0, 0))
        total[pl.ds(t, 1), :] = acc
        for u in range(4):
            picks[2 * t, na + u] = 0
            picks[2 * t + 1, nb + u] = 0
        picks[2 * t, CAP + 8] = na
        picks[2 * t + 1, CAP + 8] = nb


def interior(staged, mask, cells, count, value):
    return pl.pallas_call(
        interior_kernel,
        out_shape=[FIELD] * 6 + [jax.ShapeDtypeStruct((8, LN), F32), jax.ShapeDtypeStruct((6, CAP + 16), I32)],
        in_specs=[VM, VM, SM, SM, SM],
        out_specs=[VM] * 7 + [SM],
        scratch_shapes=[pltpu.VMEM(FIELD.shape, F32)],
        compiler_params=params(8),
        cost_estimate=cost(12),
        name="interior",
    )(staged, mask, cells, count, value)


def bands_kernel(y0i, y1i, y2i, f1i, f2i, f3i, maski, totali, picks, cells, value, above, below,
                 y0, y1, y2, f1, f2, f3, mask, total, upward, downward, y3):
    for halo, first in ((above, 0), (below, ROWS + H)):
        for j in range(H):
            base = (first + j) * COL
            for q in range(COL // 8):
                y0[pl.ds(base + q * 8, 8), :] = halo[pl.ds(j * COL + q * 8, 8), :]
            mask[pl.ds((first + j) * CT, CT), :] = halo[pl.ds(H * COL + j * CT, CT), :]
    for src, dst, reach in ((y0, y1, 2), (y1, y2, 1), (y2, y3, 0)):
        loop(-reach, 2 - reach, lambda at: forward_row(src, dst, mask, at))
        loop(ROWS - 3 + reach, ROWS - 1 + reach, lambda at: forward_row(src, dst, mask, at))
    lane = lax.broadcasted_iota(I32, (1, LN), 1)
    lane8 = lanes()
    upward[...] = jnp.zeros((PAY, LN), F32)
    downward[...] = jnp.zeros((PAY, LN), F32)
    acc = jnp.zeros((1, LN), F32)
    for t, (y, f, scale) in enumerate(((y1, f1, 25.0), (y2, f2, 25.0), (y3, f3, 5.0))):
        for side, pay in ((0, upward), (1, downward)):
            n = picks[2 * t + side, CAP + 8]
            middle = 1 if side == 0 else ROWS - 2
            shift = H * COL * LN
            move = ROWS * COL * LN if side == 0 else -ROWS * COL * LN

            def group(i, acc):
                for u in range(4):
                    j = i * 4 + u
                    s = picks[2 * t + side, j]
                    cell = cells[0, t, s]
                    spot, addr, ln = cell_parts(cell)
                    ln = jnp.where(j < n, ln, -1)
                    x = 2.0 * y[pl.ds(addr, 1), :]
                    d = jnp.where(lane == ln, x - value[0, t, s], 0.0)
                    acc = acc + d * d
                    m = mask[pl.ds(spot + H * CT, 1), :]
                    fm = scale * (m * d)
                    f[pl.ds(addr, 1), :] = f[pl.ds(addr, 1), :] + fm
                    jr, jl = j >> 7, j & (LN - 1)
                    turn = (jl - ln) & (LN - 1)
                    here = pl.ds(4 * t + jr, 1)
                    pay[here, :] = pay[here, :] + pltpu.roll(jnp.broadcast_to(fm, (8, LN)), turn, 1)[0:1]
                    code = (addr * LN + move + (cell & (LN - 1))).astype(F32)
                    there = pl.ds(16 + 4 * t + jr, 1)
                    pay[there, :] = pay[there, :] + jnp.where(lane == jl, code, 0.0)
                    if t == 2:
                        z = y2[pl.ds(addr, 1), :]
                        e = jnp.where(spot >> 3 == middle, -15.0, 0.0) * (z * z) * fm * 0.2
                        over = pl.ds(12 + jr, 1)
                        pay[over, :] = pay[over, :] + pltpu.roll(jnp.broadcast_to(e, (8, LN)), turn, 1)[0:1]
                return acc

            acc = lax.fori_loop(0, (n + 3) // 4, group, acc)
            pay[28:29, :] = pay[28:29, :] + jnp.where(lane == t, n.astype(F32), 0.0)
    both = totali[...]
    total[...] = both + jnp.where(sublanes() == 0, jnp.broadcast_to(acc, (8, LN)), 0.0)


def bands(y0, y1, y2, f1, f2, f3, mask, total, picks, cells, value, above, below):
    return pl.pallas_call(
        bands_kernel,
        out_shape=[FIELD] * 6 + [MASK, jax.ShapeDtypeStruct((8, LN), F32)] + [jax.ShapeDtypeStruct((PAY, LN), F32)] * 2,
        in_specs=[VM] * 8 + [SM] * 3 + [VM] * 2,
        out_specs=[VM] * 10,
        input_output_aliases={i: i for i in range(8)},
        scratch_shapes=[pltpu.VMEM(FIELD.shape, F32)],
        compiler_params=params(8),
        cost_estimate=cost(4),
        name="bands",
    )(y0, y1, y2, f1, f2, f3, mask, total, picks, cells, value, above, below)


def inner_adjoint_kernel(y0, y1, y2, f1i, f2i, f3, mask, f1, f2, grad):
    loop(1, 14, lambda at: adjoint_row(f3, y2, f2, mask, at))
    loop(2, 13, lambda at: adjoint_row(f2, y1, f1, mask, at))
    loop(3, 12, lambda at: gradient_row(f1, y0, grad, at))


def inner_adjoint(y0, y1, y2, f1, f2, f3, mask):
    return pl.pallas_call(
        inner_adjoint_kernel,
        out_shape=[FIELD] * 2 + [jax.ShapeDtypeStruct((ROWS * COL, LN), F32)],
        in_specs=[VM] * 7,
        out_specs=[VM] * 3,
        input_output_aliases={3: 0, 4: 1},
        compiler_params=params(4),
        cost_estimate=cost(5),
        name="inner_adjoint",
    )(y0, y1, y2, f1, f2, f3, mask)


def finish_kernel(y0, y1, y2, f1i, f2i, f3i, mask, gradi, above, below, f1, f2, f3, grad, out, staged, sems):
    lane = lax.broadcasted_iota(I32, (1, LN), 1)
    for pay in (above, below):
        for t, f in enumerate((f1, f2, f3)):
            n = pay[28, t].astype(I32)

            def item(j, _):
                jr, jl = j >> 7, j & (LN - 1)
                code = pay[16 + 4 * t + jr, jl].astype(I32)
                addr, ln = code >> 7, code & (LN - 1)
                spot = pl.ds(addr, 1)
                f[spot, :] = f[spot, :] + jnp.where(lane == ln, pay[4 * t + jr, jl], 0.0)
                if t == 2:
                    f2[spot, :] = f2[spot, :] + jnp.where(lane == ln, pay[12 + jr, jl], 0.0)
                return 0

            lax.fori_loop(0, n, item, 0)
    for src, state, dst, reach in ((f3, y2, f2, 2), (f2, y1, f1, 1)):
        loop(-reach, 2 - reach - 0, lambda at: adjoint_row(src, state, dst, mask, at))
        loop(ROWS - 3 + reach, ROWS - 1 + reach, lambda at: adjoint_row(src, state, dst, mask, at))
    loop(0, 2, lambda at: gradient_row(f1, y0, grad, at))
    loop(ROWS - 3, ROWS - 1, lambda at: gradient_row(f1, y0, grad, at))

    def copy(c):
        return pltpu.make_async_copy(staged.at[c], out.at[:, :, pl.ds(c * LN, LN)], sems.at[c])

    for c in range(CT):
        def turn(k, _):
            for half in range(2):
                v = grad[pl.ds(half * 8 * COL + c * LV + k, 8, stride=COL), :]
                staged[c, k, pl.ds(half * 8, 8), :] = v
            return 0

        lax.fori_loop(0, LV, turn, 0, unroll=8)
        copy(c).start()
    for c in range(CT):
        copy(c).wait()


def finish(y0, y1, y2, f1, f2, f3, mask, grad, above, below):
    return pl.pallas_call(
        finish_kernel,
        out_shape=[FIELD] * 3 + [jax.ShapeDtypeStruct((ROWS * COL, LN), F32), jax.ShapeDtypeStruct((LV, ROWS, CT * LN), F32)],
        in_specs=[VM] * 8 + [SM] * 2,
        out_specs=[VM] * 4 + [ANY],
        input_output_aliases={3: 0, 4: 1, 5: 2, 7: 3},
        scratch_shapes=[pltpu.VMEM((CT, LV, ROWS, LN), F32), pltpu.SemaphoreType.DMA((CT,))],
        compiler_params=params(8),
        cost_estimate=cost(4),
        name="finish",
    )(y0, y1, y2, f1, f2, f3, mask, grad, above, below)[4]


def add_kernel(a, b, out):
    out[...] = a[...] + b[...]


def reduce_kernel(scale, a, b, out):
    out[...] = jnp.sum(a[...] + b[...], keepdims=True) * scale


def small(kernel, shape, a, b, name):
    return pl.pallas_call(
        kernel,
        out_shape=jax.ShapeDtypeStruct(shape, F32),
        in_specs=[VM, VM],
        out_specs=VM,
        compiler_params=params(1),
        cost_estimate=cost(0.1),
        name=name,
    )(a, b)


def sum_along(x, scale):
    size = lax.axis_size("along")
    if size & (size - 1):
        other, x = jnp.zeros_like(x), lax.psum(x, "along")
    else:
        step, other = 1, None
        while step < size:
            if other is not None:
                x = small(add_kernel, x.shape, x, other, "add")
            other = lax.ppermute(x, "along", [(i, i ^ step) for i in range(size)])
            step *= 2
    return small(functools.partial(reduce_kernel, scale), (1, 1), x, other, "reduce").reshape(1)


def local(basic_state, land_sea, obs_cells, obs_count, obs_value):
    size = lax.axis_size("along")
    later = [(i, i + 1) for i in range(size - 1)]
    earlier = [(i + 1, i) for i in range(size - 1)]
    staged, up, down, mask = edges(basic_state, land_sea)
    above = lax.ppermute(down, "along", later)
    below = lax.ppermute(up, "along", earlier)
    y0, y1, y2, f1, f2, f3, total, picks = interior(staged, mask, obs_cells, obs_count, obs_value)
    y0, y1, y2, f1, f2, f3, mask, total, upward, downward = bands(
        y0, y1, y2, f1, f2, f3, mask, total, picks, obs_cells, obs_value, above, below
    )
    above = lax.ppermute(downward, "along", later)
    below = lax.ppermute(upward, "along", earlier)
    misfit = sum_along(total, 1.0 / (2.0 * size * obs_cells.shape[1] * obs_cells.shape[2]))
    f1, f2, grad = inner_adjoint(y0, y1, y2, f1, f2, f3, mask)
    gradient = finish(y0, y1, y2, f1, f2, f3, mask, grad, above, below)
    return gradient, misfit


def solution(mesh):
    in_specs = (
        P(None, ("ens", "along"), None),
        P(("ens", "along"), None),
        P(("ens", "along"), None, None),
        P(("ens", "along"), None),
        P(("ens", "along"), None, None),
    )
    out_specs = (P(None, ("ens", "along"), None), P("ens"))
    return jax.shard_map(local, mesh=mesh, in_specs=in_specs, out_specs=out_specs, check_vma=False)
```

```python
import functools

import jax
import jax.numpy as jnp
from jax import lax
from jax.experimental import pallas as pl
from jax.experimental.pallas import tpu as pltpu
from jax.sharding import PartitionSpec as P

F32 = jnp.float32
I32 = jnp.int32
ROWS, CT, LV, LN = 16, 8, 40, 128
H = 3
RX = ROWS + 2 * H
COL = CT * LV
EDGE = H * COL + H * CT + 16
CAP = 512
NT = 3
PAY = 16

VM = pl.BlockSpec(memory_space=pltpu.VMEM)
SM = pl.BlockSpec(memory_space=pltpu.SMEM)
HBM = pl.BlockSpec(memory_space=pltpu.MemorySpace.HBM)
ANY = pl.BlockSpec(memory_space=pl.ANY)
FIELD = jax.ShapeDtypeStruct((RX * COL, LN), F32)
MASK = jax.ShapeDtypeStruct((RX * CT, LN), F32)


def params(mib):
    return pltpu.CompilerParams(vmem_limit_bytes=mib << 20)


def cost(us):
    return pl.CostEstimate(flops=0, bytes_accessed=int(us * 3.0e6), transcendentals=0)


def lanes():
    return lax.broadcasted_iota(I32, (8, LN), 1)


def sublanes():
    return lax.broadcasted_iota(I32, (8, LN), 0)


def stencil_row(src, at, emit):
    lane, sub = lanes(), sublanes()
    first, last = lane == 0, lane == LN - 1
    low, high = sub == 0, sub == 7
    base = pl.multiple_of(at * COL, COL)
    for k in range(LV // 8):
        offs = [base + c * LV + k * 8 for c in range(CT)]
        mids = [src[pl.ds(pl.multiple_of(o, 8), 8), :] for o in offs]
        fwd = [pltpu.roll(v, 1, 1) for v in mids]
        bwd = [pltpu.roll(v, LN - 1, 1) for v in mids]
        for c in range(CT):
            v, o = mids[c], offs[c]
            west = jnp.where(first, fwd[c - 1] if c > 0 else 0.0, fwd[c])
            east = jnp.where(last, bwd[c + 1] if c < CT - 1 else 0.0, bwd[c])
            north = src[pl.ds(pl.multiple_of(o - COL, 8), 8), :]
            south = src[pl.ds(pl.multiple_of(o + COL, 8), 8), :]
            if k > 0:
                down = src[pl.ds(o - 1, 8), :]
            else:
                down = jnp.where(low, v, pltpu.roll(v, 1, 0))
            if k < LV // 8 - 1:
                up = src[pl.ds(o + 1, 8), :]
            else:
                up = jnp.where(high, v, pltpu.roll(v, 7, 0))
            s = ((north + south) + (west + east)) + 0.2 * (down + up)
            emit(c, k, v, s, o)


def mask_row(mask, at, c):
    return mask[pl.ds(at * CT + c, 8, stride=0), :]


def forward_row(src, dst, mask, at):
    ms = [mask_row(mask, at, c) for c in range(CT)]

    def emit(c, k, v, s, o):
        dst[pl.ds(pl.multiple_of(o, 8), 8), :] = ms[c] * (s + v * (0.6 - v * v))

    stencil_row(src, at, emit)


def adjoint_row(src, state, forcing, mask, at):
    ms = [mask_row(mask, at, c) for c in range(CT)]

    def emit(c, k, g, s, o):
        spot = pl.ds(pl.multiple_of(o, 8), 8)
        y = state[spot, :]
        forcing[spot, :] = ms[c] * (s + g * (0.6 - 3.0 * (y * y)) + forcing[spot, :])

    stencil_row(src, at, emit)


def gradient_row(src, state, out, at):
    def emit(c, k, g, s, o):
        y = state[pl.ds(pl.multiple_of(o, 8), 8), :]
        out[pl.ds(pl.multiple_of(o - H * COL, 8), 8), :] = 0.2 * (s + g * (0.6 - 3.0 * (y * y)))

    stencil_row(src, at, emit)


def loop(first, last, body):
    lax.fori_loop(first + H, last + H + 1, lambda at, _: (body(at), 0)[1], 0)


def column(ref, out, at):
    col = ref[at] & (CT * LN - 1)
    sub = lax.broadcasted_iota(I32, (16, CAP), 0)

    def part(i, _):
        out[pl.ds(pl.multiple_of(i * 16, 16), 16), :] = jnp.where(col == sub + i * 16, 1.0, 0.0).astype(jnp.bfloat16)
        return 0

    lax.fori_loop(0, CT * LN // 16, part, 0, unroll=2)


def split(d):
    high = d.astype(jnp.bfloat16).astype(F32)
    return high, d - high


def spread(line, terms, left, first, count):
    high, low = split(terms)
    sub = lax.broadcasted_iota(I32, (16, CAP), 0)
    for i in range(count // 16):
        hit = line == sub + i * 16
        where = pl.ds(first + i * 16, 16)
        left[where, pl.ds(0, CAP)] = jnp.where(hit, high, 0.0).astype(jnp.bfloat16)
        left[where, pl.ds(CAP, CAP)] = jnp.where(hit, low, 0.0).astype(jnp.bfloat16)


def product(left, rows, cols):
    dims = (((1,), (1,)), ((), ()))
    return lax.dot_general(left[pl.ds(0, rows), pl.ds(0, CAP)], cols, dims, preferred_element_type=F32) + lax.dot_general(
        left[pl.ds(0, rows), pl.ds(CAP, CAP)], cols, dims, preferred_element_type=F32
    )


def edges_kernel(basic, land, cells, staged, up, down, mask, sems):
    def copy(c):
        return pltpu.make_async_copy(basic.at[:, :, pl.ds(c * LN, LN)], staged.at[c], sems.at[c])

    for c in range(CT):
        copy(c).start()
    for c in range(CT):
        mask[pl.ds(H * CT + c, ROWS, stride=CT), :] = 0.2 * land[:, pl.ds(c * LN, LN)].astype(F32)
    for t in range(NT):
        for q in range(CAP // LN):
            row = cells[t, :, pl.ds(q * LN, LN)].astype(F32)
            for out in (up, down):
                out[pl.ds(H * COL + H * CT + t * 4 + q, 1), :] = row
    for c in range(CT):
        copy(c).wait()
        flat = staged.at[c].reshape(LV * ROWS, LN)
        for out, first in ((up, 0), (down, ROWS - H)):
            for j in range(H):
                r = first + j
                half = 2.5 * mask_row(mask, r + H, c)
                for k in range(LV // 8):
                    v = flat[pl.ds(k * 8 * ROWS + r, 8, stride=ROWS), :]
                    out[pl.ds((j * CT + c) * LV + k * 8, 8), :] = half * v
                out[pl.ds(H * COL + j * CT + c, 1), :] = mask[pl.ds((r + H) * CT + c, 1), :]


def edges(basic, land, cells):
    return pl.pallas_call(
        edges_kernel,
        out_shape=[
            jax.ShapeDtypeStruct((CT, LV, ROWS, LN), F32),
            jax.ShapeDtypeStruct((EDGE, LN), F32),
            jax.ShapeDtypeStruct((EDGE, LN), F32),
            MASK,
        ],
        in_specs=[HBM, VM, VM],
        out_specs=[VM] * 4,
        scratch_shapes=[pltpu.SemaphoreType.DMA((CT,))],
        compiler_params=params(4),
        cost_estimate=cost(2),
        name="edges",
    )(basic, land, cells)


def interior_kernel(staged, mask, cells, y0, y1, y2, y3, cols):
    for c in range(CT):
        flat = staged.at[c].reshape(LV * ROWS, LN)

        def turn(r, _):
            half = 2.5 * mask_row(mask, r + H, c)
            for k in range(LV // 8):
                v = flat[pl.ds(k * 8 * ROWS + r, 8, stride=ROWS), :]
                y0[pl.ds(pl.multiple_of((r + H) * COL + c * LV + k * 8, 8), 8), :] = half * v
            return 0

        lax.fori_loop(0, ROWS, turn, 0)

    zero = jnp.zeros((8, LN), F32)
    for at in (H - 2, ROWS + H + 1):
        for j in range(COL // 8):
            y2[pl.ds(at * COL + j * 8, 8), :] = zero
    loop(1, 14, lambda at: forward_row(y0, y1, mask, at))
    loop(2, 13, lambda at: forward_row(y1, y2, mask, at))
    loop(3, 12, lambda at: forward_row(y2, y3, mask, at))
    for t in range(NT):
        column(cells, cols.at[t], t)


def interior(staged, mask, cells):
    return pl.pallas_call(
        interior_kernel,
        out_shape=[FIELD] * 4 + [jax.ShapeDtypeStruct((NT, CT * LN, CAP), jnp.bfloat16)],
        in_specs=[VM] * 3,
        out_specs=[VM] * 5,
        compiler_params=params(8),
        cost_estimate=cost(9),
        name="interior",
    )(staged, mask, cells)


def bands_kernel(y0i, y1i, y2i, y3i, maski, cells, count, value, spots, above, below,
                 y0, y1, y2, mask, total, pay, terms, g1, g2, g3, g4, at_ref, sem):
    fetch = pltpu.make_async_copy(spots, at_ref, sem)
    fetch.start()
    y3 = y3i
    for halo, first in ((above, 0), (below, ROWS + H)):
        for j in range(H):
            base = (first + j) * COL
            for q in range(COL // 8):
                y0[pl.ds(base + q * 8, 8), :] = halo[pl.ds(j * COL + q * 8, 8), :]
            mask[pl.ds((first + j) * CT, CT), :] = halo[pl.ds(H * COL + j * CT, CT), :]
    for src, dst, reach in ((y0, y1, 2), (y1, y2, 1), (y2, y3, 0)):
        loop(-reach, 2 - reach, lambda at: forward_row(src, dst, mask, at))
        loop(ROWS - 3 + reach, ROWS - 1 + reach, lambda at: forward_row(src, dst, mask, at))
    fetch.wait()
    many = 8

    def group(i, _):
        for u in range(many):
            s = i * many + u
            third = at_ref[2 * CAP + s]
            g1[pl.ds(s, 1), :] = y1[pl.ds(at_ref[s], 1), :]
            g2[pl.ds(s, 1), :] = y2[pl.ds(at_ref[CAP + s], 1), :]
            g3[pl.ds(s, 1), :] = y3[pl.ds(third, 1), :]
            g4[pl.ds(s, 1), :] = y2[pl.ds(third, 1), :]
        return 0

    lax.fori_loop(0, CAP // many, group, 0)
    sub = lax.broadcasted_iota(I32, (LN, LN), 0)
    slot = lax.broadcasted_iota(I32, (1, LN), 1)
    acc = jnp.zeros((1, LN), F32)
    for t, g in enumerate((g1, g2, g3)):
        for q in range(CAP // LN):
            part = pl.ds(q * LN, LN)
            hit = (cells[t, :, part] & (LN - 1)) == sub
            x = jnp.sum(jnp.where(hit, g[part, :].T, 0.0), axis=0, keepdims=True)
            live = slot + q * LN < count[0, t]
            d = jnp.where(live, 2.0 * x - value[t, :, part], 0.0)
            acc = acc + d * d
            pay[pl.ds(4 * t + q, 1), :] = d
            terms[pl.ds(t, 1), part] = d
            if t == NT - 1:
                z = jnp.sum(jnp.where(hit, g4[part, :].T, 0.0), axis=0, keepdims=True)
                pay[pl.ds(12 + q, 1), :] = -3.0 * (z * z) * d
    total[...] = jnp.where(sublanes() == 0, jnp.broadcast_to(acc, (8, LN)), 0.0)


def bands(y0, y1, y2, y3, mask, cells, count, value, spots, above, below):
    rows = pltpu.VMEM((CAP, LN), F32)
    return pl.pallas_call(
        bands_kernel,
        out_shape=[FIELD] * 3
        + [MASK, jax.ShapeDtypeStruct((8, LN), F32), jax.ShapeDtypeStruct((PAY, LN), F32), jax.ShapeDtypeStruct((8, CAP), F32)],
        in_specs=[VM] * 6 + [SM, VM, ANY] + [VM] * 2,
        out_specs=[VM] * 7,
        input_output_aliases={0: 0, 1: 1, 2: 2, 4: 3},
        scratch_shapes=[rows, rows, rows, rows, pltpu.SMEM((NT * CAP,), I32), pltpu.SemaphoreType.DMA],
        compiler_params=params(8),
        cost_estimate=cost(5),
        name="bands",
    )(y0, y1, y2, y3, mask, cells, count, value, spots, above, below)


def inner_adjoint_kernel(y0, y1, y2, mask, cells, terms, cols, above, below, f1, f2, f3, grad, far, left):
    for t, (f, scale) in enumerate(((f1, 25.0), (f2, 25.0), (f3, 5.0))):
        cell = cells[t]
        line = ((cell >> 10) & (ROWS - 1)) * LV + (cell >> 14)
        spread(line, terms[pl.ds(t, 1), :], left, 0, ROWS * LV)

        def block(p, _):
            out = product(left, ROWS * LV, cols[t, pl.ds(pl.multiple_of(p * 2 * LN, 2 * LN), 2 * LN), :])
            for r in range(ROWS):
                for j in range(2):
                    c = 2 * p + j
                    m = scale * mask_row(mask, r + H, c)
                    for k in range(LV // 8):
                        spot = pl.ds(pl.multiple_of((r + H) * COL + c * LV + k * 8, 8), 8)
                        f[spot, :] = m * out[r * LV + k * 8 : r * LV + k * 8 + 8, j * LN : (j + 1) * LN]
            return 0

        lax.fori_loop(0, CT // 2, block, 0)
    loop(1, 14, lambda at: adjoint_row(f3, y2, f2, mask, at))
    loop(2, 13, lambda at: adjoint_row(f2, y1, f1, mask, at))
    loop(3, 12, lambda at: gradient_row(f1, y0, grad, at))
    for side, halo in enumerate((above, below)):
        for t in range(NT):
            for q in range(CAP // LN):
                far[NT * side + t, :, pl.ds(q * LN, LN)] = halo[pl.ds(H * COL + H * CT + 4 * t + q, 1), :].astype(I32)


def inner_adjoint(y0, y1, y2, mask, cells, terms, cols, above, below):
    return pl.pallas_call(
        inner_adjoint_kernel,
        out_shape=[FIELD] * 3 + [jax.ShapeDtypeStruct((ROWS * COL, LN), F32), jax.ShapeDtypeStruct((2 * NT, 1, CAP), I32)],
        in_specs=[VM] * 9,
        out_specs=[VM] * 5,
        scratch_shapes=[pltpu.VMEM((ROWS * LV, 2 * CAP), jnp.bfloat16)],
        compiler_params=params(12),
        cost_estimate=cost(9),
        name="inner_adjoint",
    )(y0, y1, y2, mask, cells, terms, cols, above, below)


def finish_kernel(y0, y1, y2, f1i, f2i, f3i, mask, gradi, far, above, below, f1, f2, f3, grad, out, staged, cols, left, line_ref, sems):
    for side, pay in enumerate((above, below)):
        for t, (f, scale) in enumerate(((f1, 25.0), (f2, 25.0), (f3, 5.0))):
            near = t + 1
            cell = far[NT * side + t]
            column(far, cols, NT * side + t)
            row, level = (cell >> 10) & (ROWS - 1), cell >> 14
            line = (row - (ROWS - near if side == 0 else 0)) * LV + level
            for q in range(CAP // LN):
                line_ref[pl.ds(0, 1), pl.ds(q * LN, LN)] = pay[pl.ds(4 * t + q, 1), :]
                if t == NT - 1:
                    line_ref[pl.ds(1, 1), pl.ds(q * LN, LN)] = pay[pl.ds(12 + q, 1), :]
            deep = (near * LV + 15) // 16 * 16
            spread(line, line_ref[pl.ds(0, 1), :], left, 0, deep)
            if t == NT - 1:
                deep = 128
                second = jnp.where(row == (ROWS - 2 if side == 0 else 1), level, -1)
                spread(second, line_ref[pl.ds(1, 1), :], left, deep, 48)
                deep = 176
            base = H - near if side == 0 else ROWS + H

            def block(p, _):
                res = product(left, deep, cols[pl.ds(pl.multiple_of(p * 2 * LN, 2 * LN), 2 * LN), :])
                for j in range(2):
                    c = 2 * p + j
                    for r in range(near):
                        m = scale * mask_row(mask, base + r, c)
                        for k in range(LV // 8):
                            spot = pl.ds(pl.multiple_of((base + r) * COL + c * LV + k * 8, 8), 8)
                            f[spot, :] = m * res[r * LV + k * 8 : r * LV + k * 8 + 8, j * LN : (j + 1) * LN]
                    if t == NT - 1:
                        m = 5.0 * mask_row(mask, base + 1, c)
                        for k in range(LV // 8):
                            spot = pl.ds(pl.multiple_of((base + 1) * COL + c * LV + k * 8, 8), 8)
                            f2[spot, :] = f2[spot, :] + m * res[128 + k * 8 : 136 + k * 8, j * LN : (j + 1) * LN]
                return 0

            lax.fori_loop(0, CT // 2, block, 0)
    for src, state, dst, reach in ((f3, y2, f2, 2), (f2, y1, f1, 1)):
        loop(-reach, 2 - reach, lambda at: adjoint_row(src, state, dst, mask, at))
        loop(ROWS - 3 + reach, ROWS - 1 + reach, lambda at: adjoint_row(src, state, dst, mask, at))
    loop(0, 2, lambda at: gradient_row(f1, y0, grad, at))
    loop(ROWS - 3, ROWS - 1, lambda at: gradient_row(f1, y0, grad, at))

    def copy(c):
        return pltpu.make_async_copy(staged.at[c], out.at[:, :, pl.ds(c * LN, LN)], sems.at[c])

    for c in range(CT):
        def turn(k, _):
            for half in range(2):
                v = grad[pl.ds(half * 8 * COL + c * LV + k, 8, stride=COL), :]
                staged[c, k, pl.ds(half * 8, 8), :] = v
            return 0

        lax.fori_loop(0, LV, turn, 0, unroll=8)
        copy(c).start()
    for c in range(CT):
        copy(c).wait()


def finish(y0, y1, y2, f1, f2, f3, mask, grad, far, above, below):
    return pl.pallas_call(
        finish_kernel,
        out_shape=[FIELD] * 3 + [jax.ShapeDtypeStruct((ROWS * COL, LN), F32), jax.ShapeDtypeStruct((LV, ROWS, CT * LN), F32)],
        in_specs=[VM] * 11,
        out_specs=[VM] * 4 + [ANY],
        input_output_aliases={3: 0, 4: 1, 5: 2, 7: 3},
        scratch_shapes=[
            pltpu.VMEM((CT, LV, ROWS, LN), F32),
            pltpu.VMEM((CT * LN, CAP), jnp.bfloat16),
            pltpu.VMEM((176, 2 * CAP), jnp.bfloat16),
            pltpu.VMEM((8, CAP), F32),
            pltpu.SemaphoreType.DMA((CT,)),
        ],
        compiler_params=params(12),
        cost_estimate=cost(4),
        name="finish",
    )(y0, y1, y2, f1, f2, f3, mask, grad, far, above, below)[4]


def add_kernel(a, b, out):
    out[...] = a[...] + b[...]


def reduce_kernel(scale, a, b, out):
    out[...] = jnp.sum(a[...] + b[...], keepdims=True) * scale


def small(kernel, shape, a, b, name):
    return pl.pallas_call(
        kernel,
        out_shape=jax.ShapeDtypeStruct(shape, F32),
        in_specs=[VM, VM],
        out_specs=VM,
        compiler_params=params(1),
        cost_estimate=cost(0.1),
        name=name,
    )(a, b)


def sum_along(x, scale):
    size = lax.axis_size("along")
    if size & (size - 1):
        other, x = jnp.zeros_like(x), lax.psum(x, "along")
    else:
        step, other = 1, None
        while step < size:
            if other is not None:
                x = small(add_kernel, x.shape, x, other, "add")
            other = lax.ppermute(x, "along", [(i, i ^ step) for i in range(size)])
            step *= 2
    return small(functools.partial(reduce_kernel, scale), (1, 1), x, other, "reduce").reshape(1)


def local(basic_state, land_sea, obs_cells, obs_count, obs_value):
    size = lax.axis_size("along")
    later = [(i, i + 1) for i in range(size - 1)]
    earlier = [(i + 1, i) for i in range(size - 1)]
    cells = obs_cells.transpose(1, 0, 2)
    value = obs_value.transpose(1, 0, 2)
    spots = (((cells >> 7) & (ROWS * CT - 1)) + H * CT) * LV + (cells >> 14)
    staged, up, down, mask = edges(basic_state, land_sea, cells)
    above = lax.ppermute(down, "along", later)
    below = lax.ppermute(up, "along", earlier)
    y0, y1, y2, y3, cols = interior(staged, mask, cells)
    y0, y1, y2, mask, total, pay, terms = bands(
        y0, y1, y2, y3, mask, cells, obs_count, value, spots.reshape(-1), above, below
    )
    above2 = lax.ppermute(pay, "along", later)
    below2 = lax.ppermute(pay, "along", earlier)
    misfit = sum_along(total, 1.0 / (2.0 * size * obs_cells.shape[1] * obs_cells.shape[2]))
    f1, f2, f3, grad, far = inner_adjoint(y0, y1, y2, mask, cells, terms, cols, above, below)
    gradient = finish(y0, y1, y2, f1, f2, f3, mask, grad, far, above2, below2)
    return gradient, misfit


def solution(mesh):
    in_specs = (
        P(None, ("ens", "along"), None),
        P(("ens", "along"), None),
        P(("ens", "along"), None, None),
        P(("ens", "along"), None),
        P(("ens", "along"), None, None),
    )
    out_specs = (P(None, ("ens", "along"), None), P("ens"))
    return jax.shard_map(local, mesh=mesh, in_specs=in_specs, out_specs=out_specs, check_vma=False)
```

```python
import functools

import jax
import jax.numpy as jnp
from jax import lax
from jax.experimental import pallas as pl
from jax.experimental.pallas import tpu as pltpu
from jax.sharding import PartitionSpec as P

F32 = jnp.float32
I32 = jnp.int32
ROWS, CT, LV, LN = 16, 8, 40, 128
H = 3
RX = ROWS + 2 * H
COL = CT * LV
EDGE = H * COL + H * CT
CAP = 512
NT = 3
PAY = 32
CODE = 16

VM = pl.BlockSpec(memory_space=pltpu.VMEM)
SM = pl.BlockSpec(memory_space=pltpu.SMEM)
HBM = pl.BlockSpec(memory_space=pltpu.MemorySpace.HBM)
ANY = pl.BlockSpec(memory_space=pl.ANY)
FIELD = jax.ShapeDtypeStruct((RX * COL, LN), F32)
MASK = jax.ShapeDtypeStruct((RX * CT, LN), F32)


def params(mib):
    return pltpu.CompilerParams(vmem_limit_bytes=mib << 20)


def cost(us):
    return pl.CostEstimate(flops=0, bytes_accessed=int(us * 3.0e6), transcendentals=0)


def lanes():
    return lax.broadcasted_iota(I32, (8, LN), 1)


def sublanes():
    return lax.broadcasted_iota(I32, (8, LN), 0)


def stencil_row(src, at, emit):
    lane, sub = lanes(), sublanes()
    first, last = lane == 0, lane == LN - 1
    low, high = sub == 0, sub == 7
    base = pl.multiple_of(at * COL, COL)
    for k in range(LV // 8):
        offs = [base + c * LV + k * 8 for c in range(CT)]
        mids = [src[pl.ds(pl.multiple_of(o, 8), 8), :] for o in offs]
        fwd = [pltpu.roll(v, 1, 1) for v in mids]
        bwd = [pltpu.roll(v, LN - 1, 1) for v in mids]
        for c in range(CT):
            v, o = mids[c], offs[c]
            west = jnp.where(first, fwd[c - 1] if c > 0 else 0.0, fwd[c])
            east = jnp.where(last, bwd[c + 1] if c < CT - 1 else 0.0, bwd[c])
            north = src[pl.ds(pl.multiple_of(o - COL, 8), 8), :]
            south = src[pl.ds(pl.multiple_of(o + COL, 8), 8), :]
            if k > 0:
                down = src[pl.ds(o - 1, 8), :]
            else:
                down = jnp.where(low, v, pltpu.roll(v, 1, 0))
            if k < LV // 8 - 1:
                up = src[pl.ds(o + 1, 8), :]
            else:
                up = jnp.where(high, v, pltpu.roll(v, 7, 0))
            s = ((north + south) + (west + east)) + 0.2 * (down + up)
            emit(c, k, v, s, o)


class Fetch:
    def __init__(self, src, dst, sems):
        self.parts = [pltpu.make_async_copy(src.at[t, 0], dst.at[pl.ds(t * CAP, CAP)], sems.at[t]) for t in range(NT)]

    def start(self):
        for part in self.parts:
            part.start()

    def wait(self):
        for part in self.parts:
            part.wait()


def mask_row(mask, at, c):
    return mask[pl.ds(at * CT + c, 8, stride=0), :]


def forward_row(src, dst, mask, at):
    ms = [mask_row(mask, at, c) for c in range(CT)]

    def emit(c, k, v, s, o):
        dst[pl.ds(pl.multiple_of(o, 8), 8), :] = ms[c] * (s + v * (0.6 - v * v))

    stencil_row(src, at, emit)


def adjoint_row(src, state, forcing, mask, at):
    ms = [mask_row(mask, at, c) for c in range(CT)]

    def emit(c, k, g, s, o):
        spot = pl.ds(pl.multiple_of(o, 8), 8)
        y = state[spot, :]
        forcing[spot, :] = ms[c] * ((s + g * (0.6 - 3.0 * (y * y))) + forcing[spot, :])

    stencil_row(src, at, emit)


def gradient_row(src, state, out, at):
    def emit(c, k, g, s, o):
        y = state[pl.ds(pl.multiple_of(o, 8), 8), :]
        out[pl.ds(pl.multiple_of(o - H * COL, 8), 8), :] = 0.2 * (s + g * (0.6 - 3.0 * (y * y)))

    stencil_row(src, at, emit)


def loop(first, last, body):
    lax.fori_loop(first + H, last + H + 1, lambda at, _: (body(at), 0)[1], 0)


def edges_kernel(basic, land_at, staged, up, down, mask, land, sems):
    def copy(c):
        return pltpu.make_async_copy(basic.at[:, :, pl.ds(c * LN, LN)], staged.at[c], sems.at[c])

    sea = pltpu.make_async_copy(land_at, land, sems.at[CT])
    sea.start()
    for c in range(CT):
        copy(c).start()
    sea.wait()
    for c in range(CT):
        mask[pl.ds(H * CT + c, ROWS, stride=CT), :] = 0.2 * land[:, pl.ds(c * LN, LN)].astype(F32)
    for c in range(CT):
        copy(c).wait()
        flat = staged.at[c].reshape(LV * ROWS, LN)
        for out, first in ((up, 0), (down, ROWS - H)):
            for j in range(H):
                r = first + j
                half = 2.5 * mask_row(mask, r + H, c)
                for k in range(LV // 8):
                    v = flat[pl.ds(k * 8 * ROWS + r, 8, stride=ROWS), :]
                    out[pl.ds((j * CT + c) * LV + k * 8, 8), :] = half * v
                out[pl.ds(H * COL + j * CT + c, 1), :] = mask[pl.ds((r + H) * CT + c, 1), :]


def edges(basic, land):
    return pl.pallas_call(
        edges_kernel,
        out_shape=[
            jax.ShapeDtypeStruct((CT, LV, ROWS, LN), F32),
            jax.ShapeDtypeStruct((EDGE, LN), F32),
            jax.ShapeDtypeStruct((EDGE, LN), F32),
            MASK,
        ],
        in_specs=[HBM, HBM],
        out_specs=[VM] * 4,
        scratch_shapes=[pltpu.VMEM((ROWS, CT * LN), I32), pltpu.SemaphoreType.DMA((CT + 1,))],
        compiler_params=params(4),
        cost_estimate=cost(2),
        name="edges",
    )(pltpu.with_memory_space_constraint(basic, pltpu.HBM), pltpu.with_memory_space_constraint(land, pltpu.HBM))


def order_kernel(cells, count, value, addr, live, sval, lane, spot, second, codes):
    slot = lax.broadcasted_iota(I32, (1, CAP), 1)
    ups, downs = [], []
    for t in range(NT):
        row = (cells[t] >> 10) & (ROWS - 1)
        alive = slot < count[0, t]
        ups.append(jnp.logical_and(alive, row <= t))
        downs.append(jnp.logical_and(alive, row >= ROWS - 1 - t))
    one = [jnp.where(f, 1.0, 0.0) for f in ups + downs]
    flags = jnp.concatenate(one + [jnp.zeros((10, CAP), F32)], axis=0).astype(jnp.bfloat16)
    tri = jnp.where(
        lax.broadcasted_iota(I32, (CAP, CAP), 0) < lax.broadcasted_iota(I32, (CAP, CAP), 1), 1.0, 0.0
    ).astype(jnp.bfloat16)
    before = jnp.dot(flags, tri, preferred_element_type=F32)
    codes[...] = jnp.zeros((CODE, LN), F32)
    sub = lax.broadcasted_iota(I32, (CAP, CAP), 0)
    first = lax.broadcasted_iota(I32, (1, LN), 1)
    tally = jnp.zeros((1, LN), F32)
    for t in range(NT):
        up, down = ups[t], downs[t]
        pu, pd = before[t : t + 1], before[NT + t : NT + t + 1]
        nu = jnp.sum(one[t], axis=1, keepdims=True)
        nd = jnp.sum(one[NT + t], axis=1, keepdims=True)
        tally = tally + jnp.where(first == t, nu, 0.0) + jnp.where(first == NT + t, nd, 0.0)
        rank = jnp.where(up, pu, jnp.where(down, CAP - nd + pd, nu + slot.astype(F32) - pu - pd)).astype(I32)
        place = jnp.where(sub == rank, 1.0, 0.0).astype(jnp.bfloat16)
        cell, v = cells[t], value[t]
        v1 = v.astype(jnp.bfloat16).astype(F32)
        v2 = (v - v1).astype(jnp.bfloat16).astype(F32)
        parts = [
            (cell >> 16).astype(F32),
            ((cell >> 8) & 255).astype(F32),
            (cell & 255).astype(F32),
            v1,
            v2,
            v - v1 - v2,
            jnp.where(slot < count[0, t], 1.0, 0.0),
        ]
        left = jnp.concatenate(parts + [jnp.zeros((9, CAP), F32)], axis=0).astype(jnp.bfloat16)
        out = lax.dot_general(left, place, (((1,), (1,)), ((), ())), preferred_element_type=F32)
        cell = (out[0:1] * 65536.0 + out[1:2] * 256.0 + out[2:3]).astype(I32)
        row, level, where = (cell >> 10) & (ROWS - 1), cell >> 14, (cell >> 7) & (ROWS * CT - 1)
        alive = out[6:7] > 0.5
        own = (where + H * CT) * LV + level
        addr[t] = own
        spot[t] = where + H * CT
        sval[t] = out[3:4] + out[4:5] + out[5:6]
        lane[t] = jnp.where(alive, (cell & (LN - 1)).astype(F32), -1.0)
        live[t] = out[6:7]
        if t == NT - 1:
            second[0] = jnp.where(jnp.logical_or(row == 1, row == ROWS - 2), -3.0, 0.0)
        far = jnp.where(row < ROWS // 2, own + ROWS * COL, own - ROWS * COL)
        near = jnp.logical_or(row <= t, row >= ROWS - 1 - t)
        code = jnp.where(near, far * LN + (cell & (LN - 1)), 0).astype(F32)
        for q in range(CAP // LN):
            codes[pl.ds(4 * t + q, 1), :] = code[:, q * LN : (q + 1) * LN]
    codes[pl.ds(12, 1), :] = tally


def order(cells, count, value):
    ints, floats = jax.ShapeDtypeStruct((NT, 1, CAP), I32), jax.ShapeDtypeStruct((NT, 1, CAP), F32)
    return pl.pallas_call(
        order_kernel,
        out_shape=[ints, floats, floats, floats, ints, jax.ShapeDtypeStruct((1, 1, CAP), F32), jax.ShapeDtypeStruct((CODE, LN), F32)],
        in_specs=[VM, SM, VM],
        out_specs=[VM] * 7,
        compiler_params=params(6),
        cost_estimate=cost(2),
        name="order",
    )(cells, count, value)


def upright(line):
    return jnp.broadcast_to(line, (LN, LN)).T


def interior_kernel(staged, mask, lane, sval, spots, y0, y1, y2, y3, f1, f2, f3, twice, known, sea, at_ref, sem):
    fetch = Fetch(spots, at_ref, sem)
    fetch.start()
    for c in range(CT):
        flat = staged.at[c].reshape(LV * ROWS, LN)

        def turn(r, _):
            half = 2.5 * mask_row(mask, r + H, c)
            for k in range(LV // 8):
                v = flat[pl.ds(k * 8 * ROWS + r, 8, stride=ROWS), :]
                y0[pl.ds(pl.multiple_of((r + H) * COL + c * LV + k * 8, 8), 8), :] = half * v
            return 0

        lax.fori_loop(0, ROWS, turn, 0, unroll=2)

    zero = jnp.zeros((8, LN), F32)
    for at in (H - 2, ROWS + H + 1):
        for j in range(COL // 8):
            y2[pl.ds(at * COL + j * 8, 8), :] = zero

    def clear(at, _):
        for f in (f1, f2, f3):
            for j in range(COL // 8):
                f[pl.ds(pl.multiple_of(at * COL, 8) + j * 8, 8), :] = zero
        return 0

    lax.fori_loop(0, RX, clear, 0)
    loop(1, 14, lambda at: forward_row(y0, y1, mask, at))
    loop(2, 13, lambda at: forward_row(y1, y2, mask, at))
    loop(3, 12, lambda at: forward_row(y2, y3, mask, at))
    ids = lax.broadcasted_iota(I32, (LN, LN), 1).astype(F32)
    for t in range(NT):
        for q in range(CAP // LN):
            part = pl.ds(q * LN, LN)
            hit = upright(lane[t, :, part]) == ids
            rows = pl.ds(t * CAP + q * LN, LN)
            twice[rows, :] = jnp.where(hit, 2.0, 0.0)
            known[rows, :] = jnp.where(hit, upright(sval[t, :, part]), 0.0)
    fetch.wait()

    def group(i, _):
        for u in range(8):
            s = i * 8 + u
            sea[pl.ds(s, 1), :] = mask[pl.ds(at_ref[2 * CAP + s], 1), :]
        return 0

    lax.fori_loop(0, CAP // 8, group, 0)


def interior(staged, mask, lane, sval, spots):
    rows = jax.ShapeDtypeStruct((NT * CAP, LN), F32)
    return pl.pallas_call(
        interior_kernel,
        out_shape=[FIELD] * 7 + [rows, rows, jax.ShapeDtypeStruct((CAP, LN), F32)],
        in_specs=[VM] * 4 + [ANY],
        out_specs=[VM] * 10,
        scratch_shapes=[pltpu.SMEM((NT * CAP,), I32), pltpu.SemaphoreType.DMA((NT,))],
        compiler_params=params(6),
        cost_estimate=cost(9),
        name="interior",
    )(staged, mask, lane, sval, spots)


def bands_kernel(y0i, y1i, y2i, y3, maski, twice, known, sea, second, codes, addrs, above, below,
                 y0, y1, y2, mask, total, pay, terms, g1, g2, g3, g4, at_ref, sem):
    fetch = Fetch(addrs, at_ref, sem)
    fetch.start()
    for halo, first in ((above, 0), (below, ROWS + H)):
        for j in range(H):
            base = (first + j) * COL
            for q in range(COL // 8):
                y0[pl.ds(base + q * 8, 8), :] = halo[pl.ds(j * COL + q * 8, 8), :]
            mask[pl.ds((first + j) * CT, CT), :] = halo[pl.ds(H * COL + j * CT, CT), :]
    for src, dst, reach in ((y0, y1, 2), (y1, y2, 1), (y2, y3, 0)):
        loop(-reach, 2 - reach, lambda at: forward_row(src, dst, mask, at))
        loop(ROWS - 3 + reach, ROWS - 1 + reach, lambda at: forward_row(src, dst, mask, at))
    fetch.wait()
    many = 8

    def group(i, _):
        for u in range(many):
            s = i * many + u
            third = at_ref[2 * CAP + s]
            g1[pl.ds(s, 1), :] = y1[pl.ds(at_ref[s], 1), :]
            g2[pl.ds(s, 1), :] = y2[pl.ds(at_ref[CAP + s], 1), :]
            g3[pl.ds(s, 1), :] = y3[pl.ds(third, 1), :]
            g4[pl.ds(s, 1), :] = y2[pl.ds(third, 1), :]
        return 0

    lax.fori_loop(0, CAP // many, group, 0)
    acc = jnp.zeros((8, LN), F32)
    for t, g in enumerate((g1, g2, g3)):
        for q in range(CAP // LN):
            part, rows = pl.ds(q * LN, LN), pl.ds(t * CAP + q * LN, LN)
            d = g[part, :] * twice[rows, :] - known[rows, :]
            acc = acc + jnp.sum((d * d).reshape(LN // 8, 8, LN), axis=0)
            if t == NT - 1:
                d = d * (5.0 * sea[part, :])
                z = g4[part, :]
                e = jnp.sum(((z * z) * d).T, axis=0, keepdims=True)
                pay[pl.ds(12 + q, 1), :] = e * second[0, :, part]
            else:
                d = 5.0 * d
            terms[rows, :] = d
            pay[pl.ds(4 * t + q, 1), :] = jnp.sum(d.T, axis=0, keepdims=True)
    pay[pl.ds(CODE, CODE), :] = codes[...]
    total[...] = acc


def bands(y0, y1, y2, y3, mask, twice, known, sea, second, codes, addrs, above, below):
    rows = pltpu.VMEM((CAP, LN), F32)
    return pl.pallas_call(
        bands_kernel,
        out_shape=[FIELD] * 3
        + [
            MASK,
            jax.ShapeDtypeStruct((8, LN), F32),
            jax.ShapeDtypeStruct((PAY, LN), F32),
            jax.ShapeDtypeStruct((NT * CAP, LN), F32),
        ],
        in_specs=[VM] * 10 + [ANY] + [VM] * 2,
        out_specs=[VM] * 7,
        input_output_aliases={0: 0, 1: 1, 2: 2, 4: 3},
        scratch_shapes=[rows, rows, rows, rows, pltpu.SMEM((NT * CAP,), I32), pltpu.SemaphoreType.DMA((NT,))],
        compiler_params=params(4),
        cost_estimate=cost(5),
        name="bands",
    )(y0, y1, y2, y3, mask, twice, known, sea, second, codes, addrs, above, below)


def scatter_kernel(f1i, f2i, f3i, terms, addrs, f1, f2, f3, at_ref, sem):
    fetch = Fetch(addrs, at_ref, sem)
    fetch.start()
    fetch.wait()

    def group(i, _):
        for u in range(8):
            s = i * 8 + u
            for t, f in enumerate((f1, f2, f3)):
                spot = pl.ds(at_ref[t * CAP + s], 1)
                f[spot, :] = f[spot, :] + terms[pl.ds(t * CAP + s, 1), :]
        return 0

    lax.fori_loop(0, CAP // 8, group, 0)


def scatter(f1, f2, f3, terms, addrs):
    return pl.pallas_call(
        scatter_kernel,
        out_shape=[FIELD] * 3,
        in_specs=[VM] * 4 + [ANY],
        out_specs=[VM] * 3,
        input_output_aliases={0: 0, 1: 1, 2: 2},
        scratch_shapes=[pltpu.SMEM((NT * CAP,), I32), pltpu.SemaphoreType.DMA((NT,))],
        compiler_params=params(2),
        cost_estimate=cost(3),
        name="scatter",
    )(f1, f2, f3, terms, addrs)


def adjoint_kernel(first, last, src, state, forcing, mask, out):
    loop(first, last, lambda at: adjoint_row(src, state, out, mask, at))


def adjoint(first, last, src, state, forcing, mask):
    return pl.pallas_call(
        functools.partial(adjoint_kernel, first, last),
        out_shape=FIELD,
        in_specs=[VM] * 4,
        out_specs=VM,
        input_output_aliases={2: 0},
        compiler_params=params(2),
        cost_estimate=cost(2),
        name="adjoint",
    )(src, state, forcing, mask)


def middle_kernel(f1, y0, grad):
    loop(3, 12, lambda at: gradient_row(f1, y0, grad, at))


def middle(f1, y0):
    return pl.pallas_call(
        middle_kernel,
        out_shape=jax.ShapeDtypeStruct((ROWS * COL, LN), F32),
        in_specs=[VM] * 2,
        out_specs=VM,
        compiler_params=params(2),
        cost_estimate=cost(2),
        name="middle",
    )(f1, y0)


def finish_kernel(y0, y1, y2, f1i, f2i, f3i, mask, gradi, above, below, f1, f2, f3, grad, out, staged, a_ref, b_ref, sems):
    fetches = [pltpu.make_async_copy(src, dst, sems.at[CT + i]) for i, (src, dst) in enumerate(((above, a_ref), (below, b_ref)))]
    for f in fetches:
        f.start()
    for f in fetches:
        f.wait()
    counts = 2 * CODE * LN - (CODE - 12) * LN
    lane = lax.broadcasted_iota(I32, (1, LN), 1)
    na = [a_ref[counts + NT + t].astype(I32) for t in range(NT)]
    nb = [b_ref[counts + t].astype(I32) for t in range(NT)]
    most = na[0]
    for n in na[1:] + nb:
        most = jnp.maximum(most, n)

    def item(j, _):
        for t, f in ((2, f3), (1, f2), (0, f1)):
            for ref, n, slot in ((a_ref, na[t], CAP - 1 - j), (b_ref, nb[t], j)):
                code = ref[CODE * LN + t * CAP + slot].astype(I32)
                hit = lane == jnp.where(j < n, code & (LN - 1), -1)
                spot = pl.ds(code >> 7, 1)
                f[spot, :] = f[spot, :] + jnp.where(hit, ref[t * CAP + slot], 0.0)
                if t == NT - 1:
                    f2[spot, :] = f2[spot, :] + jnp.where(hit, ref[12 * LN + slot], 0.0)
        return 0

    lax.fori_loop(0, most, item, 0)
    for src, state, dst, reach in ((f3, y2, f2, 2), (f2, y1, f1, 1)):
        loop(-reach, 2 - reach, lambda at: adjoint_row(src, state, dst, mask, at))
        loop(ROWS - 3 + reach, ROWS - 1 + reach, lambda at: adjoint_row(src, state, dst, mask, at))
    loop(0, 2, lambda at: gradient_row(f1, y0, grad, at))
    loop(ROWS - 3, ROWS - 1, lambda at: gradient_row(f1, y0, grad, at))

    def copy(c):
        return pltpu.make_async_copy(staged.at[c], out.at[:, :, pl.ds(c * LN, LN)], sems.at[c])

    for c in range(CT):
        def turn(k, _):
            for half in range(2):
                v = grad[pl.ds(half * 8 * COL + c * LV + k, 8, stride=COL), :]
                staged[c, k, pl.ds(half * 8, 8), :] = v
            return 0

        lax.fori_loop(0, LV, turn, 0, unroll=8)
        copy(c).start()
    for c in range(CT):
        copy(c).wait()


def finish(y0, y1, y2, f1, f2, f3, mask, grad, above, below):
    return pl.pallas_call(
        finish_kernel,
        out_shape=[FIELD] * 3 + [jax.ShapeDtypeStruct((ROWS * COL, LN), F32), jax.ShapeDtypeStruct((LV, ROWS, CT * LN), F32)],
        in_specs=[VM] * 8 + [ANY] * 2,
        out_specs=[VM] * 4 + [ANY],
        input_output_aliases={3: 0, 4: 1, 5: 2, 7: 3},
        scratch_shapes=[
            pltpu.VMEM((CT, LV, ROWS, LN), F32),
            pltpu.SMEM((PAY * LN,), F32),
            pltpu.SMEM((PAY * LN,), F32),
            pltpu.SemaphoreType.DMA((CT + 2,)),
        ],
        compiler_params=params(6),
        cost_estimate=cost(6),
        name="finish",
    )(y0, y1, y2, f1, f2, f3, mask, grad, above, below)[4]


def add_kernel(a, b, out):
    out[...] = a[...] + b[...]


def reduce_kernel(scale, a, b, out):
    out[...] = jnp.sum(a[...] + b[...], keepdims=True) * scale


def small(kernel, shape, a, b, name):
    return pl.pallas_call(
        kernel,
        out_shape=jax.ShapeDtypeStruct(shape, F32),
        in_specs=[VM, VM],
        out_specs=VM,
        compiler_params=params(1),
        cost_estimate=cost(0.1),
        name=name,
    )(a, b)


def sum_along(x, stages, scale):
    size = lax.axis_size("along")
    steps = [1 << i for i in range(size.bit_length() - 1)]
    held = ()
    if size & (size - 1):
        x, steps = lax.psum(x, "along"), []
    other = jnp.zeros_like(x)
    for i in range(max(len(steps), len(stages))):
        if i < len(steps):
            if i > 0:
                x = small(add_kernel, x.shape, x, other, "add")
                x, held = lax.optimization_barrier((x, held))
            other = lax.ppermute(x, "along", [(p, p ^ steps[i]) for p in range(size)])
        if i < len(stages):
            held = stages[i](*held)
    return small(functools.partial(reduce_kernel, scale), (1, 1), x, other, "reduce").reshape(1), held


def local(basic_state, land_sea, obs_cells, obs_count, obs_value):
    size = lax.axis_size("along")
    later = [(i, i + 1) for i in range(size - 1)]
    earlier = [(i + 1, i) for i in range(size - 1)]
    cells = obs_cells.transpose(1, 0, 2)
    value = obs_value.transpose(1, 0, 2)
    staged, up, down, mask = edges(basic_state, land_sea)
    above = lax.ppermute(down, "along", later)
    below = lax.ppermute(up, "along", earlier)
    addrs, _, sval, lane, spots, second, codes = order(cells, obs_count, value)
    y0, y1, y2, y3, f1, f2, f3, twice, known, sea = interior(staged, mask, lane, sval, spots)
    y0, y1, y2, mask, total, pay, terms = bands(
        y0, y1, y2, y3, mask, twice, known, sea, second, codes, addrs, above, below
    )
    above = lax.ppermute(pay, "along", later).reshape(-1)
    below = lax.ppermute(pay, "along", earlier).reshape(-1)
    stages = (
        lambda: scatter(f1, f2, f3, terms, addrs),
        lambda a, b, c: (a, adjoint(1, 14, c, y2, b, mask), c),
        lambda a, b, c: (adjoint(2, 13, b, y1, a, mask), b, c),
        lambda a, b, c: (a, b, c, middle(a, y0)),
    )
    misfit, held = sum_along(total, stages, 1.0 / (2.0 * size * obs_cells.shape[1] * obs_cells.shape[2]))
    gradient = finish(y0, y1, y2, *held[:3], mask, held[3], above, below)
    return gradient, misfit


def solution(mesh):
    in_specs = (
        P(None, ("ens", "along"), None),
        P(("ens", "along"), None),
        P(("ens", "along"), None, None),
        P(("ens", "along"), None),
        P(("ens", "along"), None, None),
    )
    out_specs = (P(None, ("ens", "along"), None), P("ens"))
    return jax.shard_map(local, mesh=mesh, in_specs=in_specs, out_specs=out_specs, check_vma=False)
```

```python
import functools

import jax
import jax.numpy as jnp
from jax import lax
from jax.experimental import pallas as pl
from jax.experimental.pallas import tpu as pltpu
from jax.sharding import PartitionSpec as P

F32 = jnp.float32
I32 = jnp.int32
ROWS, CT, LV, LN = 16, 8, 40, 128
H = 3
RX = ROWS + 2 * H
COL = CT * LV
EDGE = H * COL + H * CT
CAP = 512
NT = 3
PAY = 40
CODE = 16

VM = pl.BlockSpec(memory_space=pltpu.VMEM)
SM = pl.BlockSpec(memory_space=pltpu.SMEM)
HBM = pl.BlockSpec(memory_space=pltpu.MemorySpace.HBM)
ANY = pl.BlockSpec(memory_space=pl.ANY)
FIELD = jax.ShapeDtypeStruct((RX * COL, LN), F32)
MASK = jax.ShapeDtypeStruct((RX * CT, LN), F32)


def params(mib):
    return pltpu.CompilerParams(vmem_limit_bytes=mib << 20)


def cost(us):
    return pl.CostEstimate(flops=0, bytes_accessed=int(us * 3.0e6), transcendentals=0)


def lanes():
    return lax.broadcasted_iota(I32, (8, LN), 1)


def sublanes():
    return lax.broadcasted_iota(I32, (8, LN), 0)


def stencil_row(src, at, emit):
    lane, sub = lanes(), sublanes()
    first, last = lane == 0, lane == LN - 1
    low, high = sub == 0, sub == 7
    base = pl.multiple_of(at * COL, COL)
    for k in range(LV // 8):
        offs = [base + c * LV + k * 8 for c in range(CT)]
        mids = [src[pl.ds(pl.multiple_of(o, 8), 8), :] for o in offs]
        fwd = [pltpu.roll(v, 1, 1) for v in mids]
        bwd = [pltpu.roll(v, LN - 1, 1) for v in mids]
        for c in range(CT):
            v, o = mids[c], offs[c]
            west = jnp.where(first, fwd[c - 1] if c > 0 else 0.0, fwd[c])
            east = jnp.where(last, bwd[c + 1] if c < CT - 1 else 0.0, bwd[c])
            north = src[pl.ds(pl.multiple_of(o - COL, 8), 8), :]
            south = src[pl.ds(pl.multiple_of(o + COL, 8), 8), :]
            if k > 0:
                down = src[pl.ds(o - 1, 8), :]
            else:
                down = jnp.where(low, v, pltpu.roll(v, 1, 0))
            if k < LV // 8 - 1:
                up = src[pl.ds(o + 1, 8), :]
            else:
                up = jnp.where(high, v, pltpu.roll(v, 7, 0))
            s = ((north + south) + (west + east)) + 0.2 * (down + up)
            emit(c, k, v, s, o)


class Fetch:
    def __init__(self, src, dst, sems):
        self.parts = [pltpu.make_async_copy(src.at[t, 0], dst.at[pl.ds(t * CAP, CAP)], sems.at[t]) for t in range(NT)]

    def start(self):
        for part in self.parts:
            part.start()

    def wait(self):
        for part in self.parts:
            part.wait()


def mask_row(mask, at, c):
    return mask[pl.ds(at * CT + c, 8, stride=0), :]


def forward_row(src, dst, mask, at, blank=None):
    ms = [mask_row(mask, at, c) for c in range(CT)]

    def emit(c, k, v, s, o):
        dst[pl.ds(pl.multiple_of(o, 8), 8), :] = ms[c] * (s + v * (0.6 - v * v))
        if blank is not None:
            blank[pl.ds(pl.multiple_of(o, 8), 8), :] = jnp.zeros((8, LN), F32)

    stencil_row(src, at, emit)


def adjoint_row(src, state, forcing, mask, at):
    ms = [mask_row(mask, at, c) for c in range(CT)]

    def emit(c, k, g, s, o):
        spot = pl.ds(pl.multiple_of(o, 8), 8)
        y = state[spot, :]
        forcing[spot, :] = ms[c] * ((s + g * (0.6 - 3.0 * (y * y))) + forcing[spot, :])

    stencil_row(src, at, emit)


def gradient_row(src, state, out, at):
    def emit(c, k, g, s, o):
        y = state[pl.ds(pl.multiple_of(o, 8), 8), :]
        out[pl.ds(pl.multiple_of(o - H * COL, 8), 8), :] = 0.2 * (s + g * (0.6 - 3.0 * (y * y)))

    stencil_row(src, at, emit)


def loop(first, last, body):
    lax.fori_loop(first + H, last + H + 1, lambda at, _: (body(at), 0)[1], 0)


def even():
    return lax.rem(lax.axis_index("along"), 2) == 0


def edges_kernel(basic, land_at, staged, twin, other, mask, land, sems):
    def copy(c):
        return pltpu.make_async_copy(basic.at[:, :, pl.ds(c * LN, LN)], staged.at[c], sems.at[c])

    sea = pltpu.make_async_copy(land_at, land, sems.at[CT])
    sea.start()
    for c in range(CT):
        copy(c).start()
    sea.wait()
    for c in range(CT):
        mask[pl.ds(H * CT + c, ROWS, stride=CT), :] = 0.2 * land[:, pl.ds(c * LN, LN)].astype(F32)
    lower = jnp.where(even(), ROWS - H, 0)
    for c in range(CT):
        copy(c).wait()
        flat = staged.at[c].reshape(LV * ROWS, LN)
        for out, first in ((twin, lower), (other, ROWS - H - lower)):
            for j in range(H):
                r = first + j
                half = 2.5 * mask_row(mask, r + H, c)
                for k in range(LV // 8):
                    v = flat[pl.ds(k * 8 * ROWS + r, 8, stride=ROWS), :]
                    out[pl.ds((j * CT + c) * LV + k * 8, 8), :] = half * v
                out[pl.ds(H * COL + j * CT + c, 1), :] = mask[pl.ds((r + H) * CT + c, 1), :]


def edges(basic, land):
    return pl.pallas_call(
        edges_kernel,
        out_shape=[
            jax.ShapeDtypeStruct((CT, LV, ROWS, LN), F32),
            jax.ShapeDtypeStruct((EDGE, LN), F32),
            jax.ShapeDtypeStruct((EDGE, LN), F32),
            MASK,
        ],
        in_specs=[HBM, HBM],
        out_specs=[VM] * 4,
        scratch_shapes=[pltpu.VMEM((ROWS, CT * LN), I32), pltpu.SemaphoreType.DMA((CT + 1,))],
        compiler_params=params(4),
        cost_estimate=cost(2),
        name="edges",
    )(pltpu.with_memory_space_constraint(basic, pltpu.HBM), pltpu.with_memory_space_constraint(land, pltpu.HBM))


def order_kernel(cells_at, count_at, value_at, addr, sval, lane, spot, second, codes, cells, count, value, sems):
    fetches = [
        pltpu.make_async_copy(src, dst, sems.at[i])
        for i, (src, dst) in enumerate(((cells_at, cells), (count_at, count), (value_at, value)))
    ]
    for f in fetches:
        f.start()
    for f in fetches:
        f.wait()
    slot = lax.broadcasted_iota(I32, (1, CAP), 1)
    ups, downs = [], []
    for t in range(NT):
        row = (cells[t] >> 10) & (ROWS - 1)
        alive = slot < count[0, t]
        ups.append(jnp.logical_and(alive, row <= t))
        downs.append(jnp.logical_and(alive, row >= ROWS - 1 - t))
    one = [jnp.where(f, 1.0, 0.0) for f in ups + downs]
    flags = jnp.concatenate(one + [jnp.zeros((10, CAP), F32)], axis=0).astype(jnp.bfloat16)
    tri = jnp.where(
        lax.broadcasted_iota(I32, (CAP, CAP), 0) < lax.broadcasted_iota(I32, (CAP, CAP), 1), 1.0, 0.0
    ).astype(jnp.bfloat16)
    before = jnp.dot(flags, tri, preferred_element_type=F32)
    codes[...] = jnp.zeros((CODE, LN), F32)
    sub = lax.broadcasted_iota(I32, (CAP, CAP), 0)
    first = lax.broadcasted_iota(I32, (1, LN), 1)
    tally = jnp.zeros((1, LN), F32)
    for t in range(NT):
        up, down = ups[t], downs[t]
        pu, pd = before[t : t + 1], before[NT + t : NT + t + 1]
        nu = jnp.sum(one[t], axis=1, keepdims=True)
        nd = jnp.sum(one[NT + t], axis=1, keepdims=True)
        tally = tally + jnp.where(first == t, nu, 0.0) + jnp.where(first == NT + t, nd, 0.0)
        rank = jnp.where(up, pu, jnp.where(down, CAP - nd + pd, nu + slot.astype(F32) - pu - pd)).astype(I32)
        place = jnp.where(sub == rank, 1.0, 0.0).astype(jnp.bfloat16)
        cell, v = cells[t], value[t]
        v1 = v.astype(jnp.bfloat16).astype(F32)
        v2 = (v - v1).astype(jnp.bfloat16).astype(F32)
        parts = [
            (cell >> 16).astype(F32),
            ((cell >> 8) & 255).astype(F32),
            (cell & 255).astype(F32),
            v1,
            v2,
            v - v1 - v2,
            jnp.where(slot < count[0, t], 1.0, 0.0),
        ]
        left = jnp.concatenate(parts + [jnp.zeros((9, CAP), F32)], axis=0).astype(jnp.bfloat16)
        out = lax.dot_general(left, place, (((1,), (1,)), ((), ())), preferred_element_type=F32)
        cell = (out[0:1] * 65536.0 + out[1:2] * 256.0 + out[2:3]).astype(I32)
        row, level, where = (cell >> 10) & (ROWS - 1), cell >> 14, (cell >> 7) & (ROWS * CT - 1)
        alive = out[6:7] > 0.5
        own = (where + H * CT) * LV + level
        addr[t] = own
        spot[t] = where + H * CT
        sval[t] = out[3:4] + out[4:5] + out[5:6]
        lane[t] = jnp.where(alive, (cell & (LN - 1)).astype(F32), -1.0)
        if t == NT - 1:
            second[0] = jnp.where(jnp.logical_or(row == 1, row == ROWS - 2), -3.0, 0.0)
        far = jnp.where(row < ROWS // 2, own + ROWS * COL, own - ROWS * COL)
        near = jnp.logical_or(row <= t, row >= ROWS - 1 - t)
        code = jnp.where(near, far * LN + (cell & (LN - 1)), 0).astype(F32)
        for q in range(CAP // LN):
            codes[pl.ds(4 * t + q, 1), :] = code[:, q * LN : (q + 1) * LN]
    codes[pl.ds(12, 1), :] = tally


def order(cells, count, value):
    ints, floats = jax.ShapeDtypeStruct((NT, 1, CAP), I32), jax.ShapeDtypeStruct((NT, 1, CAP), F32)
    return pl.pallas_call(
        order_kernel,
        out_shape=[ints, floats, floats, ints, jax.ShapeDtypeStruct((1, 1, CAP), F32), jax.ShapeDtypeStruct((CODE, LN), F32)],
        in_specs=[HBM] * 3,
        out_specs=[VM] * 6,
        scratch_shapes=[
            pltpu.VMEM((NT, 1, CAP), I32),
            pltpu.SMEM((1, NT), I32),
            pltpu.VMEM((NT, 1, CAP), F32),
            pltpu.SemaphoreType.DMA((3,)),
        ],
        compiler_params=params(6),
        cost_estimate=cost(2),
        name="order",
    )(*(pltpu.with_memory_space_constraint(x, pltpu.HBM) for x in (cells, count, value)))


def upright(line):
    return jnp.broadcast_to(line, (LN, LN)).T


def interior_kernel(staged, mask, lane, sval, spots, y0, y1, y2, y3, f1, f2, f3, twice, known, sea, at_ref, sem):
    fetch = Fetch(spots, at_ref, sem)
    fetch.start()
    for c in range(CT):
        flat = staged.at[c].reshape(LV * ROWS, LN)

        def turn(r, _):
            half = 2.5 * mask_row(mask, r + H, c)
            for k in range(LV // 8):
                v = flat[pl.ds(k * 8 * ROWS + r, 8, stride=ROWS), :]
                y0[pl.ds(pl.multiple_of((r + H) * COL + c * LV + k * 8, 8), 8), :] = half * v
            return 0

        lax.fori_loop(0, ROWS, turn, 0, unroll=2)

    zero = jnp.zeros((8, LN), F32)
    for at in (H - 2, ROWS + H + 1):
        for j in range(COL // 8):
            y2[pl.ds(at * COL + j * 8, 8), :] = zero

    for t, f in enumerate((f1, f2, f3)):
        for at in [*range(H + t + 1), *range(ROWS + H - t - 1, RX)]:
            for j in range(COL // 8):
                f[pl.ds(at * COL + j * 8, 8), :] = zero
    loop(1, 14, lambda at: forward_row(y0, y1, mask, at, f1))
    loop(2, 13, lambda at: forward_row(y1, y2, mask, at, f2))
    loop(3, 12, lambda at: forward_row(y2, y3, mask, at, f3))
    ids = lax.broadcasted_iota(I32, (LN, LN), 1).astype(F32)
    for t in range(NT):
        for q in range(CAP // LN):
            part = pl.ds(q * LN, LN)
            hit = upright(lane[t, :, part]) == ids
            rows = pl.ds(t * CAP + q * LN, LN)
            twice[rows, :] = jnp.where(hit, 2.0, 0.0)
            known[rows, :] = jnp.where(hit, upright(sval[t, :, part]), 0.0)
    fetch.wait()

    def group(i, _):
        for u in range(8):
            s = i * 8 + u
            sea[pl.ds(s, 1), :] = mask[pl.ds(at_ref[2 * CAP + s], 1), :]
        return 0

    lax.fori_loop(0, CAP // 8, group, 0)


def interior(staged, mask, lane, sval, spots):
    rows = jax.ShapeDtypeStruct((NT * CAP, LN), F32)
    return pl.pallas_call(
        interior_kernel,
        out_shape=[FIELD] * 7 + [rows, rows, jax.ShapeDtypeStruct((CAP, LN), F32)],
        in_specs=[VM] * 4 + [ANY],
        out_specs=[VM] * 10,
        scratch_shapes=[pltpu.SMEM((NT * CAP,), I32), pltpu.SemaphoreType.DMA((NT,))],
        compiler_params=params(6),
        cost_estimate=cost(9),
        name="interior",
    )(staged, mask, lane, sval, spots)


def bands_kernel(y0i, y1i, y2i, y3, maski, twice, known, sea, second, codes, addrs, twin, other,
                 y0, y1, y2, mask, pay, terms, g1, g2, g3, g4, at_ref, sem):
    fetch = Fetch(addrs, at_ref, sem)
    fetch.start()
    lower = jnp.where(even(), ROWS + H, 0)
    for halo, first in ((twin, lower), (other, ROWS + H - lower)):
        base = pl.multiple_of(first * COL, 8)
        for q in range(H * COL // 8):
            y0[pl.ds(base + q * 8, 8), :] = halo[pl.ds(q * 8, 8), :]
        base = pl.multiple_of(first * CT, 8)
        for j in range(H):
            mask[pl.ds(base + j * CT, CT), :] = halo[pl.ds(H * COL + j * CT, CT), :]
    for src, dst, reach in ((y0, y1, 2), (y1, y2, 1), (y2, y3, 0)):
        loop(-reach, 2 - reach, lambda at: forward_row(src, dst, mask, at))
        loop(ROWS - 3 + reach, ROWS - 1 + reach, lambda at: forward_row(src, dst, mask, at))
    fetch.wait()
    many = 8

    def group(i, _):
        for u in range(many):
            s = i * many + u
            third = at_ref[2 * CAP + s]
            g1[pl.ds(s, 1), :] = y1[pl.ds(at_ref[s], 1), :]
            g2[pl.ds(s, 1), :] = y2[pl.ds(at_ref[CAP + s], 1), :]
            g3[pl.ds(s, 1), :] = y3[pl.ds(third, 1), :]
            g4[pl.ds(s, 1), :] = y2[pl.ds(third, 1), :]
        return 0

    lax.fori_loop(0, CAP // many, group, 0)
    acc = jnp.zeros((8, LN), F32)
    for t, g in enumerate((g1, g2, g3)):
        for q in range(CAP // LN):
            part, rows = pl.ds(q * LN, LN), pl.ds(t * CAP + q * LN, LN)
            d = g[part, :] * twice[rows, :] - known[rows, :]
            acc = acc + jnp.sum((d * d).reshape(LN // 8, 8, LN), axis=0)
            if t == NT - 1:
                d = d * (5.0 * sea[part, :])
                z = g4[part, :]
                e = jnp.sum(((z * z) * d).T, axis=0, keepdims=True)
                pay[pl.ds(12 + q, 1), :] = e * second[0, :, part]
            else:
                d = 5.0 * d
            terms[rows, :] = d
            pay[pl.ds(4 * t + q, 1), :] = jnp.sum(d.T, axis=0, keepdims=True)
    pay[pl.ds(CODE, CODE), :] = codes[...]
    pay[pl.ds(2 * CODE, 8), :] = acc


def bands(y0, y1, y2, y3, mask, twice, known, sea, second, codes, addrs, above, below):
    rows = pltpu.VMEM((CAP, LN), F32)
    return pl.pallas_call(
        bands_kernel,
        out_shape=[FIELD] * 3
        + [
            MASK,
            jax.ShapeDtypeStruct((PAY, LN), F32),
            jax.ShapeDtypeStruct((NT * CAP, LN), F32),
        ],
        in_specs=[VM] * 10 + [ANY] + [VM] * 2,
        out_specs=[VM] * 6,
        input_output_aliases={0: 0, 1: 1, 2: 2, 4: 3},
        scratch_shapes=[rows, rows, rows, rows, pltpu.SMEM((NT * CAP,), I32), pltpu.SemaphoreType.DMA((NT,))],
        compiler_params=params(4),
        cost_estimate=cost(5),
        name="bands",
    )(y0, y1, y2, y3, mask, twice, known, sea, second, codes, addrs, above, below)


def scatter_kernel(f1i, f2i, f3i, terms, addrs, f1, f2, f3, at_ref, sem):
    fetch = Fetch(addrs, at_ref, sem)
    fetch.start()
    fetch.wait()

    def group(i, _):
        for u in range(8):
            s = i * 8 + u
            for t, f in enumerate((f1, f2, f3)):
                spot = pl.ds(at_ref[t * CAP + s], 1)
                f[spot, :] = f[spot, :] + terms[pl.ds(t * CAP + s, 1), :]
        return 0

    lax.fori_loop(0, CAP // 8, group, 0)


def scatter(f1, f2, f3, terms, addrs):
    return pl.pallas_call(
        scatter_kernel,
        out_shape=[FIELD] * 3,
        in_specs=[VM] * 4 + [ANY],
        out_specs=[VM] * 3,
        input_output_aliases={0: 0, 1: 1, 2: 2},
        scratch_shapes=[pltpu.SMEM((NT * CAP,), I32), pltpu.SemaphoreType.DMA((NT,))],
        compiler_params=params(2),
        cost_estimate=cost(3),
        name="scatter",
    )(f1, f2, f3, terms, addrs)


def adjoint_kernel(first, last, src, state, forcing, mask, out):
    loop(first, last, lambda at: adjoint_row(src, state, out, mask, at))


def adjoint(first, last, src, state, forcing, mask):
    return pl.pallas_call(
        functools.partial(adjoint_kernel, first, last),
        out_shape=FIELD,
        in_specs=[VM] * 4,
        out_specs=VM,
        input_output_aliases={2: 0},
        compiler_params=params(2),
        cost_estimate=cost(2),
        name="adjoint",
    )(src, state, forcing, mask)


def middle_kernel(f1, y0, grad):
    loop(3, 12, lambda at: gradient_row(f1, y0, grad, at))


def middle(f1, y0):
    return pl.pallas_call(
        middle_kernel,
        out_shape=jax.ShapeDtypeStruct((ROWS * COL, LN), F32),
        in_specs=[VM] * 2,
        out_specs=VM,
        compiler_params=params(2),
        cost_estimate=cost(2),
        name="middle",
    )(f1, y0)


def finish_kernel(scale, y0, y1, y2, f1i, f2i, f3i, mask, gradi, twin, other, x, y, f1, f2, f3, grad, out, misfit,
                  staged, a_ref, b_ref, ca, cb, sems):
    misfit[...] = jnp.sum(x[...] + y[...], keepdims=True) * scale

    def fetches(above, below):
        return [pltpu.make_async_copy(src, dst, sems.at[CT + i]) for i, (src, dst) in enumerate(((above, a_ref), (below, b_ref)))]

    @pl.when(even())
    def _():
        for f in fetches(other, twin):
            f.start()

    @pl.when(jnp.logical_not(even()))
    def _():
        for f in fetches(twin, other):
            f.start()

    for q in range(COL // 8):
        for buf in (ca, cb):
            buf[pl.ds(q * 8, 8), :] = jnp.zeros((8, LN), F32)
    for f in fetches(twin, other):
        f.wait()
    counts = CODE * LN + 12 * LN
    lane = lax.broadcasted_iota(I32, (1, LN), 1)
    na = [a_ref[counts + NT + t].astype(I32) for t in range(NT)]
    nb = [b_ref[counts + t].astype(I32) for t in range(NT)]
    most = 0
    for t in range(NT):
        most = jnp.maximum(most, (jnp.maximum(na[t], nb[t]) + t) // (t + 1))

    def item(i, _):
        for t, f in ((2, f3), (1, f2), (0, f1)):
            for u in range(t + 1):
                j = i * (t + 1) + u
                slot_of = jnp.minimum(j, CAP - 1)
                for ref, n, slot, side in ((a_ref, na[t], CAP - 1 - slot_of, ca), (b_ref, nb[t], slot_of, cb)):
                    code = ref[CODE * LN + t * CAP + slot].astype(I32)
                    hit = lane == jnp.where(j < n, code & (LN - 1), -1)
                    addr = code >> 7
                    spot = pl.ds(addr, 1)
                    f[spot, :] = f[spot, :] + jnp.where(hit, ref[t * CAP + slot], 0.0)
                    if t == NT - 1:
                        start = (1 if side is ca else ROWS + H + 1) * COL
                        far = addr - start
                        inside = jnp.logical_and(far >= 0, far < COL)
                        spot = pl.ds(jnp.where(inside, far, 0), 1)
                        side[spot, :] = side[spot, :] + jnp.where(hit, ref[12 * LN + slot], 0.0)
        return 0

    lax.fori_loop(0, most, item, 0)
    for side, at in ((ca, 1), (cb, ROWS + H + 1)):
        for q in range(COL // 8):
            spot = pl.ds(at * COL + q * 8, 8)
            f2[spot, :] = f2[spot, :] + side[pl.ds(q * 8, 8), :]
    for src, state, dst, reach in ((f3, y2, f2, 2), (f2, y1, f1, 1)):
        loop(-reach, 2 - reach, lambda at: adjoint_row(src, state, dst, mask, at))
        loop(ROWS - 3 + reach, ROWS - 1 + reach, lambda at: adjoint_row(src, state, dst, mask, at))
    loop(0, 2, lambda at: gradient_row(f1, y0, grad, at))
    loop(ROWS - 3, ROWS - 1, lambda at: gradient_row(f1, y0, grad, at))

    def copy(c):
        return pltpu.make_async_copy(staged.at[c], out.at[:, :, pl.ds(c * LN, LN)], sems.at[c])

    for c in range(CT):
        def turn(k, _):
            for half in range(2):
                v = grad[pl.ds(half * 8 * COL + c * LV + k, 8, stride=COL), :]
                staged[c, k, pl.ds(half * 8, 8), :] = v
            return 0

        lax.fori_loop(0, LV, turn, 0, unroll=8)
        copy(c).start()
    for c in range(CT):
        copy(c).wait()


def finish(y0, y1, y2, f1, f2, f3, mask, grad, twin, other, x, y, scale):
    return pl.pallas_call(
        functools.partial(finish_kernel, scale),
        out_shape=[FIELD] * 3
        + [
            jax.ShapeDtypeStruct((ROWS * COL, LN), F32),
            jax.ShapeDtypeStruct((LV, ROWS, CT * LN), F32),
            jax.ShapeDtypeStruct((1, 1), F32),
        ],
        in_specs=[VM] * 8 + [ANY] * 2 + [VM] * 2,
        out_specs=[VM] * 4 + [ANY, VM],
        input_output_aliases={3: 0, 4: 1, 5: 2, 7: 3},
        scratch_shapes=[
            pltpu.VMEM((CT, LV, ROWS, LN), F32),
            pltpu.SMEM((PAY * LN,), F32),
            pltpu.SMEM((PAY * LN,), F32),
            pltpu.VMEM((COL, LN), F32),
            pltpu.VMEM((COL, LN), F32),
            pltpu.SemaphoreType.DMA((CT + 2,)),
        ],
        compiler_params=params(6),
        cost_estimate=cost(6),
        name="finish",
    )(y0, y1, y2, f1, f2, f3, mask, grad, twin, other, x, y)[4:]


def add_kernel(first, pay, twin, out):
    out[...] = pay[pl.ds(first, 8), :] + twin[pl.ds(first, 8), :]


def add(first, a, b):
    return pl.pallas_call(
        functools.partial(add_kernel, first),
        out_shape=jax.ShapeDtypeStruct((8, LN), F32),
        in_specs=[VM, VM],
        out_specs=VM,
        compiler_params=params(1),
        cost_estimate=cost(0.1),
        name="add",
    )(a, b)


def sum_along(pay, twin, stages):
    size = lax.axis_size("along")
    steps = [1 << i for i in range(1, size.bit_length() - 1)]
    held = stages[0]()
    x = add(2 * CODE, pay, twin)
    other = jnp.zeros_like(x)
    if size & (size - 1):
        x, steps = lax.psum(0.5 * x, "along"), []
    for i in range(max(len(steps), len(stages) - 1)):
        if i < len(steps):
            if i > 0:
                x = add(0, x, other)
            x, held = lax.optimization_barrier((x, held))
            other = lax.ppermute(x, "along", [(p, p ^ steps[i]) for p in range(size)])
        if i + 1 < len(stages):
            held = stages[i + 1](*held)
    return x, other, held


def local(basic_state, land_sea, obs_cells, obs_count, obs_value):
    size = lax.axis_size("along")
    twins = [(i, i ^ 1) for i in range(size)]
    others = [(i, i - 1 if i % 2 == 0 else i + 1) for i in range(1, size - 1)]
    cells = obs_cells.transpose(1, 0, 2)
    value = obs_value.transpose(1, 0, 2)
    staged, twin, other, mask = edges(basic_state, land_sea)
    other = lax.ppermute(other, "along", others)
    twin = lax.ppermute(twin, "along", twins)
    addrs, sval, lane, spots, second, codes = order(cells, obs_count, value)
    y0, y1, y2, y3, f1, f2, f3, twice, known, sea = interior(staged, mask, lane, sval, spots)
    y0, y1, y2, mask, pay, terms = bands(y0, y1, y2, y3, mask, twice, known, sea, second, codes, addrs, twin, other)
    other = lax.ppermute(pay, "along", others)
    twin = lax.ppermute(pay, "along", twins)
    stages = (
        lambda: scatter(f1, f2, f3, terms, addrs),
        lambda a, b, c: (a, adjoint(1, 14, c, y2, b, mask), c),
        lambda a, b, c: (adjoint(2, 13, b, y1, a, mask), b, c),
        lambda a, b, c: (a, b, c, middle(a, y0)),
    )
    x, y, held = sum_along(pay, twin, stages)
    scale = 1.0 / (2.0 * size * obs_cells.shape[1] * obs_cells.shape[2])
    gradient, misfit = finish(y0, y1, y2, *held[:3], mask, held[3], twin.reshape(-1), other.reshape(-1), x, y, scale)
    misfit = misfit.reshape(1)
    return gradient, misfit


def solution(mesh):
    in_specs = (
        P(None, ("ens", "along"), None),
        P(("ens", "along"), None),
        P(("ens", "along"), None, None),
        P(("ens", "along"), None),
        P(("ens", "along"), None, None),
    )
    out_specs = (P(None, ("ens", "along"), None), P("ens"))
    return jax.shard_map(local, mesh=mesh, in_specs=in_specs, out_specs=out_specs, check_vma=False)
```

```python
import functools

import jax
import jax.numpy as jnp
from jax import lax
from jax.experimental import pallas as pl
from jax.experimental.pallas import tpu as pltpu
from jax.sharding import PartitionSpec as P

F32 = jnp.float32
I32 = jnp.int32
ROWS, CT, LV, LN = 16, 8, 40, 128
H = 3
RX = ROWS + 2 * H
COL = CT * LV
EDGE = H * COL + H * CT
CAP = 512
NT = 3
PAY = 40
CODE = 16

VM = pl.BlockSpec(memory_space=pltpu.VMEM)
SM = pl.BlockSpec(memory_space=pltpu.SMEM)
HBM = pl.BlockSpec(memory_space=pltpu.MemorySpace.HBM)
ANY = pl.BlockSpec(memory_space=pl.ANY)
FIELD = jax.ShapeDtypeStruct((RX * COL, LN), F32)
MASK = jax.ShapeDtypeStruct((RX * CT, LN), F32)


def params(mib):
    return pltpu.CompilerParams(vmem_limit_bytes=mib << 20)


def cost(us):
    return pl.CostEstimate(flops=0, bytes_accessed=int(us * 3.0e6), transcendentals=0)


def lanes():
    return lax.broadcasted_iota(I32, (8, LN), 1)


def sublanes():
    return lax.broadcasted_iota(I32, (8, LN), 0)


def stencil_row(src, at, emit):
    lane, sub = lanes(), sublanes()
    first, last = lane == 0, lane == LN - 1
    low, high = sub == 0, sub == 7
    base = pl.multiple_of(at * COL, COL)
    for k in range(LV // 8):
        offs = [base + c * LV + k * 8 for c in range(CT)]
        mids = [src[pl.ds(pl.multiple_of(o, 8), 8), :] for o in offs]
        fwd = [pltpu.roll(v, 1, 1) for v in mids]
        bwd = [pltpu.roll(v, LN - 1, 1) for v in mids]
        for c in range(CT):
            v, o = mids[c], offs[c]
            west = jnp.where(first, fwd[c - 1] if c > 0 else 0.0, fwd[c])
            east = jnp.where(last, bwd[c + 1] if c < CT - 1 else 0.0, bwd[c])
            north = src[pl.ds(pl.multiple_of(o - COL, 8), 8), :]
            south = src[pl.ds(pl.multiple_of(o + COL, 8), 8), :]
            if k > 0:
                down = src[pl.ds(o - 1, 8), :]
            else:
                down = jnp.where(low, v, pltpu.roll(v, 1, 0))
            if k < LV // 8 - 1:
                up = src[pl.ds(o + 1, 8), :]
            else:
                up = jnp.where(high, v, pltpu.roll(v, 7, 0))
            s = ((north + south) + (west + east)) + 0.2 * (down + up)
            emit(c, k, v, s, o)


class Fetch:
    def __init__(self, src, dst, sems):
        count, size = src.shape[0], src.shape[2]
        self.parts = [pltpu.make_async_copy(src.at[t, 0], dst.at[pl.ds(t * size, size)], sems.at[t]) for t in range(count)]

    def start(self):
        for part in self.parts:
            part.start()

    def wait(self):
        for part in self.parts:
            part.wait()


def tally_of(ref):
    return [[ref[side * NT + t].astype(I32) for t in range(NT)] for side in range(2)]


def mask_row(mask, at, c):
    return mask[pl.ds(at * CT + c, 8, stride=0), :]


def forward_row(src, dst, mask, at, blank=None):
    ms = [mask_row(mask, at, c) for c in range(CT)]

    def emit(c, k, v, s, o):
        dst[pl.ds(pl.multiple_of(o, 8), 8), :] = ms[c] * (s + v * (0.6 - v * v))
        if blank is not None:
            blank[pl.ds(pl.multiple_of(o, 8), 8), :] = jnp.zeros((8, LN), F32)

    stencil_row(src, at, emit)


def adjoint_row(src, state, forcing, mask, at):
    ms = [mask_row(mask, at, c) for c in range(CT)]

    def emit(c, k, g, s, o):
        spot = pl.ds(pl.multiple_of(o, 8), 8)
        y = state[spot, :]
        forcing[spot, :] = ms[c] * ((s + g * (0.6 - 3.0 * (y * y))) + forcing[spot, :])

    stencil_row(src, at, emit)


def gradient_row(src, state, out, at):
    def emit(c, k, g, s, o):
        y = state[pl.ds(pl.multiple_of(o, 8), 8), :]
        out[pl.ds(pl.multiple_of(o - H * COL, 8), 8), :] = 0.2 * (s + g * (0.6 - 3.0 * (y * y)))

    stencil_row(src, at, emit)


def loop(first, last, body, unroll):
    def some(i, _):
        for u in range(unroll):
            body(first + H + i * unroll + u)
        return 0

    lax.fori_loop(0, (last + 1 - first) // unroll, some, 0)


def rims(reach, body):
    for at in [*range(-reach, 3 - reach), *range(ROWS - 3 + reach, ROWS + reach)]:
        body(at + H)


def even():
    return lax.rem(lax.axis_index("along"), 2) == 0


def edges_kernel(basic, land_at, staged, twin, other, mask, land, sems):
    def copy(c):
        return pltpu.make_async_copy(basic.at[:, :, pl.ds(c * LN, LN)], staged.at[c], sems.at[c])

    sea = pltpu.make_async_copy(land_at, land, sems.at[CT])
    sea.start()
    for c in range(CT):
        copy(c).start()
    sea.wait()
    for c in range(CT):
        mask[pl.ds(H * CT + c, ROWS, stride=CT), :] = 0.2 * land[:, pl.ds(c * LN, LN)].astype(F32)
    lower = jnp.where(even(), ROWS - H, 0)
    for c in range(CT):
        copy(c).wait()
        flat = staged.at[c].reshape(LV * ROWS, LN)
        for out, first in ((twin, lower), (other, ROWS - H - lower)):
            for j in range(H):
                r = first + j
                half = 2.5 * mask_row(mask, r + H, c)
                for k in range(LV // 8):
                    v = flat[pl.ds(k * 8 * ROWS + r, 8, stride=ROWS), :]
                    out[pl.ds((j * CT + c) * LV + k * 8, 8), :] = half * v
                out[pl.ds(H * COL + j * CT + c, 1), :] = mask[pl.ds((r + H) * CT + c, 1), :]


def edges(basic, land):
    return pl.pallas_call(
        edges_kernel,
        out_shape=[
            jax.ShapeDtypeStruct((CT, LV, ROWS, LN), F32),
            jax.ShapeDtypeStruct((EDGE, LN), F32),
            jax.ShapeDtypeStruct((EDGE, LN), F32),
            MASK,
        ],
        in_specs=[HBM, HBM],
        out_specs=[VM] * 4,
        scratch_shapes=[pltpu.VMEM((ROWS, CT * LN), I32), pltpu.SemaphoreType.DMA((CT + 1,))],
        compiler_params=params(4),
        cost_estimate=cost(2),
        name="edges",
    )(pltpu.with_memory_space_constraint(basic, pltpu.HBM), pltpu.with_memory_space_constraint(land, pltpu.HBM))


def order_kernel(cells_at, count_at, value_at, addr, sval, lane, spot, second, tallies, codes, cells, count, value, sems):
    fetches = [
        pltpu.make_async_copy(src, dst, sems.at[i])
        for i, (src, dst) in enumerate(((cells_at, cells), (count_at, count), (value_at, value)))
    ]
    for f in fetches:
        f.start()
    for f in fetches:
        f.wait()
    slot = lax.broadcasted_iota(I32, (1, CAP), 1)
    ups, downs = [], []
    for t in range(NT):
        row = (cells[t] >> 10) & (ROWS - 1)
        alive = slot < count[0, t]
        ups.append(jnp.logical_and(alive, row <= t))
        downs.append(jnp.logical_and(alive, row >= ROWS - 1 - t))
    one = [jnp.where(f, 1.0, 0.0) for f in ups + downs]
    flags = jnp.concatenate(one + [jnp.zeros((10, CAP), F32)], axis=0).astype(jnp.bfloat16)
    tri = jnp.where(
        lax.broadcasted_iota(I32, (CAP, CAP), 0) < lax.broadcasted_iota(I32, (CAP, CAP), 1), 1.0, 0.0
    ).astype(jnp.bfloat16)
    before = jnp.dot(flags, tri, preferred_element_type=F32)
    codes[...] = jnp.zeros((CODE, LN), F32)
    sub = lax.broadcasted_iota(I32, (CAP, CAP), 0)
    first = lax.broadcasted_iota(I32, (1, LN), 1)
    tally = jnp.zeros((1, LN), F32)
    for t in range(NT):
        up, down = ups[t], downs[t]
        pu, pd = before[t : t + 1], before[NT + t : NT + t + 1]
        nu = jnp.sum(one[t], axis=1, keepdims=True)
        nd = jnp.sum(one[NT + t], axis=1, keepdims=True)
        tally = tally + jnp.where(first == t, nu, 0.0) + jnp.where(first == NT + t, nd, 0.0)
        rank = jnp.where(up, pu, jnp.where(down, CAP - nd + pd, nu + slot.astype(F32) - pu - pd)).astype(I32)
        place = jnp.where(sub == rank, 1.0, 0.0).astype(jnp.bfloat16)
        cell, v = cells[t], value[t]
        v1 = v.astype(jnp.bfloat16).astype(F32)
        v2 = (v - v1).astype(jnp.bfloat16).astype(F32)
        parts = [
            (cell >> 16).astype(F32),
            ((cell >> 8) & 255).astype(F32),
            (cell & 255).astype(F32),
            v1,
            v2,
            v - v1 - v2,
            jnp.where(slot < count[0, t], 1.0, 0.0),
        ]
        left = jnp.concatenate(parts + [jnp.zeros((9, CAP), F32)], axis=0).astype(jnp.bfloat16)
        out = lax.dot_general(left, place, (((1,), (1,)), ((), ())), preferred_element_type=F32)
        cell = (out[0:1] * 65536.0 + out[1:2] * 256.0 + out[2:3]).astype(I32)
        row, level, where = (cell >> 10) & (ROWS - 1), cell >> 14, (cell >> 7) & (ROWS * CT - 1)
        alive = out[6:7] > 0.5
        own = (where + H * CT) * LV + level
        addr[t] = own
        sval[t] = out[3:4] + out[4:5] + out[5:6]
        lane[t] = jnp.where(alive, (cell & (LN - 1)).astype(F32), -1.0)
        if t == NT - 1:
            spot[0] = where + H * CT
            second[0] = jnp.where(jnp.logical_or(row == 1, row == ROWS - 2), -3.0, 0.0)
        far = jnp.where(row < ROWS // 2, own + ROWS * COL, own - ROWS * COL)
        near = jnp.logical_or(row <= t, row >= ROWS - 1 - t)
        code = jnp.where(near, far * LN + (cell & (LN - 1)), 0).astype(F32)
        for q in range(CAP // LN):
            codes[pl.ds(4 * t + q, 1), :] = code[:, q * LN : (q + 1) * LN]
    codes[pl.ds(12, 1), :] = tally
    tallies[0] = tally


def order(cells, count, value):
    ints, floats = jax.ShapeDtypeStruct((NT, 1, CAP), I32), jax.ShapeDtypeStruct((NT, 1, CAP), F32)
    return pl.pallas_call(
        order_kernel,
        out_shape=[ints, floats, floats, jax.ShapeDtypeStruct((1, 1, CAP), I32), jax.ShapeDtypeStruct((1, 1, CAP), F32), jax.ShapeDtypeStruct((1, 1, LN), F32), jax.ShapeDtypeStruct((CODE, LN), F32)],
        in_specs=[HBM] * 3,
        out_specs=[VM] * 7,
        scratch_shapes=[
            pltpu.VMEM((NT, 1, CAP), I32),
            pltpu.SMEM((1, NT), I32),
            pltpu.VMEM((NT, 1, CAP), F32),
            pltpu.SemaphoreType.DMA((3,)),
        ],
        compiler_params=params(6),
        cost_estimate=cost(2),
        name="order",
    )(*(pltpu.with_memory_space_constraint(x, pltpu.HBM) for x in (cells, count, value)))


def upright(line):
    return jnp.broadcast_to(line, (LN, LN)).T


def interior_kernel(staged, mask, lane, sval, addrs, spots, tallies, y0, y1, y2, y3, f1, f2, f3, twice, known, sea, total,
                    g1, g2, g3, terms, at_ref, spot_ref, n_ref, sems):
    fetches = [Fetch(addrs, at_ref, sems), Fetch(spots, spot_ref, sems.at[pl.ds(NT, 1)]), Fetch(tallies, n_ref, sems.at[pl.ds(NT + 1, 1)])]
    for fetch in fetches:
        fetch.start()
    for c in range(CT):
        flat = staged.at[c].reshape(LV * ROWS, LN)

        def turn(i, _):
            for u in range(4):
                r = i * 4 + u
                half = 2.5 * mask_row(mask, r + H, c)
                for k in range(LV // 8):
                    v = flat[pl.ds(k * 8 * ROWS + r, 8, stride=ROWS), :]
                    y0[pl.ds(pl.multiple_of((r + H) * COL + c * LV + k * 8, 8), 8), :] = half * v
            return 0

        lax.fori_loop(0, ROWS // 4, turn, 0)

    zero = jnp.zeros((8, LN), F32)
    for at in (H - 2, ROWS + H + 1):
        for j in range(COL // 8):
            y2[pl.ds(at * COL + j * 8, 8), :] = zero
    for t, f in enumerate((f1, f2, f3)):
        for at in [*range(H + t + 1), *range(ROWS + H - t - 1, RX)]:
            for j in range(COL // 8):
                f[pl.ds(at * COL + j * 8, 8), :] = zero
    loop(1, 14, lambda at: forward_row(y0, y1, mask, at, f1), 7)
    loop(2, 13, lambda at: forward_row(y1, y2, mask, at, f2), 6)
    loop(3, 12, lambda at: forward_row(y2, y3, mask, at, f3), 5)
    for fetch in fetches:
        fetch.wait()

    def gather(i, _):
        for u in range(8):
            s = i * 8 + u
            here = pl.ds(s, 1)
            g1[here, :] = y1[pl.ds(at_ref[s], 1), :]
            g2[here, :] = y2[pl.ds(at_ref[CAP + s], 1), :]
            g3[here, :] = y3[pl.ds(at_ref[2 * CAP + s], 1), :]
            sea[here, :] = mask[pl.ds(spot_ref[s], 1), :]
        return 0

    lax.fori_loop(0, CAP // 8, gather, 0)
    ups, downs = tally_of(n_ref)
    ids = lax.broadcasted_iota(I32, (LN, LN), 1).astype(F32)
    slot = lax.broadcasted_iota(I32, (LN, LN), 0)
    acc = zero
    for t, g in enumerate((g1, g2, g3)):
        for q in range(CAP // LN):
            part = pl.ds(q * LN, LN)
            hit = upright(lane[t, :, part]) == ids
            rows = pl.ds(t * CAP + q * LN, LN)
            two, have = jnp.where(hit, 2.0, 0.0), jnp.where(hit, upright(sval[t, :, part]), 0.0)
            twice[rows, :] = two
            known[rows, :] = have
            early = jnp.logical_and(slot + q * LN >= ups[t], slot + q * LN < CAP - downs[t])
            d = jnp.where(early, g[part, :] * two - have, 0.0)
            acc = acc + jnp.sum((d * d).reshape(LN // 8, 8, LN), axis=0)
            terms[rows, :] = d * (5.0 * sea[part, :]) if t == NT - 1 else 5.0 * d
    total[...] = acc

    def scatter(i, _):
        for u in range(8):
            s = i * 8 + u
            for t, f in enumerate((f1, f2, f3)):
                spot = pl.ds(at_ref[t * CAP + s], 1)
                f[spot, :] = f[spot, :] + terms[pl.ds(t * CAP + s, 1), :]
        return 0

    lax.fori_loop(0, CAP // 8, scatter, 0)


def interior(staged, mask, lane, sval, addrs, spots, tallies):
    rows = jax.ShapeDtypeStruct((NT * CAP, LN), F32)
    few = pltpu.VMEM((CAP, LN), F32)
    return pl.pallas_call(
        interior_kernel,
        out_shape=[FIELD] * 7 + [rows, rows, jax.ShapeDtypeStruct((CAP, LN), F32), jax.ShapeDtypeStruct((8, LN), F32)],
        in_specs=[VM] * 4 + [ANY] * 3,
        out_specs=[VM] * 11,
        scratch_shapes=[
            few,
            few,
            few,
            pltpu.VMEM((NT * CAP, LN), F32),
            pltpu.SMEM((NT * CAP,), I32),
            pltpu.SMEM((CAP,), I32),
            pltpu.SMEM((LN,), F32),
            pltpu.SemaphoreType.DMA((NT + 2,)),
        ],
        compiler_params=params(6),
        cost_estimate=cost(11),
        name="interior",
    )(staged, mask, lane, sval, addrs, spots, tallies)


def bands_kernel(y0i, y1i, y2i, y3, f1i, f2i, f3i, maski, twice, known, sea, totali, second, codes, addrs, tallies, twin, other,
                 y0, y1, y2, f1, f2, f3, mask, pay, terms, extra, at_ref, n_ref, sems):
    fetches = [Fetch(addrs, at_ref, sems), Fetch(tallies, n_ref, sems.at[pl.ds(NT, 1)])]
    for fetch in fetches:
        fetch.start()
    lower = jnp.where(even(), ROWS + H, 0)
    for halo, first in ((twin, lower), (other, ROWS + H - lower)):
        base = pl.multiple_of(first * COL, 8)
        for q in range(H * COL // 8):
            y0[pl.ds(base + q * 8, 8), :] = halo[pl.ds(q * 8, 8), :]
        base = pl.multiple_of(first * CT, 8)
        for j in range(H):
            mask[pl.ds(base + j * CT, CT), :] = halo[pl.ds(H * COL + j * CT, CT), :]
    for src, dst, reach in ((y0, y1, 2), (y1, y2, 1), (y2, y3, 0)):
        rims(reach, lambda at: forward_row(src, dst, mask, at))
    for fetch in fetches:
        fetch.wait()
    ups, downs = tally_of(n_ref)
    most = 0
    for t in range(NT):
        most = jnp.maximum(most, (jnp.maximum(ups[t], downs[t]) + t) // (t + 1))

    def item(i, acc):
        for t, (y, f) in ((2, (y3, f3)), (1, (y2, f2)), (0, (y1, f1))):
            for u in range(t + 1):
                j = i * (t + 1) + u
                near = jnp.minimum(j, CAP - 1)
                for n, slot in ((ups[t], near), (downs[t], CAP - 1 - near)):
                    ok = j < n
                    row = t * CAP + slot
                    spot = pl.ds(at_ref[row], 1)
                    d = jnp.where(ok, y[spot, :] * twice[pl.ds(row, 1), :] - known[pl.ds(row, 1), :], 0.0)
                    acc = acc + d * d
                    if t == NT - 1:
                        d = d * (5.0 * sea[pl.ds(slot, 1), :])
                        z = y2[spot, :]
                        extra[pl.ds(jnp.where(ok, slot, CAP), 1), :] = (z * z) * d
                    else:
                        d = 5.0 * d
                    f[spot, :] = f[spot, :] + d
                    terms[pl.ds(jnp.where(ok, row, NT * CAP), 1), :] = d
        return acc

    acc = lax.fori_loop(0, most, item, jnp.zeros((1, LN), F32))
    for q in range(CAP // LN):
        for t in range(NT):

            @pl.when(jnp.logical_or(ups[t] > q * LN, downs[t] > CAP - (q + 1) * LN))
            def _():
                pay[pl.ds(4 * t + q, 1), :] = jnp.sum(terms[pl.ds(t * CAP + q * LN, LN), :].T, axis=0, keepdims=True)
                if t == NT - 1:
                    e = jnp.sum(extra[pl.ds(q * LN, LN), :].T, axis=0, keepdims=True)
                    pay[pl.ds(12 + q, 1), :] = e * second[0, :, pl.ds(q * LN, LN)]

    pay[pl.ds(CODE, CODE), :] = codes[...]
    pay[pl.ds(2 * CODE, 8), :] = totali[...] + jnp.where(sublanes() == 0, jnp.broadcast_to(acc, (8, LN)), 0.0)


def bands(y0, y1, y2, y3, f1, f2, f3, mask, twice, known, sea, total, second, codes, addrs, tallies, twin, other):
    return pl.pallas_call(
        bands_kernel,
        out_shape=[FIELD] * 6 + [MASK, jax.ShapeDtypeStruct((PAY, LN), F32)],
        in_specs=[VM] * 14 + [ANY] * 2 + [VM] * 2,
        out_specs=[VM] * 8,
        input_output_aliases={0: 0, 1: 1, 2: 2, 4: 3, 5: 4, 6: 5, 7: 6},
        scratch_shapes=[
            pltpu.VMEM((NT * CAP + 8, LN), F32),
            pltpu.VMEM((CAP + 8, LN), F32),
            pltpu.SMEM((NT * CAP,), I32),
            pltpu.SMEM((LN,), F32),
            pltpu.SemaphoreType.DMA((NT + 1,)),
        ],
        compiler_params=params(4),
        cost_estimate=cost(5),
        name="bands",
    )(y0, y1, y2, y3, f1, f2, f3, mask, twice, known, sea, total, second, codes, addrs, tallies, twin, other)


def adjoint_kernel(first, last, unroll, src, state, forcing, mask, out):
    loop(first, last, lambda at: adjoint_row(src, state, out, mask, at), unroll)


def adjoint(first, last, unroll, src, state, forcing, mask):
    return pl.pallas_call(
        functools.partial(adjoint_kernel, first, last, unroll),
        out_shape=FIELD,
        in_specs=[VM] * 4,
        out_specs=VM,
        input_output_aliases={2: 0},
        compiler_params=params(2),
        cost_estimate=cost(2),
        name="adjoint",
    )(src, state, forcing, mask)


def finish_kernel(scale, y0, y1, y2, f1i, f2i, f3i, mask, twin, other, x, y, f1, f2, f3, out, misfit, grad, staged,
                  a_ref, b_ref, ca, cb, sems):
    misfit[...] = jnp.sum(x[...] + y[...], keepdims=True) * scale

    def fetches(above, below):
        return [pltpu.make_async_copy(src, dst, sems.at[CT + i]) for i, (src, dst) in enumerate(((above, a_ref), (below, b_ref)))]

    @pl.when(even())
    def _():
        for f in fetches(other, twin):
            f.start()

    @pl.when(jnp.logical_not(even()))
    def _():
        for f in fetches(twin, other):
            f.start()

    for q in range(COL // 8):
        for buf in (ca, cb):
            buf[pl.ds(q * 8, 8), :] = jnp.zeros((8, LN), F32)
    loop(3, 12, lambda at: gradient_row(f1, y0, grad, at), 5)
    for f in fetches(twin, other):
        f.wait()
    counts = CODE * LN + 12 * LN
    lane = lax.broadcasted_iota(I32, (1, LN), 1)
    na = [a_ref[counts + NT + t].astype(I32) for t in range(NT)]
    nb = [b_ref[counts + t].astype(I32) for t in range(NT)]
    most = 0
    for t in range(NT):
        most = jnp.maximum(most, (jnp.maximum(na[t], nb[t]) + t) // (t + 1))

    def item(i, _):
        for t, f in ((2, f3), (1, f2), (0, f1)):
            for u in range(t + 1):
                j = i * (t + 1) + u
                slot_of = jnp.minimum(j, CAP - 1)
                for ref, n, slot, side in ((a_ref, na[t], CAP - 1 - slot_of, ca), (b_ref, nb[t], slot_of, cb)):
                    code = ref[CODE * LN + t * CAP + slot].astype(I32)
                    hit = lane == jnp.where(j < n, code & (LN - 1), -1)
                    addr = code >> 7
                    spot = pl.ds(addr, 1)
                    f[spot, :] = f[spot, :] + jnp.where(hit, ref[t * CAP + slot], 0.0)
                    if t == NT - 1:
                        start = (1 if side is ca else ROWS + H + 1) * COL
                        far = addr - start
                        inside = jnp.logical_and(far >= 0, far < COL)
                        spot = pl.ds(jnp.where(inside, far, 0), 1)
                        side[spot, :] = side[spot, :] + jnp.where(hit, ref[12 * LN + slot], 0.0)
        return 0

    lax.fori_loop(0, most, item, 0)
    for side, at in ((ca, 1), (cb, ROWS + H + 1)):
        for q in range(COL // 8):
            spot = pl.ds(at * COL + q * 8, 8)
            f2[spot, :] = f2[spot, :] + side[pl.ds(q * 8, 8), :]
    for src, state, dst, reach in ((f3, y2, f2, 2), (f2, y1, f1, 1)):
        rims(reach, lambda at: adjoint_row(src, state, dst, mask, at))
    rims(0, lambda at: gradient_row(f1, y0, grad, at))

    def copy(c):
        return pltpu.make_async_copy(staged.at[c], out.at[:, :, pl.ds(c * LN, LN)], sems.at[c])

    for c in range(CT):
        def turn(k, _):
            for half in range(2):
                v = grad[pl.ds(half * 8 * COL + c * LV + k, 8, stride=COL), :]
                staged[c, k, pl.ds(half * 8, 8), :] = v
            return 0

        for k in range(LV):
            turn(k, 0)
        copy(c).start()
    for c in range(CT):
        copy(c).wait()


def finish(y0, y1, y2, f1, f2, f3, mask, twin, other, x, y, scale):
    return pl.pallas_call(
        functools.partial(finish_kernel, scale),
        out_shape=[FIELD] * 3 + [jax.ShapeDtypeStruct((LV, ROWS, CT * LN), F32), jax.ShapeDtypeStruct((1, 1), F32)],
        in_specs=[VM] * 7 + [ANY] * 2 + [VM] * 2,
        out_specs=[VM] * 3 + [ANY, VM],
        input_output_aliases={3: 0, 4: 1, 5: 2},
        scratch_shapes=[
            pltpu.VMEM((ROWS * COL, LN), F32),
            pltpu.VMEM((CT, LV, ROWS, LN), F32),
            pltpu.SMEM((PAY * LN,), F32),
            pltpu.SMEM((PAY * LN,), F32),
            pltpu.VMEM((COL, LN), F32),
            pltpu.VMEM((COL, LN), F32),
            pltpu.SemaphoreType.DMA((CT + 2,)),
        ],
        compiler_params=params(14),
        cost_estimate=cost(7),
        name="finish",
    )(y0, y1, y2, f1, f2, f3, mask, twin, other, x, y)[3:]


def add_kernel(first, pay, twin, out):
    out[...] = pay[pl.ds(first, 8), :] + twin[pl.ds(first, 8), :]


def add(first, a, b):
    return pl.pallas_call(
        functools.partial(add_kernel, first),
        out_shape=jax.ShapeDtypeStruct((8, LN), F32),
        in_specs=[VM, VM],
        out_specs=VM,
        compiler_params=params(1),
        cost_estimate=cost(0.1),
        name="add",
    )(a, b)


def sum_along(pay, twin, stages, held):
    size = lax.axis_size("along")
    steps = [1 << i for i in range(1, size.bit_length() - 1)]
    x = add(2 * CODE, pay, twin)
    other = jnp.zeros_like(x)
    if size & (size - 1):
        x, steps = lax.psum(0.5 * x, "along"), []
    for i in range(max(len(steps), len(stages))):
        if i < len(steps):
            if i > 0:
                x = add(0, x, other)
            x, held = lax.optimization_barrier((x, held))
            other = lax.ppermute(x, "along", [(p, p ^ steps[i]) for p in range(size)])
        if i < len(stages):
            held = stages[i](*held)
    return x, other, held


def local(basic_state, land_sea, obs_cells, obs_count, obs_value):
    size = lax.axis_size("along")
    twins = [(i, i ^ 1) for i in range(size)]
    others = [(i, i - 1 if i % 2 == 0 else i + 1) for i in range(1, size - 1)]
    cells = obs_cells.transpose(1, 0, 2)
    value = obs_value.transpose(1, 0, 2)
    staged, twin, other, mask = edges(basic_state, land_sea)
    other = lax.ppermute(other, "along", others)
    twin = lax.ppermute(twin, "along", twins)
    addrs, sval, lane, spots, second, tallies, codes = order(cells, obs_count, value)
    y0, y1, y2, y3, f1, f2, f3, twice, known, sea, total = interior(staged, mask, lane, sval, addrs, spots, tallies)
    y0, y1, y2, f1, f2, f3, mask, pay = bands(
        y0, y1, y2, y3, f1, f2, f3, mask, twice, known, sea, total, second, codes, addrs, tallies, twin, other
    )
    other = lax.ppermute(pay, "along", others)
    twin = lax.ppermute(pay, "along", twins)
    stages = (
        lambda a, b, c: (a, adjoint(1, 14, 7, c, y2, b, mask), c),
        lambda a, b, c: (adjoint(2, 13, 6, b, y1, a, mask), b, c),
    )
    x, y, held = sum_along(pay, twin, stages, (f1, f2, f3))
    scale = 1.0 / (2.0 * size * obs_cells.shape[1] * obs_cells.shape[2])
    gradient, misfit = finish(y0, y1, y2, *held, mask, twin.reshape(-1), other.reshape(-1), x, y, scale)
    misfit = misfit.reshape(1)
    return gradient, misfit


def solution(mesh):
    in_specs = (
        P(None, ("ens", "along"), None),
        P(("ens", "along"), None),
        P(("ens", "along"), None, None),
        P(("ens", "along"), None),
        P(("ens", "along"), None, None),
    )
    out_specs = (P(None, ("ens", "along"), None), P("ens"))
    return jax.shard_map(local, mesh=mesh, in_specs=in_specs, out_specs=out_specs, check_vma=False)
```

```python
import functools

import jax
import jax.numpy as jnp
from jax import lax
from jax.experimental import pallas as pl
from jax.experimental.pallas import tpu as pltpu
from jax.sharding import PartitionSpec as P

F32 = jnp.float32
I32 = jnp.int32
ROWS, CT, LV, LN = 16, 8, 40, 128
H = 3
RX = ROWS + 2 * H
COL = CT * LV
EDGE = H * COL + H * CT
CAP = 512
NT = 3
PAY = 40
CODE = 16

VM = pl.BlockSpec(memory_space=pltpu.VMEM)
SM = pl.BlockSpec(memory_space=pltpu.SMEM)
HBM = pl.BlockSpec(memory_space=pltpu.MemorySpace.HBM)
ANY = pl.BlockSpec(memory_space=pl.ANY)
FIELD = jax.ShapeDtypeStruct((RX * COL, LN), F32)
MASK = jax.ShapeDtypeStruct((RX * CT, LN), F32)


def params(mib):
    return pltpu.CompilerParams(vmem_limit_bytes=mib << 20)


def cost(us):
    return pl.CostEstimate(flops=0, bytes_accessed=int(us * 3.0e6), transcendentals=0)


def lanes():
    return lax.broadcasted_iota(I32, (8, LN), 1)


def sublanes():
    return lax.broadcasted_iota(I32, (8, LN), 0)


def stencil_row(src, at, emit):
    lane, sub = lanes(), sublanes()
    first, last = lane == 0, lane == LN - 1
    low, high = sub == 0, sub == 7
    base = pl.multiple_of(at * COL, COL)
    for k in range(LV // 8):
        offs = [base + c * LV + k * 8 for c in range(CT)]
        mids = [src[pl.ds(pl.multiple_of(o, 8), 8), :] for o in offs]
        fwd = [pltpu.roll(v, 1, 1) for v in mids]
        bwd = [pltpu.roll(v, LN - 1, 1) for v in mids]
        for c in range(CT):
            v, o = mids[c], offs[c]
            west = jnp.where(first, fwd[c - 1] if c > 0 else 0.0, fwd[c])
            east = jnp.where(last, bwd[c + 1] if c < CT - 1 else 0.0, bwd[c])
            north = src[pl.ds(pl.multiple_of(o - COL, 8), 8), :]
            south = src[pl.ds(pl.multiple_of(o + COL, 8), 8), :]
            if k > 0:
                down = src[pl.ds(o - 1, 8), :]
            else:
                down = jnp.where(low, v, pltpu.roll(v, 1, 0))
            if k < LV // 8 - 1:
                up = src[pl.ds(o + 1, 8), :]
            else:
                up = jnp.where(high, v, pltpu.roll(v, 7, 0))
            s = ((north + south) + (west + east)) + 0.2 * (down + up)
            emit(c, k, v, s, o)


class Fetch:
    def __init__(self, src, dst, sems):
        count, size = src.shape[0], src.shape[2]
        self.parts = [pltpu.make_async_copy(src.at[t, 0], dst.at[pl.ds(t * size, size)], sems.at[t]) for t in range(count)]

    def start(self):
        for part in self.parts:
            part.start()

    def wait(self):
        for part in self.parts:
            part.wait()


def tally_of(ref):
    return [[ref[side * NT + t].astype(I32) for t in range(NT)] for side in range(2)]


def mask_row(mask, at, c):
    return mask[pl.ds(at * CT + c, 8, stride=0), :]


def forward_row(src, dst, mask, at, blank=None):
    ms = [mask_row(mask, at, c) for c in range(CT)]

    def emit(c, k, v, s, o):
        dst[pl.ds(pl.multiple_of(o, 8), 8), :] = ms[c] * (s + v * (0.6 - v * v))
        if blank is not None:
            blank[pl.ds(pl.multiple_of(o, 8), 8), :] = jnp.zeros((8, LN), F32)

    stencil_row(src, at, emit)


def adjoint_row(src, state, forcing, mask, at):
    ms = [mask_row(mask, at, c) for c in range(CT)]

    def emit(c, k, g, s, o):
        spot = pl.ds(pl.multiple_of(o, 8), 8)
        y = state[spot, :]
        forcing[spot, :] = ms[c] * ((s + g * (0.6 - 3.0 * (y * y))) + forcing[spot, :])

    stencil_row(src, at, emit)


def gradient_row(src, state, out, at):
    def emit(c, k, g, s, o):
        y = state[pl.ds(pl.multiple_of(o, 8), 8), :]
        out[pl.ds(pl.multiple_of(o - H * COL, 8), 8), :] = 0.2 * (s + g * (0.6 - 3.0 * (y * y)))

    stencil_row(src, at, emit)


def loop(first, last, body, unroll):
    def some(i, _):
        for u in range(unroll):
            body(first + H + i * unroll + u)
        return 0

    lax.fori_loop(0, (last + 1 - first) // unroll, some, 0)


def rims(reach, body):
    for at in [*range(-reach, 3 - reach), *range(ROWS - 3 + reach, ROWS + reach)]:
        body(at + H)


def even():
    return lax.rem(lax.axis_index("along"), 2) == 0


def edges_kernel(basic, land_at, staged, twin, other, mask, land, sems):
    def copy(c):
        return pltpu.make_async_copy(basic.at[:, :, pl.ds(c * LN, LN)], staged.at[c], sems.at[c])

    sea = pltpu.make_async_copy(land_at, land, sems.at[CT])
    sea.start()
    for c in range(CT):
        copy(c).start()
    sea.wait()
    for c in range(CT):
        mask[pl.ds(H * CT + c, ROWS, stride=CT), :] = 0.2 * land[:, pl.ds(c * LN, LN)].astype(F32)
    lower = jnp.where(even(), ROWS - H, 0)
    for c in range(CT):
        copy(c).wait()
        flat = staged.at[c].reshape(LV * ROWS, LN)
        for out, first in ((twin, lower), (other, ROWS - H - lower)):
            for j in range(H):
                r = first + j
                half = 2.5 * mask_row(mask, r + H, c)
                for k in range(LV // 8):
                    v = flat[pl.ds(k * 8 * ROWS + r, 8, stride=ROWS), :]
                    out[pl.ds((j * CT + c) * LV + k * 8, 8), :] = half * v
                out[pl.ds(H * COL + j * CT + c, 1), :] = mask[pl.ds((r + H) * CT + c, 1), :]


def edges(basic, land):
    return pl.pallas_call(
        edges_kernel,
        out_shape=[
            jax.ShapeDtypeStruct((CT, LV, ROWS, LN), F32),
            jax.ShapeDtypeStruct((EDGE, LN), F32),
            jax.ShapeDtypeStruct((EDGE, LN), F32),
            MASK,
        ],
        in_specs=[HBM, HBM],
        out_specs=[VM] * 4,
        scratch_shapes=[pltpu.VMEM((ROWS, CT * LN), I32), pltpu.SemaphoreType.DMA((CT + 1,))],
        compiler_params=params(4),
        cost_estimate=cost(2),
        name="edges",
    )(pltpu.with_memory_space_constraint(basic, pltpu.HBM), pltpu.with_memory_space_constraint(land, pltpu.HBM))


def order_kernel(cells_at, count_at, value_at, addr, sval, lane, spot, second, tallies, codes, cells, count, value, sems):
    fetches = [
        pltpu.make_async_copy(src, dst, sems.at[i])
        for i, (src, dst) in enumerate(((cells_at, cells), (count_at, count), (value_at, value)))
    ]
    for f in fetches:
        f.start()
    for f in fetches:
        f.wait()
    slot = lax.broadcasted_iota(I32, (1, CAP), 1)
    ups, downs = [], []
    for t in range(NT):
        row = (cells[t] >> 10) & (ROWS - 1)
        alive = slot < count[0, t]
        ups.append(jnp.logical_and(alive, row <= t))
        downs.append(jnp.logical_and(alive, row >= ROWS - 1 - t))
    one = [jnp.where(f, 1.0, 0.0) for f in ups + downs]
    flags = jnp.concatenate(one + [jnp.zeros((10, CAP), F32)], axis=0).astype(jnp.bfloat16)
    tri = jnp.where(
        lax.broadcasted_iota(I32, (CAP, CAP), 0) < lax.broadcasted_iota(I32, (CAP, CAP), 1), 1.0, 0.0
    ).astype(jnp.bfloat16)
    before = jnp.dot(flags, tri, preferred_element_type=F32)
    codes[...] = jnp.zeros((CODE, LN), F32)
    sub = lax.broadcasted_iota(I32, (CAP, CAP), 0)
    first = lax.broadcasted_iota(I32, (1, LN), 1)
    tally = jnp.zeros((1, LN), F32)
    for t in range(NT):
        up, down = ups[t], downs[t]
        pu, pd = before[t : t + 1], before[NT + t : NT + t + 1]
        nu = jnp.sum(one[t], axis=1, keepdims=True)
        nd = jnp.sum(one[NT + t], axis=1, keepdims=True)
        tally = tally + jnp.where(first == t, nu, 0.0) + jnp.where(first == NT + t, nd, 0.0)
        rank = jnp.where(up, pu, jnp.where(down, CAP - nd + pd, nu + slot.astype(F32) - pu - pd)).astype(I32)
        place = jnp.where(sub == rank, 1.0, 0.0).astype(jnp.bfloat16)
        cell, v = cells[t], value[t]
        v1 = v.astype(jnp.bfloat16).astype(F32)
        v2 = (v - v1).astype(jnp.bfloat16).astype(F32)
        parts = [
            (cell >> 16).astype(F32),
            ((cell >> 8) & 255).astype(F32),
            (cell & 255).astype(F32),
            v1,
            v2,
            v - v1 - v2,
            jnp.where(slot < count[0, t], 1.0, 0.0),
        ]
        left = jnp.concatenate(parts + [jnp.zeros((9, CAP), F32)], axis=0).astype(jnp.bfloat16)
        out = lax.dot_general(left, place, (((1,), (1,)), ((), ())), preferred_element_type=F32)
        cell = (out[0:1] * 65536.0 + out[1:2] * 256.0 + out[2:3]).astype(I32)
        row, level, where = (cell >> 10) & (ROWS - 1), cell >> 14, (cell >> 7) & (ROWS * CT - 1)
        alive = out[6:7] > 0.5
        own = (where + H * CT) * LV + level
        addr[t] = own
        sval[t] = out[3:4] + out[4:5] + out[5:6]
        lane[t] = jnp.where(alive, (cell & (LN - 1)).astype(F32), -1.0)
        if t == NT - 1:
            spot[0] = where + H * CT
            second[0] = jnp.where(jnp.logical_or(row == 1, row == ROWS - 2), -3.0, 0.0)
        far = jnp.where(row < ROWS // 2, own + ROWS * COL, own - ROWS * COL)
        near = jnp.logical_or(row <= t, row >= ROWS - 1 - t)
        code = jnp.where(near, far * LN + (cell & (LN - 1)), 0).astype(F32)
        for q in range(CAP // LN):
            codes[pl.ds(4 * t + q, 1), :] = code[:, q * LN : (q + 1) * LN]
    codes[pl.ds(12, 1), :] = tally
    tallies[0] = tally


def order(cells, count, value):
    ints, floats = jax.ShapeDtypeStruct((NT, 1, CAP), I32), jax.ShapeDtypeStruct((NT, 1, CAP), F32)
    return pl.pallas_call(
        order_kernel,
        out_shape=[ints, floats, floats, jax.ShapeDtypeStruct((1, 1, CAP), I32), jax.ShapeDtypeStruct((1, 1, CAP), F32), jax.ShapeDtypeStruct((1, 1, LN), F32), jax.ShapeDtypeStruct((CODE, LN), F32)],
        in_specs=[HBM] * 3,
        out_specs=[VM] * 7,
        scratch_shapes=[
            pltpu.VMEM((NT, 1, CAP), I32),
            pltpu.SMEM((1, NT), I32),
            pltpu.VMEM((NT, 1, CAP), F32),
            pltpu.SemaphoreType.DMA((3,)),
        ],
        compiler_params=params(6),
        cost_estimate=cost(2),
        name="order",
    )(*(pltpu.with_memory_space_constraint(x, pltpu.HBM) for x in (cells, count, value)))


def upright(line):
    return jnp.broadcast_to(line, (LN, LN)).T


def interior_kernel(staged, mask, lane, sval, addrs, spots, tallies, y0, y1, y2, y3, f1, f2, f3, twice, known, sea, total,
                    g1, g2, g3, terms, at_ref, spot_ref, n_ref, sems):
    fetches = [Fetch(addrs, at_ref, sems), Fetch(spots, spot_ref, sems.at[pl.ds(NT, 1)]), Fetch(tallies, n_ref, sems.at[pl.ds(NT + 1, 1)])]
    for fetch in fetches:
        fetch.start()
    for c in range(CT):
        flat = staged.at[c].reshape(LV * ROWS, LN)

        def turn(i, _):
            for u in range(4):
                r = i * 4 + u
                half = 2.5 * mask_row(mask, r + H, c)
                for k in range(LV // 8):
                    v = flat[pl.ds(k * 8 * ROWS + r, 8, stride=ROWS), :]
                    y0[pl.ds(pl.multiple_of((r + H) * COL + c * LV + k * 8, 8), 8), :] = half * v
            return 0

        lax.fori_loop(0, ROWS // 4, turn, 0)

    zero = jnp.zeros((8, LN), F32)
    for at in (H - 2, ROWS + H + 1):
        for j in range(COL // 8):
            y2[pl.ds(at * COL + j * 8, 8), :] = zero
    for t, f in enumerate((f1, f2, f3)):
        for at in [*range(H + t + 1), *range(ROWS + H - t - 1, RX)]:
            for j in range(COL // 8):
                f[pl.ds(at * COL + j * 8, 8), :] = zero
    loop(1, 14, lambda at: forward_row(y0, y1, mask, at, f1), 7)
    loop(2, 13, lambda at: forward_row(y1, y2, mask, at, f2), 6)
    loop(3, 12, lambda at: forward_row(y2, y3, mask, at, f3), 5)
    for fetch in fetches:
        fetch.wait()

    def gather(i, _):
        for u in range(8):
            s = i * 8 + u
            here = pl.ds(s, 1)
            g1[here, :] = y1[pl.ds(at_ref[s], 1), :]
            g2[here, :] = y2[pl.ds(at_ref[CAP + s], 1), :]
            g3[here, :] = y3[pl.ds(at_ref[2 * CAP + s], 1), :]
            sea[here, :] = mask[pl.ds(spot_ref[s], 1), :]
        return 0

    lax.fori_loop(0, CAP // 8, gather, 0)
    ups, downs = tally_of(n_ref)
    ids = lax.broadcasted_iota(I32, (LN, LN), 1).astype(F32)
    slot = lax.broadcasted_iota(I32, (LN, LN), 0)
    acc = zero
    for t, g in enumerate((g1, g2, g3)):
        for q in range(CAP // LN):
            part = pl.ds(q * LN, LN)
            hit = upright(lane[t, :, part]) == ids
            rows = pl.ds(t * CAP + q * LN, LN)
            two, have = jnp.where(hit, 2.0, 0.0), jnp.where(hit, upright(sval[t, :, part]), 0.0)
            twice[rows, :] = two
            known[rows, :] = have
            early = jnp.logical_and(slot + q * LN >= ups[t], slot + q * LN < CAP - downs[t])
            d = jnp.where(early, g[part, :] * two - have, 0.0)
            acc = acc + jnp.sum((d * d).reshape(LN // 8, 8, LN), axis=0)
            terms[rows, :] = d * (5.0 * sea[part, :]) if t == NT - 1 else 5.0 * d
    total[...] = acc

    def scatter(i, _):
        for u in range(8):
            s = i * 8 + u
            for t, f in enumerate((f1, f2, f3)):
                spot = pl.ds(at_ref[t * CAP + s], 1)
                f[spot, :] = f[spot, :] + terms[pl.ds(t * CAP + s, 1), :]
        return 0

    lax.fori_loop(0, CAP // 8, scatter, 0)


def interior(staged, mask, lane, sval, addrs, spots, tallies):
    rows = jax.ShapeDtypeStruct((NT * CAP, LN), F32)
    few = pltpu.VMEM((CAP, LN), F32)
    return pl.pallas_call(
        interior_kernel,
        out_shape=[FIELD] * 7 + [rows, rows, jax.ShapeDtypeStruct((CAP, LN), F32), jax.ShapeDtypeStruct((8, LN), F32)],
        in_specs=[VM] * 4 + [ANY] * 3,
        out_specs=[VM] * 11,
        scratch_shapes=[
            few,
            few,
            few,
            pltpu.VMEM((NT * CAP, LN), F32),
            pltpu.SMEM((NT * CAP,), I32),
            pltpu.SMEM((CAP,), I32),
            pltpu.SMEM((LN,), F32),
            pltpu.SemaphoreType.DMA((NT + 2,)),
        ],
        compiler_params=params(6),
        cost_estimate=cost(11),
        name="interior",
    )(staged, mask, lane, sval, addrs, spots, tallies)


def bands_kernel(y0i, y1i, y2i, y3, f1i, f2i, f3i, maski, twice, known, sea, totali, second, codes, addrs, tallies, twin, other,
                 y0, y1, y2, f1, f2, f3, mask, pay, terms, extra, at_ref, n_ref, sems):
    fetches = [Fetch(addrs, at_ref, sems), Fetch(tallies, n_ref, sems.at[pl.ds(NT, 1)])]
    for fetch in fetches:
        fetch.start()
    lower = jnp.where(even(), ROWS + H, 0)
    for halo, first in ((twin, lower), (other, ROWS + H - lower)):
        base = pl.multiple_of(first * COL, 8)
        for q in range(H * COL // 8):
            y0[pl.ds(base + q * 8, 8), :] = halo[pl.ds(q * 8, 8), :]
        base = pl.multiple_of(first * CT, 8)
        for j in range(H):
            mask[pl.ds(base + j * CT, CT), :] = halo[pl.ds(H * COL + j * CT, CT), :]
    for src, dst, reach in ((y0, y1, 2), (y1, y2, 1), (y2, y3, 0)):
        rims(reach, lambda at: forward_row(src, dst, mask, at))
    for fetch in fetches:
        fetch.wait()
    ups, downs = tally_of(n_ref)
    most = 0
    for t in range(NT):
        most = jnp.maximum(most, (jnp.maximum(ups[t], downs[t]) + t) // (t + 1))

    def item(i, acc):
        for t, (y, f) in ((2, (y3, f3)), (1, (y2, f2)), (0, (y1, f1))):
            for u in range(t + 1):
                j = i * (t + 1) + u
                near = jnp.minimum(j, CAP - 1)
                for n, slot in ((ups[t], near), (downs[t], CAP - 1 - near)):
                    ok = j < n
                    row = t * CAP + slot
                    spot = pl.ds(at_ref[row], 1)
                    d = jnp.where(ok, y[spot, :] * twice[pl.ds(row, 1), :] - known[pl.ds(row, 1), :], 0.0)
                    acc = acc + d * d
                    if t == NT - 1:
                        d = d * (5.0 * sea[pl.ds(slot, 1), :])
                        z = y2[spot, :]
                        extra[pl.ds(jnp.where(ok, slot, CAP), 1), :] = (z * z) * d
                    else:
                        d = 5.0 * d
                    f[spot, :] = f[spot, :] + d
                    terms[pl.ds(jnp.where(ok, row, NT * CAP), 1), :] = d
        return acc

    acc = lax.fori_loop(0, most, item, jnp.zeros((1, LN), F32))
    for q in range(CAP // LN):
        for t in range(NT):

            @pl.when(jnp.logical_or(ups[t] > q * LN, downs[t] > CAP - (q + 1) * LN))
            def _():
                pay[pl.ds(4 * t + q, 1), :] = jnp.sum(terms[pl.ds(t * CAP + q * LN, LN), :].T, axis=0, keepdims=True)
                if t == NT - 1:
                    e = jnp.sum(extra[pl.ds(q * LN, LN), :].T, axis=0, keepdims=True)
                    pay[pl.ds(12 + q, 1), :] = e * second[0, :, pl.ds(q * LN, LN)]

    pay[pl.ds(CODE, CODE), :] = codes[...]
    pay[pl.ds(2 * CODE, 8), :] = totali[...] + jnp.where(sublanes() == 0, jnp.broadcast_to(acc, (8, LN)), 0.0)


def bands(y0, y1, y2, y3, f1, f2, f3, mask, twice, known, sea, total, second, codes, addrs, tallies, twin, other):
    return pl.pallas_call(
        bands_kernel,
        out_shape=[FIELD] * 6 + [MASK, jax.ShapeDtypeStruct((PAY, LN), F32)],
        in_specs=[VM] * 14 + [ANY] * 2 + [VM] * 2,
        out_specs=[VM] * 8,
        input_output_aliases={0: 0, 1: 1, 2: 2, 4: 3, 5: 4, 6: 5, 7: 6},
        scratch_shapes=[
            pltpu.VMEM((NT * CAP + 8, LN), F32),
            pltpu.VMEM((CAP + 8, LN), F32),
            pltpu.SMEM((NT * CAP,), I32),
            pltpu.SMEM((LN,), F32),
            pltpu.SemaphoreType.DMA((NT + 1,)),
        ],
        compiler_params=params(4),
        cost_estimate=cost(5),
        name="bands",
    )(y0, y1, y2, y3, f1, f2, f3, mask, twice, known, sea, total, second, codes, addrs, tallies, twin, other)


def adjoint_kernel(first, last, unroll, src, state, forcing, mask, out):
    loop(first, last, lambda at: adjoint_row(src, state, out, mask, at), unroll)


def adjoint(first, last, unroll, src, state, forcing, mask):
    return pl.pallas_call(
        functools.partial(adjoint_kernel, first, last, unroll),
        out_shape=FIELD,
        in_specs=[VM] * 4,
        out_specs=VM,
        input_output_aliases={2: 0},
        compiler_params=params(2),
        cost_estimate=cost(2),
        name="adjoint",
    )(src, state, forcing, mask)


SIDE = 28 * LN
LANES, ADDRS, FARS = 0, 12 * LN, 24 * LN


def edge_terms_kernel(y0, y1, y2, f1i, f2i, f3i, mask, twin, other, twin_flat, other_flat,
                      f1, f2, f3, grad, a_ref, b_ref, ca, cb, lines, line_ref, sems):
    def fetches(above, below):
        return [pltpu.make_async_copy(src, dst, sems.at[i]) for i, (src, dst) in enumerate(((above, a_ref), (below, b_ref)))]

    @pl.when(even())
    def _():
        for f in fetches(other_flat, twin_flat):
            f.start()

    @pl.when(jnp.logical_not(even()))
    def _():
        for f in fetches(twin_flat, other_flat):
            f.start()

    slot = lax.broadcasted_iota(I32, (1, LN), 1)
    for side, (x, y) in enumerate(((other, twin), (twin, other))):
        counts = jnp.where(even(), x[pl.ds(CODE + 12, 1), :], y[pl.ds(CODE + 12, 1), :]).astype(I32)
        for t in range(NT):
            n = jnp.sum(jnp.where(slot == (1 - side) * NT + t, counts, 0), axis=1, keepdims=True)
            for q in range(CAP // LN):
                row = pl.ds(CODE + 4 * t + q, 1)
                code = jnp.where(even(), x[row, :], y[row, :]).astype(I32)
                at = slot + q * LN
                live = at >= CAP - n if side == 0 else at < n
                base = side * SIDE + (4 * t + q) * LN
                addr = jnp.where(live, code >> 7, 0)
                lines[0, :, pl.ds(base + LANES, LN)] = jnp.where(live, code & (LN - 1), -1)
                lines[0, :, pl.ds(base + ADDRS, LN)] = addr
                if t == NT - 1:
                    far = addr - (1 if side == 0 else ROWS + H + 1) * COL
                    far = jnp.where(jnp.logical_and(far >= 0, far < COL), far, 0)
                    lines[0, :, pl.ds(side * SIDE + FARS + q * LN, LN)] = far
    prepared = Fetch(lines, line_ref, sems.at[pl.ds(2, 1)])
    prepared.start()
    for q in range(COL // 8):
        for buf in (ca, cb):
            buf[pl.ds(q * 8, 8), :] = jnp.zeros((8, LN), F32)
    loop(3, 12, lambda at: gradient_row(f1, y0, grad, at), 5)
    for f in fetches(twin_flat, other_flat):
        f.wait()
    prepared.wait()
    counts = (CODE + 12) * LN
    most = 0
    for t in range(NT):
        n = jnp.maximum(a_ref[counts + NT + t].astype(I32), b_ref[counts + t].astype(I32))
        most = jnp.maximum(most, (n + t) // (t + 1))

    def item(i, _):
        for t, f in ((2, f3), (1, f2), (0, f1)):
            for u in range(t + 1):
                near = jnp.minimum(i * (t + 1) + u, CAP - 1)
                for ref, slot_at, first, side in ((a_ref, CAP - 1 - near, 0, ca), (b_ref, near, SIDE, cb)):
                    at = t * CAP + slot_at
                    hit = slot == line_ref[first + LANES + at]
                    spot = pl.ds(line_ref[first + ADDRS + at], 1)
                    f[spot, :] = f[spot, :] + jnp.where(hit, ref[at], 0.0)
                    if t == NT - 1:
                        spot = pl.ds(line_ref[first + FARS + slot_at], 1)
                        side[spot, :] = side[spot, :] + jnp.where(hit, ref[12 * LN + slot_at], 0.0)
        return 0

    lax.fori_loop(0, most, item, 0)
    for side, at in ((ca, 1), (cb, ROWS + H + 1)):
        for q in range(COL // 8):
            spot = pl.ds(at * COL + q * 8, 8)
            f2[spot, :] = f2[spot, :] + side[pl.ds(q * 8, 8), :]
    for src, state, dst, reach in ((f3, y2, f2, 2), (f2, y1, f1, 1)):
        rims(reach, lambda at: adjoint_row(src, state, dst, mask, at))


def edge_terms(y0, y1, y2, f1, f2, f3, mask, twin, other):
    return pl.pallas_call(
        edge_terms_kernel,
        out_shape=[FIELD] * 3 + [jax.ShapeDtypeStruct((ROWS * COL, LN), F32)],
        in_specs=[VM] * 9 + [ANY] * 2,
        out_specs=[VM] * 4,
        input_output_aliases={3: 0, 4: 1, 5: 2},
        scratch_shapes=[
            pltpu.SMEM((PAY * LN,), F32),
            pltpu.SMEM((PAY * LN,), F32),
            pltpu.VMEM((COL, LN), F32),
            pltpu.VMEM((COL, LN), F32),
            pltpu.VMEM((1, 1, 2 * SIDE), I32),
            pltpu.SMEM((2 * SIDE,), I32),
            pltpu.SemaphoreType.DMA((3,)),
        ],
        compiler_params=params(4),
        cost_estimate=cost(5),
        name="edge_terms",
    )(y0, y1, y2, f1, f2, f3, mask, twin, other, twin.reshape(-1), other.reshape(-1))


def finish_kernel(scale, y0, f1, gradi, x, y, grad, out, misfit, staged, sems):
    misfit[...] = jnp.sum(x[...] + y[...], keepdims=True) * scale
    rims(0, lambda at: gradient_row(f1, y0, grad, at))

    def copy(c):
        return pltpu.make_async_copy(staged.at[c], out.at[:, :, pl.ds(c * LN, LN)], sems.at[c])

    for c in range(CT):
        for k in range(LV):
            for half in range(2):
                v = grad[pl.ds(half * 8 * COL + c * LV + k, 8, stride=COL), :]
                staged[c, k, pl.ds(half * 8, 8), :] = v
        copy(c).start()
    for c in range(CT):
        copy(c).wait()


def finish(y0, f1, grad, x, y, scale):
    return pl.pallas_call(
        functools.partial(finish_kernel, scale),
        out_shape=[
            jax.ShapeDtypeStruct((ROWS * COL, LN), F32),
            jax.ShapeDtypeStruct((LV, ROWS, CT * LN), F32),
            jax.ShapeDtypeStruct((1, 1), F32),
        ],
        in_specs=[VM] * 5,
        out_specs=[VM, ANY, VM],
        input_output_aliases={2: 0},
        scratch_shapes=[pltpu.VMEM((CT, LV, ROWS, LN), F32), pltpu.SemaphoreType.DMA((CT,))],
        compiler_params=params(8),
        cost_estimate=cost(4),
        name="finish",
    )(y0, f1, grad, x, y)[1:]


def add_kernel(first, pay, twin, out):
    out[...] = pay[pl.ds(first, 8), :] + twin[pl.ds(first, 8), :]


def add(first, a, b):
    return pl.pallas_call(
        functools.partial(add_kernel, first),
        out_shape=jax.ShapeDtypeStruct((8, LN), F32),
        in_specs=[VM, VM],
        out_specs=VM,
        compiler_params=params(1),
        cost_estimate=cost(0.1),
        name="add",
    )(a, b)


def sum_along(pay, twin, stages, held):
    size = lax.axis_size("along")
    steps = [1 << i for i in range(1, size.bit_length() - 1)]
    x = add(2 * CODE, pay, twin)
    other = jnp.zeros_like(x)
    if size & (size - 1):
        x, steps = lax.psum(0.5 * x, "along"), []
    for i in range(max(len(steps), len(stages))):
        if i < len(steps):
            if i > 0:
                x = add(0, x, other)
            x, held = lax.optimization_barrier((x, held))
            other = lax.ppermute(x, "along", [(p, p ^ steps[i]) for p in range(size)])
        if i < len(stages):
            held = stages[i](*held)
    return x, other, held


def local(basic_state, land_sea, obs_cells, obs_count, obs_value):
    size = lax.axis_size("along")
    twins = [(i, i ^ 1) for i in range(size)]
    others = [(i, i - 1 if i % 2 == 0 else i + 1) for i in range(1, size - 1)]
    cells = obs_cells.transpose(1, 0, 2)
    value = obs_value.transpose(1, 0, 2)
    staged, twin, other, mask = edges(basic_state, land_sea)
    other = lax.ppermute(other, "along", others)
    twin = lax.ppermute(twin, "along", twins)
    addrs, sval, lane, spots, second, tallies, codes = order(cells, obs_count, value)
    y0, y1, y2, y3, f1, f2, f3, twice, known, sea, total = interior(staged, mask, lane, sval, addrs, spots, tallies)
    y0, y1, y2, f1, f2, f3, mask, pay = bands(
        y0, y1, y2, y3, f1, f2, f3, mask, twice, known, sea, total, second, codes, addrs, tallies, twin, other
    )
    other = lax.ppermute(pay, "along", others)
    twin = lax.ppermute(pay, "along", twins)
    stages = (
        lambda a, b, c: (a, adjoint(1, 14, 7, c, y2, b, mask), c),
        lambda a, b, c: (adjoint(2, 13, 6, b, y1, a, mask), b, c),
        lambda a, b, c: edge_terms(y0, y1, y2, a, b, c, mask, twin, other),
    )
    x, y, held = sum_along(pay, twin, stages, (f1, f2, f3))
    scale = 1.0 / (2.0 * size * obs_cells.shape[1] * obs_cells.shape[2])
    gradient, misfit = finish(y0, held[0], held[3], x, y, scale)
    misfit = misfit.reshape(1)
    return gradient, misfit


def solution(mesh):
    in_specs = (
        P(None, ("ens", "along"), None),
        P(("ens", "along"), None),
        P(("ens", "along"), None, None),
        P(("ens", "along"), None),
        P(("ens", "along"), None, None),
    )
    out_specs = (P(None, ("ens", "along"), None), P("ens"))
    return jax.shard_map(local, mesh=mesh, in_specs=in_specs, out_specs=out_specs, check_vma=False)
```

```python
import functools

import jax
import jax.numpy as jnp
from jax import lax
from jax.experimental import pallas as pl
from jax.experimental.pallas import tpu as pltpu
from jax.sharding import PartitionSpec as P

F32 = jnp.float32
I32 = jnp.int32
ROWS, CT, LV, LN = 16, 8, 40, 128
H = 3
RX = ROWS + 2 * H
COL = CT * LV
EDGE = H * COL + H * CT
CAP = 512
NT = 3
PAY = 40
CODE = 16

VM = pl.BlockSpec(memory_space=pltpu.VMEM)
SM = pl.BlockSpec(memory_space=pltpu.SMEM)
HBM = pl.BlockSpec(memory_space=pltpu.MemorySpace.HBM)
ANY = pl.BlockSpec(memory_space=pl.ANY)
FIELD = jax.ShapeDtypeStruct((RX * COL, LN), F32)
MASK = jax.ShapeDtypeStruct((RX * CT, LN), F32)


def params(mib):
    return pltpu.CompilerParams(vmem_limit_bytes=mib << 20)


def cost(us):
    return pl.CostEstimate(flops=0, bytes_accessed=int(us * 3.0e6), transcendentals=0)


def lanes():
    return lax.broadcasted_iota(I32, (8, LN), 1)


def sublanes():
    return lax.broadcasted_iota(I32, (8, LN), 0)


def stencil_row(src, at, emit):
    lane, sub = lanes(), sublanes()
    first, last = lane == 0, lane == LN - 1
    low, high = sub == 0, sub == 7
    base = pl.multiple_of(at * COL, COL)
    for k in range(LV // 8):
        offs = [base + c * LV + k * 8 for c in range(CT)]
        mids = [src[pl.ds(pl.multiple_of(o, 8), 8), :] for o in offs]
        fwd = [pltpu.roll(v, 1, 1) for v in mids]
        bwd = [pltpu.roll(v, LN - 1, 1) for v in mids]
        for c in range(CT):
            v, o = mids[c], offs[c]
            west = jnp.where(first, fwd[c - 1] if c > 0 else 0.0, fwd[c])
            east = jnp.where(last, bwd[c + 1] if c < CT - 1 else 0.0, bwd[c])
            north = src[pl.ds(pl.multiple_of(o - COL, 8), 8), :]
            south = src[pl.ds(pl.multiple_of(o + COL, 8), 8), :]
            if k > 0:
                down = src[pl.ds(o - 1, 8), :]
            else:
                down = jnp.where(low, v, pltpu.roll(v, 1, 0))
            if k < LV // 8 - 1:
                up = src[pl.ds(o + 1, 8), :]
            else:
                up = jnp.where(high, v, pltpu.roll(v, 7, 0))
            s = ((north + south) + (west + east)) + 0.2 * (down + up)
            emit(c, k, v, s, o)


class Fetch:
    def __init__(self, src, dst, sems):
        count, size = src.shape[0], src.shape[2]
        self.parts = [pltpu.make_async_copy(src.at[t, 0], dst.at[pl.ds(t * size, size)], sems.at[t]) for t in range(count)]

    def start(self):
        for part in self.parts:
            part.start()

    def wait(self):
        for part in self.parts:
            part.wait()


def tally_of(ref):
    return [[ref[side * NT + t].astype(I32) for t in range(NT)] for side in range(2)]


def mask_row(mask, at, c):
    return mask[pl.ds(at * CT + c, 8, stride=0), :]


def forward_row(src, dst, mask, at, blank=None):
    ms = [mask_row(mask, at, c) for c in range(CT)]

    def emit(c, k, v, s, o):
        dst[pl.ds(pl.multiple_of(o, 8), 8), :] = ms[c] * (s + v * (0.6 - v * v))
        if blank is not None:
            blank[pl.ds(pl.multiple_of(o, 8), 8), :] = jnp.zeros((8, LN), F32)

    stencil_row(src, at, emit)


def adjoint_row(src, state, forcing, mask, at):
    ms = [mask_row(mask, at, c) for c in range(CT)]

    def emit(c, k, g, s, o):
        spot = pl.ds(pl.multiple_of(o, 8), 8)
        y = state[spot, :]
        forcing[spot, :] = ms[c] * ((s + g * (0.6 - 3.0 * (y * y))) + forcing[spot, :])

    stencil_row(src, at, emit)


def gradient_row(src, state, out, at):
    def emit(c, k, g, s, o):
        y = state[pl.ds(pl.multiple_of(o, 8), 8), :]
        out[pl.ds(pl.multiple_of(o - H * COL, 8), 8), :] = 0.2 * (s + g * (0.6 - 3.0 * (y * y)))

    stencil_row(src, at, emit)


def loop(first, last, body, unroll):
    def some(i, _):
        for u in range(unroll):
            body(first + H + i * unroll + u)
        return 0

    lax.fori_loop(0, (last + 1 - first) // unroll, some, 0)


def rims(reach, body):
    for at in [*range(-reach, 3 - reach), *range(ROWS - 3 + reach, ROWS + reach)]:
        body(at + H)


def even():
    return lax.rem(lax.axis_index("along"), 2) == 0


def edges_kernel(basic, land_at, staged, twin, other, mask, land, sems):
    def copy(c):
        return pltpu.make_async_copy(basic.at[:, :, pl.ds(c * LN, LN)], staged.at[c], sems.at[c])

    sea = pltpu.make_async_copy(land_at, land, sems.at[CT])
    sea.start()
    for c in range(CT):
        copy(c).start()
    sea.wait()
    for c in range(CT):
        mask[pl.ds(H * CT + c, ROWS, stride=CT), :] = 0.2 * land[:, pl.ds(c * LN, LN)].astype(F32)
    lower = jnp.where(even(), ROWS - H, 0)
    for c in range(CT):
        copy(c).wait()
        flat = staged.at[c].reshape(LV * ROWS, LN)
        for out, first in ((twin, lower), (other, ROWS - H - lower)):
            for j in range(H):
                r = first + j
                half = 2.5 * mask_row(mask, r + H, c)
                for k in range(LV // 8):
                    v = flat[pl.ds(k * 8 * ROWS + r, 8, stride=ROWS), :]
                    out[pl.ds((j * CT + c) * LV + k * 8, 8), :] = half * v
                out[pl.ds(H * COL + j * CT + c, 1), :] = mask[pl.ds((r + H) * CT + c, 1), :]


def edges(basic, land):
    return pl.pallas_call(
        edges_kernel,
        out_shape=[
            jax.ShapeDtypeStruct((CT, LV, ROWS, LN), F32),
            jax.ShapeDtypeStruct((EDGE, LN), F32),
            jax.ShapeDtypeStruct((EDGE, LN), F32),
            MASK,
        ],
        in_specs=[HBM, HBM],
        out_specs=[VM] * 4,
        scratch_shapes=[pltpu.VMEM((ROWS, CT * LN), I32), pltpu.SemaphoreType.DMA((CT + 1,))],
        compiler_params=params(4),
        cost_estimate=cost(2),
        name="edges",
    )(pltpu.with_memory_space_constraint(basic, pltpu.HBM), pltpu.with_memory_space_constraint(land, pltpu.HBM))


def order_kernel(cells_at, count_at, value_at, addr, sval, lane, spot, second, tallies, codes, cells, count, value, sems):
    fetches = [
        pltpu.make_async_copy(src, dst, sems.at[i])
        for i, (src, dst) in enumerate(((cells_at, cells), (count_at, count), (value_at, value)))
    ]
    for f in fetches:
        f.start()
    for f in fetches:
        f.wait()
    slot = lax.broadcasted_iota(I32, (1, CAP), 1)
    ups, downs = [], []
    for t in range(NT):
        row = (cells[t] >> 10) & (ROWS - 1)
        alive = slot < count[0, t]
        ups.append(jnp.logical_and(alive, row <= t))
        downs.append(jnp.logical_and(alive, row >= ROWS - 1 - t))
    one = [jnp.where(f, 1.0, 0.0) for f in ups + downs]
    flags = jnp.concatenate(one + [jnp.zeros((10, CAP), F32)], axis=0).astype(jnp.bfloat16)
    tri = jnp.where(
        lax.broadcasted_iota(I32, (CAP, CAP), 0) < lax.broadcasted_iota(I32, (CAP, CAP), 1), 1.0, 0.0
    ).astype(jnp.bfloat16)
    before = jnp.dot(flags, tri, preferred_element_type=F32)
    codes[...] = jnp.zeros((CODE, LN), F32)
    sub = lax.broadcasted_iota(I32, (CAP, CAP), 0)
    first = lax.broadcasted_iota(I32, (1, LN), 1)
    tally = jnp.zeros((1, LN), F32)
    for t in range(NT):
        up, down = ups[t], downs[t]
        pu, pd = before[t : t + 1], before[NT + t : NT + t + 1]
        nu = jnp.sum(one[t], axis=1, keepdims=True)
        nd = jnp.sum(one[NT + t], axis=1, keepdims=True)
        tally = tally + jnp.where(first == t, nu, 0.0) + jnp.where(first == NT + t, nd, 0.0)
        rank = jnp.where(up, pu, jnp.where(down, CAP - nd + pd, nu + slot.astype(F32) - pu - pd)).astype(I32)
        place = jnp.where(sub == rank, 1.0, 0.0).astype(jnp.bfloat16)
        cell, v = cells[t], value[t]
        v1 = v.astype(jnp.bfloat16).astype(F32)
        v2 = (v - v1).astype(jnp.bfloat16).astype(F32)
        parts = [
            (cell >> 16).astype(F32),
            ((cell >> 8) & 255).astype(F32),
            (cell & 255).astype(F32),
            v1,
            v2,
            v - v1 - v2,
            jnp.where(slot < count[0, t], 1.0, 0.0),
        ]
        left = jnp.concatenate(parts + [jnp.zeros((9, CAP), F32)], axis=0).astype(jnp.bfloat16)
        out = lax.dot_general(left, place, (((1,), (1,)), ((), ())), preferred_element_type=F32)
        cell = (out[0:1] * 65536.0 + out[1:2] * 256.0 + out[2:3]).astype(I32)
        row, level, where = (cell >> 10) & (ROWS - 1), cell >> 14, (cell >> 7) & (ROWS * CT - 1)
        alive = out[6:7] > 0.5
        own = (where + H * CT) * LV + level
        addr[t] = own
        sval[t] = out[3:4] + out[4:5] + out[5:6]
        lane[t] = jnp.where(alive, (cell & (LN - 1)).astype(F32), -1.0)
        if t == NT - 1:
            spot[0] = where + H * CT
            second[0] = jnp.where(jnp.logical_or(row == 1, row == ROWS - 2), -3.0, 0.0)
        far = jnp.where(row < ROWS // 2, own + ROWS * COL, own - ROWS * COL)
        near = jnp.logical_or(row <= t, row >= ROWS - 1 - t)
        code = jnp.where(near, far * LN + (cell & (LN - 1)), 0).astype(F32)
        for q in range(CAP // LN):
            codes[pl.ds(4 * t + q, 1), :] = code[:, q * LN : (q + 1) * LN]
    codes[pl.ds(12, 1), :] = tally
    tallies[0] = tally


def order(cells, count, value):
    ints, floats = jax.ShapeDtypeStruct((NT, 1, CAP), I32), jax.ShapeDtypeStruct((NT, 1, CAP), F32)
    return pl.pallas_call(
        order_kernel,
        out_shape=[ints, floats, floats, jax.ShapeDtypeStruct((1, 1, CAP), I32), jax.ShapeDtypeStruct((1, 1, CAP), F32), jax.ShapeDtypeStruct((1, 1, LN), F32), jax.ShapeDtypeStruct((CODE, LN), F32)],
        in_specs=[HBM] * 3,
        out_specs=[VM] * 7,
        scratch_shapes=[
            pltpu.VMEM((NT, 1, CAP), I32),
            pltpu.SMEM((1, NT), I32),
            pltpu.VMEM((NT, 1, CAP), F32),
            pltpu.SemaphoreType.DMA((3,)),
        ],
        compiler_params=params(6),
        cost_estimate=cost(2),
        name="order",
    )(*(pltpu.with_memory_space_constraint(x, pltpu.HBM) for x in (cells, count, value)))


def upright(line):
    return jnp.broadcast_to(line, (LN, LN)).T


def interior_kernel(staged, mask, lane, sval, addrs, spots, tallies, y0, y1, y2, y3, f1, f2, f3, twice, known, sea, total,
                    g1, g2, g3, terms, at_ref, spot_ref, n_ref, sems):
    fetches = [Fetch(addrs, at_ref, sems), Fetch(spots, spot_ref, sems.at[pl.ds(NT, 1)]), Fetch(tallies, n_ref, sems.at[pl.ds(NT + 1, 1)])]
    for fetch in fetches:
        fetch.start()
    for c in range(CT):
        flat = staged.at[c].reshape(LV * ROWS, LN)

        def turn(i, _):
            for u in range(4):
                r = i * 4 + u
                half = 2.5 * mask_row(mask, r + H, c)
                for k in range(LV // 8):
                    v = flat[pl.ds(k * 8 * ROWS + r, 8, stride=ROWS), :]
                    y0[pl.ds(pl.multiple_of((r + H) * COL + c * LV + k * 8, 8), 8), :] = half * v
            return 0

        lax.fori_loop(0, ROWS // 4, turn, 0)

    zero = jnp.zeros((8, LN), F32)
    for at in (H - 2, ROWS + H + 1):
        for j in range(COL // 8):
            y2[pl.ds(at * COL + j * 8, 8), :] = zero
    for t, f in enumerate((f1, f2, f3)):
        for at in [*range(H + t + 1), *range(ROWS + H - t - 1, RX)]:
            for j in range(COL // 8):
                f[pl.ds(at * COL + j * 8, 8), :] = zero
    loop(1, 14, lambda at: forward_row(y0, y1, mask, at, f1), 7)
    loop(2, 13, lambda at: forward_row(y1, y2, mask, at, f2), 6)
    loop(3, 12, lambda at: forward_row(y2, y3, mask, at, f3), 5)
    for fetch in fetches:
        fetch.wait()

    def gather(i, _):
        for u in range(8):
            s = i * 8 + u
            here = pl.ds(s, 1)
            g1[here, :] = y1[pl.ds(at_ref[s], 1), :]
            g2[here, :] = y2[pl.ds(at_ref[CAP + s], 1), :]
            g3[here, :] = y3[pl.ds(at_ref[2 * CAP + s], 1), :]
            sea[here, :] = mask[pl.ds(spot_ref[s], 1), :]
        return 0

    lax.fori_loop(0, CAP // 8, gather, 0)
    ups, downs = tally_of(n_ref)
    ids = lax.broadcasted_iota(I32, (LN, LN), 1).astype(F32)
    slot = lax.broadcasted_iota(I32, (LN, LN), 0)
    acc = zero
    for t, g in enumerate((g1, g2, g3)):
        for q in range(CAP // LN):
            part = pl.ds(q * LN, LN)
            hit = upright(lane[t, :, part]) == ids
            rows = pl.ds(t * CAP + q * LN, LN)
            two, have = jnp.where(hit, 2.0, 0.0), jnp.where(hit, upright(sval[t, :, part]), 0.0)
            twice[rows, :] = two
            known[rows, :] = have
            early = jnp.logical_and(slot + q * LN >= ups[t], slot + q * LN < CAP - downs[t])
            d = jnp.where(early, g[part, :] * two - have, 0.0)
            acc = acc + jnp.sum((d * d).reshape(LN // 8, 8, LN), axis=0)
            terms[rows, :] = d * (5.0 * sea[part, :]) if t == NT - 1 else 5.0 * d
    total[...] = acc

    def scatter(i, _):
        for u in range(8):
            s = i * 8 + u
            for t, f in enumerate((f1, f2, f3)):
                spot = pl.ds(at_ref[t * CAP + s], 1)
                f[spot, :] = f[spot, :] + terms[pl.ds(t * CAP + s, 1), :]
        return 0

    lax.fori_loop(0, CAP // 8, scatter, 0)


def interior(staged, mask, lane, sval, addrs, spots, tallies):
    rows = jax.ShapeDtypeStruct((NT * CAP, LN), F32)
    few = pltpu.VMEM((CAP, LN), F32)
    return pl.pallas_call(
        interior_kernel,
        out_shape=[FIELD] * 7 + [rows, rows, jax.ShapeDtypeStruct((CAP, LN), F32), jax.ShapeDtypeStruct((8, LN), F32)],
        in_specs=[VM] * 4 + [ANY] * 3,
        out_specs=[VM] * 11,
        scratch_shapes=[
            few,
            few,
            few,
            pltpu.VMEM((NT * CAP, LN), F32),
            pltpu.SMEM((NT * CAP,), I32),
            pltpu.SMEM((CAP,), I32),
            pltpu.SMEM((LN,), F32),
            pltpu.SemaphoreType.DMA((NT + 2,)),
        ],
        compiler_params=params(6),
        cost_estimate=cost(11),
        name="interior",
    )(staged, mask, lane, sval, addrs, spots, tallies)


def bands_kernel(y0i, y1i, y2i, y3, f1i, f2i, f3i, maski, twice, known, sea, totali, second, codes, addrs, tallies, twin, other,
                 y0, y1, y2, f1, f2, f3, mask, pay, terms, extra, at_ref, n_ref, sems):
    fetches = [Fetch(addrs, at_ref, sems), Fetch(tallies, n_ref, sems.at[pl.ds(NT, 1)])]
    for fetch in fetches:
        fetch.start()
    lower = jnp.where(even(), ROWS + H, 0)
    for halo, first in ((twin, lower), (other, ROWS + H - lower)):
        base = pl.multiple_of(first * COL, 8)
        for q in range(H * COL // 8):
            y0[pl.ds(base + q * 8, 8), :] = halo[pl.ds(q * 8, 8), :]
        base = pl.multiple_of(first * CT, 8)
        for j in range(H):
            mask[pl.ds(base + j * CT, CT), :] = halo[pl.ds(H * COL + j * CT, CT), :]
    for src, dst, reach in ((y0, y1, 2), (y1, y2, 1), (y2, y3, 0)):
        rims(reach, lambda at: forward_row(src, dst, mask, at))
    for fetch in fetches:
        fetch.wait()
    ups, downs = tally_of(n_ref)
    most = 0
    for t in range(NT):
        most = jnp.maximum(most, (jnp.maximum(ups[t], downs[t]) + t) // (t + 1))

    def item(i, acc):
        for t, (y, f) in ((2, (y3, f3)), (1, (y2, f2)), (0, (y1, f1))):
            for u in range(t + 1):
                j = i * (t + 1) + u
                near = jnp.minimum(j, CAP - 1)
                for n, slot in ((ups[t], near), (downs[t], CAP - 1 - near)):
                    ok = j < n
                    row = t * CAP + slot
                    spot = pl.ds(at_ref[row], 1)
                    d = jnp.where(ok, y[spot, :] * twice[pl.ds(row, 1), :] - known[pl.ds(row, 1), :], 0.0)
                    acc = acc + d * d
                    if t == NT - 1:
                        d = d * (5.0 * sea[pl.ds(slot, 1), :])
                        z = y2[spot, :]
                        extra[pl.ds(jnp.where(ok, slot, CAP), 1), :] = (z * z) * d
                    else:
                        d = 5.0 * d
                    f[spot, :] = f[spot, :] + d
                    terms[pl.ds(jnp.where(ok, row, NT * CAP), 1), :] = d
        return acc

    acc = lax.fori_loop(0, most, item, jnp.zeros((1, LN), F32))
    for q in range(CAP // LN):
        for t in range(NT):

            @pl.when(jnp.logical_or(ups[t] > q * LN, downs[t] > CAP - (q + 1) * LN))
            def _():
                pay[pl.ds(4 * t + q, 1), :] = jnp.sum(terms[pl.ds(t * CAP + q * LN, LN), :].T, axis=0, keepdims=True)
                if t == NT - 1:
                    e = jnp.sum(extra[pl.ds(q * LN, LN), :].T, axis=0, keepdims=True)
                    pay[pl.ds(12 + q, 1), :] = e * second[0, :, pl.ds(q * LN, LN)]

    pay[pl.ds(CODE, CODE), :] = codes[...]
    pay[pl.ds(2 * CODE, 8), :] = totali[...] + jnp.where(sublanes() == 0, jnp.broadcast_to(acc, (8, LN)), 0.0)


def bands(y0, y1, y2, y3, f1, f2, f3, mask, twice, known, sea, total, second, codes, addrs, tallies, twin, other):
    return pl.pallas_call(
        bands_kernel,
        out_shape=[FIELD] * 6 + [MASK, jax.ShapeDtypeStruct((PAY, LN), F32)],
        in_specs=[VM] * 14 + [ANY] * 2 + [VM] * 2,
        out_specs=[VM] * 8,
        input_output_aliases={0: 0, 1: 1, 2: 2, 4: 3, 5: 4, 6: 5, 7: 6},
        scratch_shapes=[
            pltpu.VMEM((NT * CAP + 8, LN), F32),
            pltpu.VMEM((CAP + 8, LN), F32),
            pltpu.SMEM((NT * CAP,), I32),
            pltpu.SMEM((LN,), F32),
            pltpu.SemaphoreType.DMA((NT + 1,)),
        ],
        compiler_params=params(4),
        cost_estimate=cost(5),
        name="bands",
    )(y0, y1, y2, y3, f1, f2, f3, mask, twice, known, sea, total, second, codes, addrs, tallies, twin, other)


def adjoint_kernel(first, last, unroll, src, state, forcing, mask, out):
    loop(first, last, lambda at: adjoint_row(src, state, out, mask, at), unroll)


def adjoint(first, last, unroll, src, state, forcing, mask):
    return pl.pallas_call(
        functools.partial(adjoint_kernel, first, last, unroll),
        out_shape=FIELD,
        in_specs=[VM] * 4,
        out_specs=VM,
        input_output_aliases={2: 0},
        compiler_params=params(2),
        cost_estimate=cost(2),
        name="adjoint",
    )(src, state, forcing, mask)


SIDE = 28 * LN
LANES, ADDRS, FARS = 0, 12 * LN, 24 * LN


def edge_terms_kernel(y0, y1, y2, f1i, f2i, f3i, mask, twin, other, twin_flat, other_flat,
                      f1, f2, f3, grad, a_ref, b_ref, ca, cb, lines, line_ref, sems):
    def fetches(above, below):
        return [pltpu.make_async_copy(src, dst, sems.at[i]) for i, (src, dst) in enumerate(((above, a_ref), (below, b_ref)))]

    @pl.when(even())
    def _():
        for f in fetches(other_flat, twin_flat):
            f.start()

    @pl.when(jnp.logical_not(even()))
    def _():
        for f in fetches(twin_flat, other_flat):
            f.start()

    slot = lax.broadcasted_iota(I32, (1, LN), 1)
    for side, (x, y) in enumerate(((other, twin), (twin, other))):
        counts = jnp.where(even(), x[pl.ds(CODE + 12, 1), :], y[pl.ds(CODE + 12, 1), :]).astype(I32)
        for t in range(NT):
            n = jnp.sum(jnp.where(slot == (1 - side) * NT + t, counts, 0), axis=1, keepdims=True)
            for q in range(CAP // LN):
                row = pl.ds(CODE + 4 * t + q, 1)
                code = jnp.where(even(), x[row, :], y[row, :]).astype(I32)
                at = slot + q * LN
                live = at >= CAP - n if side == 0 else at < n
                base = side * SIDE + (4 * t + q) * LN
                addr = jnp.where(live, code >> 7, 0)
                lines[0, :, pl.ds(base + LANES, LN)] = jnp.where(live, code & (LN - 1), -1)
                lines[0, :, pl.ds(base + ADDRS, LN)] = addr
                if t == NT - 1:
                    far = addr - (1 if side == 0 else ROWS + H + 1) * COL
                    far = jnp.where(jnp.logical_and(far >= 0, far < COL), far, 0)
                    lines[0, :, pl.ds(side * SIDE + FARS + q * LN, LN)] = far
    prepared = Fetch(lines, line_ref, sems.at[pl.ds(2, 1)])
    prepared.start()
    for q in range(COL // 8):
        for buf in (ca, cb):
            buf[pl.ds(q * 8, 8), :] = jnp.zeros((8, LN), F32)
    loop(3, 12, lambda at: gradient_row(f1, y0, grad, at), 5)
    for f in fetches(twin_flat, other_flat):
        f.wait()
    prepared.wait()
    counts = (CODE + 12) * LN
    most = 0
    for t in range(NT):
        n = jnp.maximum(a_ref[counts + NT + t].astype(I32), b_ref[counts + t].astype(I32))
        most = jnp.maximum(most, (n + t) // (t + 1))

    def item(i, _):
        for t, f in ((2, f3), (1, f2), (0, f1)):
            for u in range(t + 1):
                near = jnp.minimum(i * (t + 1) + u, CAP - 1)
                for ref, slot_at, first, side in ((a_ref, CAP - 1 - near, 0, ca), (b_ref, near, SIDE, cb)):
                    at = t * CAP + slot_at
                    hit = slot == line_ref[first + LANES + at]
                    spot = pl.ds(line_ref[first + ADDRS + at], 1)
                    f[spot, :] = f[spot, :] + jnp.where(hit, ref[at], 0.0)
                    if t == NT - 1:
                        spot = pl.ds(line_ref[first + FARS + slot_at], 1)
                        side[spot, :] = side[spot, :] + jnp.where(hit, ref[12 * LN + slot_at], 0.0)
        return 0

    lax.fori_loop(0, most, item, 0)
    for side, at in ((ca, 1), (cb, ROWS + H + 1)):
        for q in range(COL // 8):
            spot = pl.ds(at * COL + q * 8, 8)
            f2[spot, :] = f2[spot, :] + side[pl.ds(q * 8, 8), :]
    for src, state, dst, reach in ((f3, y2, f2, 2), (f2, y1, f1, 1)):
        rims(reach, lambda at: adjoint_row(src, state, dst, mask, at))


def edge_terms(y0, y1, y2, f1, f2, f3, mask, twin, other):
    return pl.pallas_call(
        edge_terms_kernel,
        out_shape=[FIELD] * 3 + [jax.ShapeDtypeStruct((ROWS * COL, LN), F32)],
        in_specs=[VM] * 9 + [ANY] * 2,
        out_specs=[VM] * 4,
        input_output_aliases={3: 0, 4: 1, 5: 2},
        scratch_shapes=[
            pltpu.SMEM((PAY * LN,), F32),
            pltpu.SMEM((PAY * LN,), F32),
            pltpu.VMEM((COL, LN), F32),
            pltpu.VMEM((COL, LN), F32),
            pltpu.VMEM((1, 1, 2 * SIDE), I32),
            pltpu.SMEM((2 * SIDE,), I32),
            pltpu.SemaphoreType.DMA((3,)),
        ],
        compiler_params=params(4),
        cost_estimate=cost(5),
        name="edge_terms",
    )(y0, y1, y2, f1, f2, f3, mask, twin, other, twin.reshape(-1), other.reshape(-1))


def finish_kernel(y0, f1, gradi, grad, out, staged, sems):
    rims(0, lambda at: gradient_row(f1, y0, grad, at))

    def copy(c):
        return pltpu.make_async_copy(staged.at[c], out.at[:, :, pl.ds(c * LN, LN)], sems.at[c])

    for c in range(CT):

        def turn(k, _):
            for half in range(2):
                v = grad[pl.ds(half * 8 * COL + c * LV + k, 8, stride=COL), :]
                staged[c, k, pl.ds(half * 8, 8), :] = v
            return 0

        lax.fori_loop(0, LV, turn, 0, unroll=8)
        copy(c).start()
    for c in range(CT):
        copy(c).wait()


def finish(y0, f1, grad):
    return pl.pallas_call(
        finish_kernel,
        out_shape=[jax.ShapeDtypeStruct((ROWS * COL, LN), F32), jax.ShapeDtypeStruct((LV, ROWS, CT * LN), F32)],
        in_specs=[VM] * 3,
        out_specs=[VM, ANY],
        input_output_aliases={2: 0},
        scratch_shapes=[pltpu.VMEM((CT, LV, ROWS, LN), F32), pltpu.SemaphoreType.DMA((CT,))],
        compiler_params=params(8),
        cost_estimate=cost(4),
        name="finish",
    )(y0, f1, grad)


def total_kernel(scale, x, y, out):
    out[...] = jnp.sum(x[...] + y[...], keepdims=True) * scale


def total(x, y, scale):
    return pl.pallas_call(
        functools.partial(total_kernel, scale),
        out_shape=jax.ShapeDtypeStruct((1, 1), F32),
        in_specs=[VM, VM],
        out_specs=VM,
        compiler_params=params(1),
        cost_estimate=cost(0.1),
        name="total",
    )(x, y).reshape(1)


def add_kernel(first, pay, twin, out):
    out[...] = pay[pl.ds(first, 8), :] + twin[pl.ds(first, 8), :]


def add(first, a, b):
    return pl.pallas_call(
        functools.partial(add_kernel, first),
        out_shape=jax.ShapeDtypeStruct((8, LN), F32),
        in_specs=[VM, VM],
        out_specs=VM,
        compiler_params=params(1),
        cost_estimate=cost(0.1),
        name="add",
    )(a, b)


def sum_along(pay, twin, stages, held):
    size = lax.axis_size("along")
    steps = [1 << i for i in range(1, size.bit_length() - 1)]
    x = add(2 * CODE, pay, twin)
    other = jnp.zeros_like(x)
    if size & (size - 1):
        x, steps = lax.psum(0.5 * x, "along"), []
    for i in range(max(len(steps), len(stages))):
        if i < len(steps):
            if i > 0:
                x = add(0, x, other)
            x, held = lax.optimization_barrier((x, held))
            other = lax.ppermute(x, "along", [(p, p ^ steps[i]) for p in range(size)])
        if i < len(stages):
            held = stages[i](*held)
    return x, other, held


def local(basic_state, land_sea, obs_cells, obs_count, obs_value):
    size = lax.axis_size("along")
    twins = [(i, i ^ 1) for i in range(size)]
    others = [(i, i - 1 if i % 2 == 0 else i + 1) for i in range(1, size - 1)]
    cells = obs_cells.transpose(1, 0, 2)
    value = obs_value.transpose(1, 0, 2)
    staged, twin, other, mask = edges(basic_state, land_sea)
    other = lax.ppermute(other, "along", others)
    twin = lax.ppermute(twin, "along", twins)
    addrs, sval, lane, spots, second, tallies, codes = order(cells, obs_count, value)
    y0, y1, y2, y3, f1, f2, f3, twice, known, sea, squares = interior(staged, mask, lane, sval, addrs, spots, tallies)
    y0, y1, y2, f1, f2, f3, mask, pay = bands(
        y0, y1, y2, y3, f1, f2, f3, mask, twice, known, sea, squares, second, codes, addrs, tallies, twin, other
    )
    other = lax.ppermute(pay, "along", others)
    twin = lax.ppermute(pay, "along", twins)
    def inner(a, b, c):
        b = adjoint(1, 14, 7, c, y2, b, mask)
        return adjoint(2, 13, 6, b, y1, a, mask), b, c

    stages = (
        inner,
        lambda a, b, c: edge_terms(y0, y1, y2, a, b, c, mask, twin, other),
        lambda a, b, c, g: finish(y0, a, g),
    )
    x, y, held = sum_along(pay, twin, stages, (f1, f2, f3))
    gradient = held[1]
    misfit = total(x, y, 1.0 / (2.0 * size * obs_cells.shape[1] * obs_cells.shape[2]))
    return gradient, misfit


def solution(mesh):
    in_specs = (
        P(None, ("ens", "along"), None),
        P(("ens", "along"), None),
        P(("ens", "along"), None, None),
        P(("ens", "along"), None),
        P(("ens", "along"), None, None),
    )
    out_specs = (P(None, ("ens", "along"), None), P("ens"))
    return jax.shard_map(local, mesh=mesh, in_specs=in_specs, out_specs=out_specs, check_vma=False)
```

```python
import functools

import jax
import jax.numpy as jnp
from jax import lax
from jax.experimental import pallas as pl
from jax.experimental.pallas import tpu as pltpu
from jax.sharding import PartitionSpec as P

F32 = jnp.float32
I32 = jnp.int32
ROWS, CT, LV, LN = 16, 8, 40, 128
H = 3
RX = ROWS + 2 * H
COL = CT * LV
EDGE = H * COL + H * CT
CAP = 512
NT = 3
PAY = 40
CODE = 16

VM = pl.BlockSpec(memory_space=pltpu.VMEM)
SM = pl.BlockSpec(memory_space=pltpu.SMEM)
HBM = pl.BlockSpec(memory_space=pltpu.MemorySpace.HBM)
ANY = pl.BlockSpec(memory_space=pl.ANY)
FIELD = jax.ShapeDtypeStruct((RX * COL, LN), F32)
MASK = jax.ShapeDtypeStruct((RX * CT, LN), F32)


def params(mib):
    return pltpu.CompilerParams(vmem_limit_bytes=mib << 20)


def cost(us):
    return pl.CostEstimate(flops=0, bytes_accessed=int(us * 3.0e6), transcendentals=0)


def lanes():
    return lax.broadcasted_iota(I32, (8, LN), 1)


def sublanes():
    return lax.broadcasted_iota(I32, (8, LN), 0)


def stencil_row(src, at, emit):
    lane, sub = lanes(), sublanes()
    first, last = lane == 0, lane == LN - 1
    low, high = sub == 0, sub == 7
    base = pl.multiple_of(at * COL, COL)
    for k in range(LV // 8):
        offs = [base + c * LV + k * 8 for c in range(CT)]
        mids = [src[pl.ds(pl.multiple_of(o, 8), 8), :] for o in offs]
        fwd = [pltpu.roll(v, 1, 1) for v in mids]
        bwd = [pltpu.roll(v, LN - 1, 1) for v in mids]
        for c in range(CT):
            v, o = mids[c], offs[c]
            west = jnp.where(first, fwd[c - 1] if c > 0 else 0.0, fwd[c])
            east = jnp.where(last, bwd[c + 1] if c < CT - 1 else 0.0, bwd[c])
            north = src[pl.ds(pl.multiple_of(o - COL, 8), 8), :]
            south = src[pl.ds(pl.multiple_of(o + COL, 8), 8), :]
            if k > 0:
                down = src[pl.ds(o - 1, 8), :]
            else:
                down = jnp.where(low, v, pltpu.roll(v, 1, 0))
            if k < LV // 8 - 1:
                up = src[pl.ds(o + 1, 8), :]
            else:
                up = jnp.where(high, v, pltpu.roll(v, 7, 0))
            s = ((north + south) + (west + east)) + 0.2 * (down + up)
            emit(c, k, v, s, o)


class Fetch:
    def __init__(self, src, dst, sems):
        count, size = src.shape[0], src.shape[2]
        self.parts = [pltpu.make_async_copy(src.at[t, 0], dst.at[pl.ds(t * size, size)], sems.at[t]) for t in range(count)]

    def start(self):
        for part in self.parts:
            part.start()

    def wait(self):
        for part in self.parts:
            part.wait()


def tally_of(ref):
    return [[ref[side * NT + t].astype(I32) for t in range(NT)] for side in range(2)]


def mask_row(mask, at, c):
    return mask[pl.ds(at * CT + c, 8, stride=0), :]


def forward_row(src, dst, mask, at, blank=None):
    ms = [mask_row(mask, at, c) for c in range(CT)]

    def emit(c, k, v, s, o):
        dst[pl.ds(pl.multiple_of(o, 8), 8), :] = ms[c] * (s + v * (0.6 - v * v))
        if blank is not None:
            blank[pl.ds(pl.multiple_of(o, 8), 8), :] = jnp.zeros((8, LN), F32)

    stencil_row(src, at, emit)


def adjoint_row(src, state, forcing, mask, at):
    ms = [mask_row(mask, at, c) for c in range(CT)]

    def emit(c, k, g, s, o):
        spot = pl.ds(pl.multiple_of(o, 8), 8)
        y = state[spot, :]
        forcing[spot, :] = ms[c] * ((s + g * (0.6 - 3.0 * (y * y))) + forcing[spot, :])

    stencil_row(src, at, emit)


def gradient_row(src, state, out, at):
    def emit(c, k, g, s, o):
        y = state[pl.ds(pl.multiple_of(o, 8), 8), :]
        out[pl.ds(pl.multiple_of(o - H * COL, 8), 8), :] = 0.2 * (s + g * (0.6 - 3.0 * (y * y)))

    stencil_row(src, at, emit)


def loop(first, last, body, unroll):
    def some(i, _):
        for u in range(unroll):
            body(first + H + i * unroll + u)
        return 0

    lax.fori_loop(0, (last + 1 - first) // unroll, some, 0)


def rims(reach, body):
    for at in [*range(-reach, 3 - reach), *range(ROWS - 3 + reach, ROWS + reach)]:
        body(at + H)


def even():
    return lax.rem(lax.axis_index("along"), 2) == 0


def edges_kernel(basic, land_at, staged, twin, other, mask, land, sems):
    def copy(c):
        return pltpu.make_async_copy(basic.at[:, :, pl.ds(c * LN, LN)], staged.at[c], sems.at[c])

    sea = pltpu.make_async_copy(land_at, land, sems.at[CT])
    sea.start()
    for c in range(CT):
        copy(c).start()
    sea.wait()
    for c in range(CT):
        mask[pl.ds(H * CT + c, ROWS, stride=CT), :] = 0.2 * land[:, pl.ds(c * LN, LN)].astype(F32)
    lower = jnp.where(even(), ROWS - H, 0)
    for c in range(CT):
        copy(c).wait()
        flat = staged.at[c].reshape(LV * ROWS, LN)
        for out, first in ((twin, lower), (other, ROWS - H - lower)):
            for j in range(H):
                r = first + j
                half = 2.5 * mask_row(mask, r + H, c)
                for k in range(LV // 8):
                    v = flat[pl.ds(k * 8 * ROWS + r, 8, stride=ROWS), :]
                    out[pl.ds((j * CT + c) * LV + k * 8, 8), :] = half * v
                out[pl.ds(H * COL + j * CT + c, 1), :] = mask[pl.ds((r + H) * CT + c, 1), :]


def edges(basic, land):
    return pl.pallas_call(
        edges_kernel,
        out_shape=[
            jax.ShapeDtypeStruct((CT, LV, ROWS, LN), F32),
            jax.ShapeDtypeStruct((EDGE, LN), F32),
            jax.ShapeDtypeStruct((EDGE, LN), F32),
            MASK,
        ],
        in_specs=[HBM, HBM],
        out_specs=[VM] * 4,
        scratch_shapes=[pltpu.VMEM((ROWS, CT * LN), I32), pltpu.SemaphoreType.DMA((CT + 1,))],
        compiler_params=params(4),
        cost_estimate=cost(2),
        name="edges",
    )(pltpu.with_memory_space_constraint(basic, pltpu.HBM), pltpu.with_memory_space_constraint(land, pltpu.HBM))


def order_kernel(cells_at, count_at, value_at, addr, sval, lane, spot, second, tallies, codes, cells, count, value, sems):
    fetches = [
        pltpu.make_async_copy(src, dst, sems.at[i])
        for i, (src, dst) in enumerate(((cells_at, cells), (count_at, count), (value_at, value)))
    ]
    for f in fetches:
        f.start()
    for f in fetches:
        f.wait()
    slot = lax.broadcasted_iota(I32, (1, CAP), 1)
    ups, downs = [], []
    for t in range(NT):
        row = (cells[t] >> 10) & (ROWS - 1)
        alive = slot < count[0, t]
        ups.append(jnp.logical_and(alive, row <= t))
        downs.append(jnp.logical_and(alive, row >= ROWS - 1 - t))
    one = [jnp.where(f, 1.0, 0.0) for f in ups + downs]
    flags = jnp.concatenate(one + [jnp.zeros((10, CAP), F32)], axis=0).astype(jnp.bfloat16)
    tri = jnp.where(
        lax.broadcasted_iota(I32, (CAP, CAP), 0) < lax.broadcasted_iota(I32, (CAP, CAP), 1), 1.0, 0.0
    ).astype(jnp.bfloat16)
    before = jnp.dot(flags, tri, preferred_element_type=F32)
    codes[...] = jnp.zeros((CODE, LN), F32)
    sub = lax.broadcasted_iota(I32, (CAP, CAP), 0)
    first = lax.broadcasted_iota(I32, (1, LN), 1)
    tally = jnp.zeros((1, LN), F32)
    for t in range(NT):
        up, down = ups[t], downs[t]
        pu, pd = before[t : t + 1], before[NT + t : NT + t + 1]
        nu = jnp.sum(one[t], axis=1, keepdims=True)
        nd = jnp.sum(one[NT + t], axis=1, keepdims=True)
        tally = tally + jnp.where(first == t, nu, 0.0) + jnp.where(first == NT + t, nd, 0.0)
        rank = jnp.where(up, pu, jnp.where(down, CAP - nd + pd, nu + slot.astype(F32) - pu - pd)).astype(I32)
        place = jnp.where(sub == rank, 1.0, 0.0).astype(jnp.bfloat16)
        cell, v = cells[t], value[t]
        v1 = v.astype(jnp.bfloat16).astype(F32)
        v2 = (v - v1).astype(jnp.bfloat16).astype(F32)
        parts = [
            (cell >> 16).astype(F32),
            ((cell >> 8) & 255).astype(F32),
            (cell & 255).astype(F32),
            v1,
            v2,
            v - v1 - v2,
            jnp.where(slot < count[0, t], 1.0, 0.0),
        ]
        left = jnp.concatenate(parts + [jnp.zeros((9, CAP), F32)], axis=0).astype(jnp.bfloat16)
        out = lax.dot_general(left, place, (((1,), (1,)), ((), ())), preferred_element_type=F32)
        cell = (out[0:1] * 65536.0 + out[1:2] * 256.0 + out[2:3]).astype(I32)
        row, level, where = (cell >> 10) & (ROWS - 1), cell >> 14, (cell >> 7) & (ROWS * CT - 1)
        alive = out[6:7] > 0.5
        own = (where + H * CT) * LV + level
        addr[t] = own
        sval[t] = out[3:4] + out[4:5] + out[5:6]
        lane[t] = jnp.where(alive, (cell & (LN - 1)).astype(F32), -1.0)
        if t == NT - 1:
            spot[0] = where + H * CT
            second[0] = jnp.where(jnp.logical_or(row == 1, row == ROWS - 2), -3.0, 0.0)
        far = jnp.where(row < ROWS // 2, own + ROWS * COL, own - ROWS * COL)
        near = jnp.logical_or(row <= t, row >= ROWS - 1 - t)
        code = jnp.where(near, far * LN + (cell & (LN - 1)), 0).astype(F32)
        for q in range(CAP // LN):
            codes[pl.ds(4 * t + q, 1), :] = code[:, q * LN : (q + 1) * LN]
    codes[pl.ds(12, 1), :] = tally
    tallies[0] = tally


def order(cells, count, value):
    ints, floats = jax.ShapeDtypeStruct((NT, 1, CAP), I32), jax.ShapeDtypeStruct((NT, 1, CAP), F32)
    return pl.pallas_call(
        order_kernel,
        out_shape=[ints, floats, floats, jax.ShapeDtypeStruct((1, 1, CAP), I32), jax.ShapeDtypeStruct((1, 1, CAP), F32), jax.ShapeDtypeStruct((1, 1, LN), F32), jax.ShapeDtypeStruct((CODE, LN), F32)],
        in_specs=[HBM] * 3,
        out_specs=[VM] * 7,
        scratch_shapes=[
            pltpu.VMEM((NT, 1, CAP), I32),
            pltpu.SMEM((1, NT), I32),
            pltpu.VMEM((NT, 1, CAP), F32),
            pltpu.SemaphoreType.DMA((3,)),
        ],
        compiler_params=params(6),
        cost_estimate=cost(2),
        name="order",
    )(*(pltpu.with_memory_space_constraint(x, pltpu.HBM) for x in (cells, count, value)))


def interior_kernel(staged, mask, lane, sval, addrs, spots, tallies, y0, y1, y2, y3, f1, f2, f3, twice, known, sea, total,
                    g1, g2, g3, terms, lying, at_ref, spot_ref, n_ref, sems):
    fetches = [Fetch(addrs, at_ref, sems), Fetch(spots, spot_ref, sems.at[pl.ds(NT, 1)]), Fetch(tallies, n_ref, sems.at[pl.ds(NT + 1, 1)])]
    for fetch in fetches:
        fetch.start()
    for c in range(CT):
        flat = staged.at[c].reshape(LV * ROWS, LN)

        def turn(i, _):
            for u in range(4):
                r = i * 4 + u
                half = 2.5 * mask_row(mask, r + H, c)
                for k in range(LV // 8):
                    v = flat[pl.ds(k * 8 * ROWS + r, 8, stride=ROWS), :]
                    y0[pl.ds(pl.multiple_of((r + H) * COL + c * LV + k * 8, 8), 8), :] = half * v
            return 0

        lax.fori_loop(0, ROWS // 4, turn, 0)

    zero = jnp.zeros((8, LN), F32)
    for at in (H - 2, ROWS + H + 1):
        for j in range(COL // 8):
            y2[pl.ds(at * COL + j * 8, 8), :] = zero
    for t, f in enumerate((f1, f2, f3)):
        for at in [*range(H + t + 1), *range(ROWS + H - t - 1, RX)]:
            for j in range(COL // 8):
                f[pl.ds(at * COL + j * 8, 8), :] = zero
    loop(1, 14, lambda at: forward_row(y0, y1, mask, at, f1), 7)
    loop(2, 13, lambda at: forward_row(y1, y2, mask, at, f2), 6)
    loop(3, 12, lambda at: forward_row(y2, y3, mask, at, f3), 5)
    for fetch in fetches:
        fetch.wait()

    def gather(i, _):
        for u in range(8):
            s = i * 8 + u
            here = pl.ds(s, 1)
            g1[here, :] = y1[pl.ds(at_ref[s], 1), :]
            g2[here, :] = y2[pl.ds(at_ref[CAP + s], 1), :]
            g3[here, :] = y3[pl.ds(at_ref[2 * CAP + s], 1), :]
            sea[here, :] = mask[pl.ds(spot_ref[s], 1), :]
        return 0

    lax.fori_loop(0, CAP // 8, gather, 0)
    ups, downs = tally_of(n_ref)
    for t in range(NT):
        for q in range(CAP // LN):
            part = pl.ds(q * LN, LN)
            lying[pl.ds(4 * t + q, 1), :] = lane[t, :, part]
            lying[pl.ds(12 + 4 * t + q, 1), :] = sval[t, :, part]
    lying[pl.ds(24, LN - 24), :] = jnp.zeros((LN - 24, LN), F32)
    uprights = lying[...].T
    ids = lax.broadcasted_iota(I32, (LN, LN), 1).astype(F32)
    slot = lax.broadcasted_iota(I32, (LN, LN), 0)
    acc = zero
    for t, g in enumerate((g1, g2, g3)):
        for q in range(CAP // LN):
            part = pl.ds(q * LN, LN)
            hit = jnp.broadcast_to(uprights[:, 4 * t + q : 4 * t + q + 1], (LN, LN)) == ids
            rows = pl.ds(t * CAP + q * LN, LN)
            two, have = jnp.where(hit, 2.0, 0.0), jnp.where(hit, jnp.broadcast_to(uprights[:, 12 + 4 * t + q : 13 + 4 * t + q], (LN, LN)), 0.0)
            twice[rows, :] = two
            known[rows, :] = have
            early = jnp.logical_and(slot + q * LN >= ups[t], slot + q * LN < CAP - downs[t])
            d = jnp.where(early, g[part, :] * two - have, 0.0)
            acc = acc + jnp.sum((d * d).reshape(LN // 8, 8, LN), axis=0)
            terms[rows, :] = d * (5.0 * sea[part, :]) if t == NT - 1 else 5.0 * d
    total[...] = acc

    def scatter(i, _):
        for u in range(8):
            s = i * 8 + u
            for t, f in enumerate((f1, f2, f3)):
                spot = pl.ds(at_ref[t * CAP + s], 1)
                f[spot, :] = f[spot, :] + terms[pl.ds(t * CAP + s, 1), :]
        return 0

    lax.fori_loop(0, CAP // 8, scatter, 0)


def interior(staged, mask, lane, sval, addrs, spots, tallies):
    rows = jax.ShapeDtypeStruct((NT * CAP, LN), F32)
    few = pltpu.VMEM((CAP, LN), F32)
    return pl.pallas_call(
        interior_kernel,
        out_shape=[FIELD] * 7 + [rows, rows, jax.ShapeDtypeStruct((CAP, LN), F32), jax.ShapeDtypeStruct((8, LN), F32)],
        in_specs=[VM] * 4 + [ANY] * 3,
        out_specs=[VM] * 11,
        scratch_shapes=[
            few,
            few,
            few,
            pltpu.VMEM((NT * CAP, LN), F32),
            pltpu.VMEM((LN, LN), F32),
            pltpu.SMEM((NT * CAP,), I32),
            pltpu.SMEM((CAP,), I32),
            pltpu.SMEM((LN,), F32),
            pltpu.SemaphoreType.DMA((NT + 2,)),
        ],
        compiler_params=params(6),
        cost_estimate=cost(11),
        name="interior",
    )(staged, mask, lane, sval, addrs, spots, tallies)


def bands_kernel(y0i, y1i, y2i, y3, f1i, f2i, f3i, maski, twice, known, sea, totali, second, codes, addrs, tallies, twin, other,
                 y0, y1, y2, f1, f2, f3, mask, pay, terms, extra, at_ref, n_ref, sems):
    fetches = [Fetch(addrs, at_ref, sems), Fetch(tallies, n_ref, sems.at[pl.ds(NT, 1)])]
    for fetch in fetches:
        fetch.start()
    lower = jnp.where(even(), ROWS + H, 0)
    for halo, first in ((twin, lower), (other, ROWS + H - lower)):
        base = pl.multiple_of(first * COL, 8)
        for q in range(H * COL // 8):
            y0[pl.ds(base + q * 8, 8), :] = halo[pl.ds(q * 8, 8), :]
        base = pl.multiple_of(first * CT, 8)
        for j in range(H):
            mask[pl.ds(base + j * CT, CT), :] = halo[pl.ds(H * COL + j * CT, CT), :]
    for src, dst, reach in ((y0, y1, 2), (y1, y2, 1), (y2, y3, 0)):
        rims(reach, lambda at: forward_row(src, dst, mask, at))
    for fetch in fetches:
        fetch.wait()
    ups, downs = tally_of(n_ref)
    most = 0
    for t in range(NT):
        most = jnp.maximum(most, (jnp.maximum(ups[t], downs[t]) + 2 * t + 1) // (2 * t + 2))

    def item(i, acc):
        for t, (y, f) in ((2, (y3, f3)), (1, (y2, f2)), (0, (y1, f1))):
            for u in range(2 * t + 2):
                j = i * (2 * t + 2) + u
                near = jnp.minimum(j, CAP - 1)
                for n, slot in ((ups[t], near), (downs[t], CAP - 1 - near)):
                    ok = j < n
                    row = t * CAP + slot
                    spot = pl.ds(at_ref[row], 1)
                    d = jnp.where(ok, y[spot, :] * twice[pl.ds(row, 1), :] - known[pl.ds(row, 1), :], 0.0)
                    acc = acc + d * d
                    if t == NT - 1:
                        d = d * (5.0 * sea[pl.ds(slot, 1), :])
                        z = y2[spot, :]
                        extra[pl.ds(jnp.where(ok, slot, CAP), 1), :] = (z * z) * d
                    else:
                        d = 5.0 * d
                    f[spot, :] = f[spot, :] + d
                    terms[pl.ds(jnp.where(ok, row, NT * CAP), 1), :] = d
        return acc

    acc = lax.fori_loop(0, most, item, jnp.zeros((1, LN), F32))
    for q in range(CAP // LN):
        for t in range(NT):

            @pl.when(jnp.logical_or(ups[t] > q * LN, downs[t] > CAP - (q + 1) * LN))
            def _():
                pay[pl.ds(4 * t + q, 1), :] = jnp.sum(terms[pl.ds(t * CAP + q * LN, LN), :].T, axis=0, keepdims=True)
                if t == NT - 1:
                    e = jnp.sum(extra[pl.ds(q * LN, LN), :].T, axis=0, keepdims=True)
                    pay[pl.ds(12 + q, 1), :] = e * second[0, :, pl.ds(q * LN, LN)]

    pay[pl.ds(CODE, CODE), :] = codes[...]
    pay[pl.ds(2 * CODE, 8), :] = totali[...] + jnp.where(sublanes() == 0, jnp.broadcast_to(acc, (8, LN)), 0.0)


def bands(y0, y1, y2, y3, f1, f2, f3, mask, twice, known, sea, total, second, codes, addrs, tallies, twin, other):
    return pl.pallas_call(
        bands_kernel,
        out_shape=[FIELD] * 6 + [MASK, jax.ShapeDtypeStruct((PAY, LN), F32)],
        in_specs=[VM] * 14 + [ANY] * 2 + [VM] * 2,
        out_specs=[VM] * 8,
        input_output_aliases={0: 0, 1: 1, 2: 2, 4: 3, 5: 4, 6: 5, 7: 6},
        scratch_shapes=[
            pltpu.VMEM((NT * CAP + 8, LN), F32),
            pltpu.VMEM((CAP + 8, LN), F32),
            pltpu.SMEM((NT * CAP,), I32),
            pltpu.SMEM((LN,), F32),
            pltpu.SemaphoreType.DMA((NT + 1,)),
        ],
        compiler_params=params(4),
        cost_estimate=cost(5),
        name="bands",
    )(y0, y1, y2, y3, f1, f2, f3, mask, twice, known, sea, total, second, codes, addrs, tallies, twin, other)


def adjoint_kernel(first, last, unroll, src, state, forcing, mask, out):
    loop(first, last, lambda at: adjoint_row(src, state, out, mask, at), unroll)


def adjoint(first, last, unroll, src, state, forcing, mask):
    return pl.pallas_call(
        functools.partial(adjoint_kernel, first, last, unroll),
        out_shape=FIELD,
        in_specs=[VM] * 4,
        out_specs=VM,
        input_output_aliases={2: 0},
        compiler_params=params(2),
        cost_estimate=cost(2),
        name="adjoint",
    )(src, state, forcing, mask)


SIDE = 28 * LN
LANES, ADDRS, FARS = 0, 12 * LN, 24 * LN


def edge_terms_kernel(y0, y1, y2, f1i, f2i, f3i, mask, twin, other, twin_flat, other_flat,
                      f1, f2, f3, grad, a_ref, b_ref, ca, cb, lines, line_ref, sems):
    def fetches(above, below):
        return [pltpu.make_async_copy(src, dst, sems.at[i]) for i, (src, dst) in enumerate(((above, a_ref), (below, b_ref)))]

    @pl.when(even())
    def _():
        for f in fetches(other_flat, twin_flat):
            f.start()

    @pl.when(jnp.logical_not(even()))
    def _():
        for f in fetches(twin_flat, other_flat):
            f.start()

    slot = lax.broadcasted_iota(I32, (1, LN), 1)
    for side, (x, y) in enumerate(((other, twin), (twin, other))):
        counts = jnp.where(even(), x[pl.ds(CODE + 12, 1), :], y[pl.ds(CODE + 12, 1), :]).astype(I32)
        for t in range(NT):
            n = jnp.sum(jnp.where(slot == (1 - side) * NT + t, counts, 0), axis=1, keepdims=True)
            for q in range(CAP // LN):
                row = pl.ds(CODE + 4 * t + q, 1)
                code = jnp.where(even(), x[row, :], y[row, :]).astype(I32)
                at = slot + q * LN
                live = at >= CAP - n if side == 0 else at < n
                base = side * SIDE + (4 * t + q) * LN
                addr = jnp.where(live, code >> 7, 0)
                lines[0, :, pl.ds(base + LANES, LN)] = jnp.where(live, code & (LN - 1), -1)
                lines[0, :, pl.ds(base + ADDRS, LN)] = addr
                if t == NT - 1:
                    far = addr - (1 if side == 0 else ROWS + H + 1) * COL
                    far = jnp.where(jnp.logical_and(far >= 0, far < COL), far, 0)
                    lines[0, :, pl.ds(side * SIDE + FARS + q * LN, LN)] = far
    prepared = Fetch(lines, line_ref, sems.at[pl.ds(2, 1)])
    prepared.start()
    for q in range(COL // 8):
        for buf in (ca, cb):
            buf[pl.ds(q * 8, 8), :] = jnp.zeros((8, LN), F32)
    loop(3, 12, lambda at: gradient_row(f1, y0, grad, at), 5)
    for f in fetches(twin_flat, other_flat):
        f.wait()
    prepared.wait()
    counts = (CODE + 12) * LN
    most = 0
    for t in range(NT):
        n = jnp.maximum(a_ref[counts + NT + t].astype(I32), b_ref[counts + t].astype(I32))
        most = jnp.maximum(most, (n + 2 * t + 1) // (2 * t + 2))

    def item(i, _):
        for t, f in ((2, f3), (1, f2), (0, f1)):
            for u in range(2 * t + 2):
                near = jnp.minimum(i * (2 * t + 2) + u, CAP - 1)
                for ref, slot_at, first, side in ((a_ref, CAP - 1 - near, 0, ca), (b_ref, near, SIDE, cb)):
                    at = t * CAP + slot_at
                    hit = slot == line_ref[first + LANES + at]
                    spot = pl.ds(line_ref[first + ADDRS + at], 1)
                    f[spot, :] = f[spot, :] + jnp.where(hit, ref[at], 0.0)
                    if t == NT - 1:
                        spot = pl.ds(line_ref[first + FARS + slot_at], 1)
                        side[spot, :] = side[spot, :] + jnp.where(hit, ref[12 * LN + slot_at], 0.0)
        return 0

    lax.fori_loop(0, most, item, 0)
    for side, at in ((ca, 1), (cb, ROWS + H + 1)):
        for q in range(COL // 8):
            spot = pl.ds(at * COL + q * 8, 8)
            f2[spot, :] = f2[spot, :] + side[pl.ds(q * 8, 8), :]
    for src, state, dst, reach in ((f3, y2, f2, 2), (f2, y1, f1, 1)):
        rims(reach, lambda at: adjoint_row(src, state, dst, mask, at))


def edge_terms(y0, y1, y2, f1, f2, f3, mask, twin, other):
    return pl.pallas_call(
        edge_terms_kernel,
        out_shape=[FIELD] * 3 + [jax.ShapeDtypeStruct((ROWS * COL, LN), F32)],
        in_specs=[VM] * 9 + [ANY] * 2,
        out_specs=[VM] * 4,
        input_output_aliases={3: 0, 4: 1, 5: 2},
        scratch_shapes=[
            pltpu.SMEM((PAY * LN,), F32),
            pltpu.SMEM((PAY * LN,), F32),
            pltpu.VMEM((COL, LN), F32),
            pltpu.VMEM((COL, LN), F32),
            pltpu.VMEM((1, 1, 2 * SIDE), I32),
            pltpu.SMEM((2 * SIDE,), I32),
            pltpu.SemaphoreType.DMA((3,)),
        ],
        compiler_params=params(4),
        cost_estimate=cost(5),
        name="edge_terms",
    )(y0, y1, y2, f1, f2, f3, mask, twin, other, twin.reshape(-1), other.reshape(-1))


def finish_kernel(y0, f1, gradi, grad, out, staged, sems):
    rims(0, lambda at: gradient_row(f1, y0, grad, at))

    def copy(c):
        return pltpu.make_async_copy(staged.at[c], out.at[:, :, pl.ds(c * LN, LN)], sems.at[c])

    for c in range(CT):

        def turn(k, _):
            for half in range(2):
                v = grad[pl.ds(half * 8 * COL + c * LV + k, 8, stride=COL), :]
                staged[c, k, pl.ds(half * 8, 8), :] = v
            return 0

        lax.fori_loop(0, LV, turn, 0, unroll=8)
        copy(c).start()
    for c in range(CT):
        copy(c).wait()


def finish(y0, f1, grad):
    return pl.pallas_call(
        finish_kernel,
        out_shape=[jax.ShapeDtypeStruct((ROWS * COL, LN), F32), jax.ShapeDtypeStruct((LV, ROWS, CT * LN), F32)],
        in_specs=[VM] * 3,
        out_specs=[VM, ANY],
        input_output_aliases={2: 0},
        scratch_shapes=[pltpu.VMEM((CT, LV, ROWS, LN), F32), pltpu.SemaphoreType.DMA((CT,))],
        compiler_params=params(8),
        cost_estimate=cost(4),
        name="finish",
    )(y0, f1, grad)


def total_kernel(scale, x, y, out):
    out[...] = jnp.sum(x[...] + y[...], keepdims=True) * scale


def total(x, y, scale):
    return pl.pallas_call(
        functools.partial(total_kernel, scale),
        out_shape=jax.ShapeDtypeStruct((1, 1), F32),
        in_specs=[VM, VM],
        out_specs=VM,
        compiler_params=params(1),
        cost_estimate=cost(0.1),
        name="total",
    )(x, y).reshape(1)


def add_kernel(first, pay, twin, out):
    out[...] = pay[pl.ds(first, 8), :] + twin[pl.ds(first, 8), :]


def add(first, a, b):
    return pl.pallas_call(
        functools.partial(add_kernel, first),
        out_shape=jax.ShapeDtypeStruct((8, LN), F32),
        in_specs=[VM, VM],
        out_specs=VM,
        compiler_params=params(1),
        cost_estimate=cost(0.1),
        name="add",
    )(a, b)


def sum_along(pay, twin, stages, held):
    size = lax.axis_size("along")
    steps = [1 << i for i in range(1, size.bit_length() - 1)]
    x = add(2 * CODE, pay, twin)
    other = jnp.zeros_like(x)
    if size & (size - 1):
        x, steps = lax.psum(0.5 * x, "along"), []
    for i in range(max(len(steps), len(stages))):
        if i < len(steps):
            if i > 0:
                x = add(0, x, other)
            x, held = lax.optimization_barrier((x, held))
            other = lax.ppermute(x, "along", [(p, p ^ steps[i]) for p in range(size)])
        if i < len(stages):
            held = stages[i](*held)
    return x, other, held


def local(basic_state, land_sea, obs_cells, obs_count, obs_value):
    size = lax.axis_size("along")
    twins = [(i, i ^ 1) for i in range(size)]
    others = [(i, i - 1 if i % 2 == 0 else i + 1) for i in range(1, size - 1)]
    cells = obs_cells.transpose(1, 0, 2)
    value = obs_value.transpose(1, 0, 2)
    staged, twin, other, mask = edges(basic_state, land_sea)
    other = lax.ppermute(other, "along", others)
    twin = lax.ppermute(twin, "along", twins)
    addrs, sval, lane, spots, second, tallies, codes = order(cells, obs_count, value)
    y0, y1, y2, y3, f1, f2, f3, twice, known, sea, squares = interior(staged, mask, lane, sval, addrs, spots, tallies)
    y0, y1, y2, f1, f2, f3, mask, pay = bands(
        y0, y1, y2, y3, f1, f2, f3, mask, twice, known, sea, squares, second, codes, addrs, tallies, twin, other
    )
    other = lax.ppermute(pay, "along", others)
    twin = lax.ppermute(pay, "along", twins)
    def inner(a, b, c):
        b = adjoint(1, 14, 7, c, y2, b, mask)
        return adjoint(2, 13, 6, b, y1, a, mask), b, c

    stages = (
        inner,
        lambda a, b, c: edge_terms(y0, y1, y2, a, b, c, mask, twin, other),
        lambda a, b, c, g: finish(y0, a, g),
    )
    x, y, held = sum_along(pay, twin, stages, (f1, f2, f3))
    gradient = held[1]
    misfit = total(x, y, 1.0 / (2.0 * size * obs_cells.shape[1] * obs_cells.shape[2]))
    return gradient, misfit


def solution(mesh):
    in_specs = (
        P(None, ("ens", "along"), None),
        P(("ens", "along"), None),
        P(("ens", "along"), None, None),
        P(("ens", "along"), None),
        P(("ens", "along"), None, None),
    )
    out_specs = (P(None, ("ens", "along"), None), P("ens"))
    return jax.shard_map(local, mesh=mesh, in_specs=in_specs, out_specs=out_specs, check_vma=False)
```
